32 devices in a mesh: grp: 4 (over y, x), tok: 8 (over z, core).
Axes of the slice: x: 2, y: 2, z: 4, core: 2. Of those that a mesh axis runs over, the one named last changes fastest.
Arguments:
- queries: bfloat16 [4096, 768], P(('grp', 'tok')), may hold values from -6 to 6
- key_tokens: float32 [4096, 768], P(('grp', 'tok')), may hold values from -6 to 6
- values: float32 [4096, 768], P(('grp', 'tok')), may hold values from -6 to 6
- out_grad: bfloat16 [4096, 768], P(('grp', 'tok')), may hold values from -6 to 6
- w_gate: float32 [768, 768], replicated, may hold values from -0.21875 to 0.21875
- w_up: float32 [768, 768], replicated, may hold values from -0.21875 to 0.21875
- w_down: float32 [768, 768], replicated, may hold values from -0.21875 to 0.21875
Outputs:
- d_queries: bfloat16 [4096, 768], P(('grp', 'tok'))
- d_keys: float32 [4096, 768], P(('grp', 'tok'))
- d_values: float32 [4096, 768], P(('grp', 'tok'))
- d_gate: float32 [768, 768], P('tok')
- d_up: float32 [768, 768], P('tok')
- d_down: float32 [768, 768], P('tok')
The draws below stay inside these ranges and needn't reach their ends.
All inputs are finite; a program needn't handle non-finite values.
Results may differ from the reference program's by a relative error of at most 0.012.
Values may be sent and summed in bfloat16 or wider, within the bound.
A program may use at most 128 MiB of HBM per device.

```python
import jax
import jax.numpy as jnp
from jax import lax

D = 768
TOK_DEV = 128
TOKENS = 4096


def block_scale(key, dims, pieces, low, high):
    def one(axis_at, shards_of):
        steps = jax.random.uniform(jax.random.fold_in(jax.random.fold_in(key, 6), axis_at), (shards_of,), jnp.float32, low / len(pieces), high / len(pieces))
        return jnp.repeat(jnp.exp(steps), dims[axis_at] // shards_of).reshape((-1,) + (1,) * (len(dims) - axis_at - 1))

    gain = one(*pieces[0])
    for cut in pieces[1:]:
        gain = gain * one(*cut)
    return gain


def centred(key, dims, width, limit, shards=(), kind=jnp.bfloat16):
    values = jax.random.normal(key, dims, jnp.float32) * width
    if len(shards) > 0:
        values = block_scale(key, dims, shards, -0.22, 0.18) * values
    return jnp.clip(values, min=-limit, max=limit).astype(kind)


def setup_inputs(seed: int = 0) -> dict:
    keys = jax.random.split(jax.random.key(seed), 8)
    return {
        "queries": centred(keys[0], (TOKENS, D), 1.0, 6.0, ((0, 32),)),
        "key_tokens": centred(keys[1], (TOKENS, D), 1.0, 6.0, ((0, 32),), jnp.float32),
        "values": centred(keys[2], (TOKENS, D), 1.0, 6.0, ((0, 32),), jnp.float32),
        "out_grad": centred(keys[3], (TOKENS, D), 1.0, 6.0, ((0, 32),)),
        "w_gate": centred(keys[4], (D, D), D ** -0.5, 0.21875, (), jnp.float32),
        "w_up": centred(keys[5], (D, D), D ** -0.5, 0.21875, (), jnp.float32),
        "w_down": centred(keys[6], (D, D), D ** -0.5, 0.21875, (), jnp.float32),
    }


STEP_SIZE = 0.02
EPSILON = 1e-06
HIGH = lax.Precision.HIGHEST

def matmul(left, right):
    return jnp.dot(left, right, precision=HIGH, preferred_element_type=jnp.float32)

def key_grad(w_gate, w_up, w_down, key_rows, value_rows):
    hidden_gate = matmul(key_rows, w_gate)
    hidden_up = matmul(key_rows, w_up)
    sig = jax.nn.sigmoid(hidden_gate)
    active = hidden_gate * sig * hidden_up
    error = matmul(active, w_down) - value_rows
    d_active = matmul(error, w_down.T)
    d_hup = d_active * hidden_gate * sig
    d_hgate = d_active * hidden_up * sig * (1.0 + hidden_gate * (1.0 - sig))
    return (matmul(key_rows.T, d_hgate), matmul(key_rows.T, d_hup), matmul(active.T, error))

def query_grad(fast_weights, query_rows, grad_rows):
    fast_gate, fast_up, fast_down = fast_weights
    hidden_gate = jnp.dot(query_rows, fast_gate, preferred_element_type=jnp.float32)
    hidden_up = jnp.dot(query_rows, fast_up, preferred_element_type=jnp.float32)
    sig = jax.nn.sigmoid(hidden_gate)
    active = (hidden_gate * sig * hidden_up).astype(jnp.bfloat16)
    d_active = jnp.dot(grad_rows, fast_down.T, preferred_element_type=jnp.float32)
    d_hup = (d_active * hidden_gate * sig).astype(jnp.bfloat16)
    d_hgate = (d_active * hidden_up * sig * (1.0 + hidden_gate * (1.0 - sig))).astype(jnp.bfloat16)
    d_rows = (jnp.dot(d_hgate, fast_gate.T, preferred_element_type=jnp.float32) + jnp.dot(d_hup, fast_up.T, preferred_element_type=jnp.float32)).astype(jnp.bfloat16)
    grads = (jnp.dot(query_rows.T, d_hgate, preferred_element_type=jnp.float32), jnp.dot(query_rows.T, d_hup, preferred_element_type=jnp.float32), jnp.dot(active.T, grad_rows, preferred_element_type=jnp.float32))
    return (d_rows, grads)

def column_sums(matrices):
    return tuple((lax.optimization_barrier(jnp.sum(matrix * matrix, axis=0)) for matrix in matrices))

def apply_update(weight_rows, grad_parts, squares, full_width):
    scales = tuple((jnp.sqrt(square / full_width + EPSILON) for square in squares))
    fast_weights = tuple(((weight - STEP_SIZE * grad / scale).astype(jnp.bfloat16) for weight, grad, scale in zip(weight_rows, grad_parts, scales)))
    return (fast_weights, scales)

def back_products(query_parts, grad_parts):
    return tuple((lax.optimization_barrier(jnp.sum(-STEP_SIZE * dpart * gpart, axis=0)) for dpart, gpart in zip(query_parts, grad_parts)))

def normal_back(query_parts, grad_parts, scales, products, full_width):
    return tuple(((-STEP_SIZE * dpart / scale - gpart * product / (full_width * scale * scale * scale)).astype(jnp.bfloat16) for dpart, gpart, scale, product in zip(query_parts, grad_parts, scales, products)))

def reference(queries, key_tokens, values, out_grad, w_gate, w_up, w_down):
    weights = (w_gate, w_up, w_down)
    full_width = w_gate.shape[0]
    key_blocks = key_tokens.reshape(-1, TOK_DEV, full_width)
    value_blocks = values.reshape(-1, TOK_DEV, full_width)
    query_blocks = queries.reshape(-1, TOK_DEV, full_width)
    grad_blocks = out_grad.reshape(-1, TOK_DEV, full_width)
    zeros = tuple((jnp.zeros((full_width, full_width), jnp.float32) for weight in weights))

    def forward_step(summed, block):
        local = key_grad(w_gate, w_up, w_down, block[0], block[1])
        return (tuple((left + right for left, right in zip(summed, local))), None)
    grad_sum, unused = lax.scan(forward_step, zeros, (key_blocks, value_blocks))
    fast_weights, scales = apply_update(weights, grad_sum, column_sums(grad_sum), full_width)

    def query_step(summed, block):
        d_rows, local = query_grad(fast_weights, block[0], block[1])
        return (tuple((left + right for left, right in zip(summed, local))), d_rows)
    query_sum, d_query_blocks = lax.scan(query_step, zeros, (query_blocks, grad_blocks))
    rounded = normal_back(query_sum, grad_sum, scales, back_products(query_sum, grad_sum), full_width)
    rounded = lax.optimization_barrier(rounded)
    cotangent = tuple((item.astype(jnp.float32) for item in rounded))

    def second_step(summed, block):
        unused_out, pullback = jax.vjp(key_grad, w_gate, w_up, w_down, block[0], block[1])
        grads = pullback(cotangent)
        return (tuple((left + right for left, right in zip(summed, grads[:3]))), (grads[3], grads[4]))
    second_sum, pair = lax.scan(second_step, zeros, (key_blocks, value_blocks))
    inverse = 1.0 / TOKENS
    summed = tuple(((left + right) * inverse for left, right in zip(query_sum, second_sum)))
    return (d_query_blocks.reshape(-1, full_width), pair[0].reshape(-1, full_width), pair[1].reshape(-1, full_width), summed[0], summed[1], summed[2])
```

```python
import functools

import jax
import jax.numpy as jnp
from jax import lax
from jax.experimental import pallas as pl
from jax.experimental.pallas import tpu as pltpu
from jax.sharding import PartitionSpec as P

STEP_SIZE = 0.02
EPSILON = 1e-06
MESH = pl.DeviceIdType.MESH
BF = jnp.bfloat16
F32 = jnp.float32
VM = pltpu.VMEM
DMA = pltpu.SemaphoreType.DMA


def dot(left, right):
    return jnp.dot(left, right, preferred_element_type=F32)


def dot_nt(left, right):
    return lax.dot_general(left, right, (((1,), (1,)), ((), ())), preferred_element_type=F32)


def flip_bits(z, m):
    out, bit = z, 1
    while bit <= m:
        if m & bit:
            out = out + bit - 2 * bit * lax.rem(out // bit if bit > 1 else out, 2)
        bit *= 2
    return out


def block(index, size):
    return pl.ds(pl.multiple_of(index * size, size), size)


class Net:
    def __init__(self, zs, rows, width):
        g, t = lax.axis_index("grp"), lax.axis_index("tok")
        self.zs, self.rows = zs, rows
        self.g, self.z, self.c = g, t // 2, lax.rem(t, 2)
        self.y, self.x = g // 2, lax.rem(g, 2)
        self.t = t
        cut = 128 * ((width // 128 + 1) // 2)
        self.lanes = (pl.ds(0, cut), pl.ds(cut, width - cut))
        self.twin = (g, 2 * self.z + 1 - self.c)

    def flip(self, *directions):
        y, x = self.y, self.x
        for a in directions:
            if a == 0:
                x = 1 - x
            else:
                y = 1 - y
        return y, x

    def side(self, a):
        y, x = self.flip(a)
        return (2 * y + x, self.t)

    def zpeer(self, m):
        return (self.g, 2 * flip_bits(self.z, m) + self.c)

    def chunk(self, zb, yx):
        return block(4 * zb + 2 * yx[0] + yx[1], self.rows)

    def greet(self):
        barrier = pltpu.get_barrier_semaphore()
        peers = [self.twin, self.side(0), self.side(1)]
        peers += [self.zpeer(m) for m in range(1, self.zs)]
        for peer in peers:
            pl.semaphore_signal(barrier, inc=1, device_id=peer, device_id_type=MESH)
        pl.semaphore_wait(barrier, len(peers))


def send(src, dst, sems, at, peer):
    copy = pltpu.make_async_remote_copy(
        src_ref=src, dst_ref=dst, send_sem=sems[0].at[at], recv_sem=sems[1].at[at],
        device_id=peer, device_id_type=MESH,
    )
    copy.start()
    return copy


def reduce_scatter(net, pay, s, total, produce, fillers):
    zs = net.zs
    order = list(range(zs - 1, -1, -1))
    first, second, third = {}, {}, {}
    sent = []

    def start_first(i):
        m = order[i]
        zb = flip_bits(net.z, m)
        produce(zb, i)
        for k in range(2):
            for p in range(2):
                a = (p + m) % 2
                yx = net.flip(a, 1 - a) if k == 0 else net.flip(a)
                c = send(pay.at[net.chunk(zb, yx), net.lanes[p]], s["r1"][p].at[i, k],
                         s["s1"], (i, p, k), net.side(a))
                first[i, p, k] = c

    def start_second(i):
        m = order[i]
        zb = flip_bits(net.z, m)
        for p in range(2):
            a = (p + m) % 2
            first[i, p, 0].wait_recv()
            at = (net.chunk(zb, net.flip(1 - a)), net.lanes[p])
            pay[at] = (pay[at].astype(F32) + s["r1"][p][i, 0].astype(F32)).astype(BF)
            second[i, p] = send(pay.at[at], s["r2"][p].at[i], s["s2"], (i, p), net.side(1 - a))

    def start_third(i):
        m = order[i]
        zb = flip_bits(net.z, m)
        for p in range(2):
            first[i, p, 1].wait_recv()
            second[i, p].wait_recv()
            at = (net.chunk(zb, (net.y, net.x)), net.lanes[p])
            value = (pay[at].astype(F32) + s["r1"][p][i, 1].astype(F32)
                     + s["r2"][p][i].astype(F32))
            if m:
                s["zb"][p][i] = value.astype(BF)
                third[i, p] = send(s["zb"][p].at[i], s["zr"][p].at[i], s["s3"], (i, p),
                                   net.zpeer(m))
            else:
                total[:, net.lanes[p]] = value

    for i in range(zs + 2):
        if i < zs:
            start_first(i)
            if i in fillers:
                fillers[i]()
        if 1 <= i <= zs:
            start_second(i - 1)
        if i >= 2:
            start_third(i - 2)
    for p in range(2):
        value = total[:, net.lanes[p]]
        for i in range(zs - 1):
            third[i, p].wait_recv()
            value = value + s["zr"][p][i].astype(F32)
        total[:, net.lanes[p]] = value
    return [*first.values(), *second.values(), *third.values()]


def spread_own(net, full, zb, i, p, s):
    a = (p + i) % 2
    at = (net.chunk(zb, (net.y, net.x)), net.lanes[p])
    return [send(full.at[at], full.at[at], s["o"], (i, p, k), net.side(d))
            for k, d in enumerate((a, 1 - a))]


def relay_side(net, full, zb, i, p, s):
    a = (p + i) % 2
    at = (net.chunk(zb, net.flip(a)), net.lanes[p])
    return send(full.at[at], full.at[at], s["f"], (i, p), net.side(1 - a))


def all_gather(net, full, s, parts):
    zs = net.zs
    own = {}
    relays = {}
    far = {}
    for p in range(2):
        parts[p]()
        at = (net.chunk(net.z, (net.y, net.x)), net.lanes[p])
        for m in range(1, zs):
            far[m, p] = send(full.at[at], full.at[at], s["z"], (m - 1, p), net.zpeer(m))
        own[0, p] = spread_own(net, full, net.z, 0, p, s)

    def forward(i):
        zb = flip_bits(net.z, i)
        for p in range(2):
            own[i, p][0].wait_recv()
            relays[i, p] = relay_side(net, full, zb, i, p, s)

    for i in range(1, zs):
        zb = flip_bits(net.z, i)
        for p in range(2):
            far[i, p].wait_recv()
            own[i, p] = spread_own(net, full, zb, i, p, s)
        forward(i - 1)
    forward(zs - 1)
    for i in range(zs):
        for p in range(2):
            own[i, p][1].wait_recv()
            relays[i, p].wait_recv()
    copies = [*far.values(), *relays.values()]
    for pair in own.values():
        copies += pair
    return copies


def drain(copies):
    for copy in copies:
        copy.wait_send()


def by_rows(count, step, body):
    def run(i, carry):
        body(pl.ds(pl.multiple_of(i * step, step), step))
        return carry
    lax.fori_loop(0, count // step, run, 0)


def step_body(zs, names, inverse, *refs):
    r = dict(zip(names, refs))
    (queries, keys, values, out_grad, w_gate, w_up, w_down) = refs[:7]
    (d_queries, d_keys, d_values, d_gate, d_up, d_down) = refs[7:13]
    toks, width = queries.shape
    half = width // 2
    every = 2 * toks
    rows = width // (4 * zs)
    zrows = 4 * rows
    net = Net(zs, rows, width + half)
    c = net.c
    mine, theirs = block(c, toks), block(1 - c, toks)
    gl, ul, dl = pl.ds(0, half), pl.ds(half, half), pl.ds(width, half)
    wide = pl.ds(0, width)
    hid = block(c, half)

    loads = {}
    for i, (name, src, dst) in enumerate((
        ("k", keys, r["kf"]),
        ("a", w_gate.at[:, hid], r["wab"].at[:, gl]),
        ("b", w_up.at[:, hid], r["wab"].at[:, ul]),
        ("c", w_down.at[hid, :], r["wc"]),
        ("v", values, r["vf"]),
        ("q", queries, r["qb"].at[mine, :]),
        ("o", out_grad, r["ob"].at[mine, :]),
    )):
        loads[name] = pltpu.make_async_copy(src, dst, r["ld"].at[i])
        loads[name].start()
    net.greet()
    tsem = (r["ts"], r["tr"])
    done = []

    def twin(src, dst, k):
        copy = send(src, dst, tsem, k, net.twin)
        done.append(copy)
        return copy

    def scratch_of(kind, k):
        if kind == "rs":
            return {
                "r1": (r["r1a%d" % k], r["r1b%d" % k]), "r2": (r["r2a%d" % k], r["r2b%d" % k]),
                "zb": (r["zba%d" % k], r["zbb%d" % k]), "zr": (r["zra%d" % k], r["zrb%d" % k]),
                "s1": (r["s1s%d" % k], r["s1r%d" % k]), "s2": (r["s2s%d" % k], r["s2r%d" % k]),
                "s3": (r["s3s%d" % k], r["s3r%d" % k]),
            }
        return {
            "z": (r["azs%d" % k], r["azr%d" % k]), "o": (r["aos%d" % k], r["aor%d" % k]),
            "f": (r["afs%d" % k], r["afr%d" % k]),
        }

    xb, gu, ab, eb = r["xb"], r["gu"], r["ab"], r["eb"]
    loads["k"].wait()
    xb[mine, :] = r["kf"][...].astype(BF)
    keys_in = twin(xb.at[mine, :], xb.at[mine, :], 0)
    loads["a"].wait()
    loads["b"].wait()
    r["abb"][...] = r["wab"][...].astype(BF)
    loads["c"].wait()
    r["cb"][...] = r["wc"][...].astype(BF)
    loads["q"].wait()
    queries_in = twin(r["qb"].at[mine, :], r["qb"].at[mine, :], 1)
    loads["o"].wait()
    grads_in = twin(r["ob"].at[mine, :], r["ob"].at[mine, :], 2)
    keys_in.wait_recv()
    gu[...] = dot(xb[...], r["abb"][...])

    def active_rows(at):
        g, u = gu[at, gl], gu[at, ul]
        ab[at, :] = (g * jax.nn.sigmoid(g) * u).astype(BF)
    by_rows(every, 32, active_rows)

    loads["v"].wait()
    ep, er = r["ep"], r["er"]
    ep[mine, :] = dot(ab[mine, :], r["cb"][...]) - r["vf"][...]
    e_out = [twin(ep.at[mine, :], er.at[mine, :], 3)]
    ep[theirs, :] = dot(ab[theirs, :], r["cb"][...])
    e_out.append(twin(ep.at[theirs, :], er.at[theirs, :], 4))
    for copy, at in zip(e_out, (theirs, mine)):
        copy.wait_recv()
        eb[at, :] = (ep[at, :] + er[at, :]).astype(BF)
    da, dgu = r["da"], r["dgu"]
    da[...] = dot_nt(eb[...], r["cb"][...])

    def d_rows(at):
        g, u, d = gu[at, gl], gu[at, ul], da[at, :]
        sig = jax.nn.sigmoid(g)
        dgu[at, ul] = (d * g * sig).astype(BF)
        dgu[at, gl] = (d * u * sig * (1.0 + g * (1.0 - sig))).astype(BF)
    by_rows(every, 32, d_rows)
    r["dguT"][...] = dgu[...].T
    r["eT"][...] = eb[...].T

    pay = r["pay0"]

    def key_block(zb, i):
        at = block(zb, zrows)
        pay[at, wide] = dot(r["dguT"][at, :], xb[...]).astype(BF)
        pay[at, dl] = dot(r["eT"][at, :], ab[...]).astype(BF)

    def turn_weights():
        r["wabt"][...] = r["wab"][...].T
        r["wct"][...] = r["wc"][...].T

    def turn_grads():
        grads_in.wait_recv()
        r["oT"][...] = r["ob"][...].T

    def turn_queries():
        queries_in.wait_recv()
        r["qT"][...] = r["qb"][...].T

    def turn_keys():
        r["xT"][...] = xb[...].T

    grad = r["grad"]
    rs0 = reduce_scatter(net, pay, scratch_of("rs", 0), grad, key_block,
                         {0: turn_grads, 1: turn_queries, 2: turn_keys, 3: turn_weights})

    own = net.chunk(net.z, (net.y, net.x))
    squares = jnp.sum(grad[:, dl] * grad[:, dl], axis=1, keepdims=True)
    r["sq"][0] = jnp.broadcast_to(squares, (rows, 128))
    norm_in = twin(r["sq"].at[0], r["sq"].at[1], 5)
    scale_of = lambda sq: jnp.sqrt(sq / width + EPSILON)
    full = r["full0"]
    scale = r["scale"]

    def wide_part():
        g = grad[:, wide]
        sc = scale_of(jnp.sum(g * g, axis=1, keepdims=True))
        scale[0] = jnp.broadcast_to(sc, (rows, 128))
        full[own, wide] = (r["wabt"][own, :] - STEP_SIZE * g / sc).astype(BF)

    def down_part():
        norm_in.wait_recv()
        sc = scale_of((r["sq"][0] + r["sq"][1])[:, :1])
        scale[1] = jnp.broadcast_to(sc, (rows, 128))
        full[own, dl] = (r["wct"][own, :] - STEP_SIZE * grad[:, dl] / sc).astype(BF)

    ag0 = all_gather(net, full, scratch_of("ag", 0), (wide_part, down_part))

    hgu, hd, hact, dact = r["hgu"], r["hd"], r["hact"], r["dact"]
    hgu[...] = dot_nt(r["qb"][...], full[:, wide])
    dact[...] = dot(r["ob"][...], full[:, dl])

    def query_rows(at):
        g, u, d = hgu[at, gl], hgu[at, ul], dact[at, :]
        sig = jax.nn.sigmoid(g)
        hact[at, :] = (g * sig * u).astype(BF)
        hd[at, ul] = (d * g * sig).astype(BF)
        hd[at, gl] = (d * u * sig * (1.0 + g * (1.0 - sig))).astype(BF)
    by_rows(every, 32, query_rows)
    r["hdT"][...] = hd[...].T
    pay1 = r["pay1"]

    def query_block(zb, i):
        at = block(zb, zrows)
        pay1[at, wide] = dot(r["hdT"][at, :], r["qb"][...]).astype(BF)
        pay1[at, dl] = dot(r["oT"][at, :], hact[...]).astype(BF)

    def query_back():
        r["qp"][...] = dot(hd[...], full[:, wide])
        r["qin"] = twin(r["qp"].at[theirs, :], r["qr"], 6)

    def plain_wide():
        r["hp"][...] = dot(r["qT"][...], hd[...])

    def plain_down():
        r["haT"][...] = hact[...].T
        r["hdn"][...] = dot(r["haT"][...], r["ob"][...])

    hsum = r["hsum"]
    rs1 = reduce_scatter(net, pay1, scratch_of("rs", 1), hsum, query_block,
                         {0: query_back, 1: plain_wide, 2: plain_down})

    product = jnp.sum(-STEP_SIZE * hsum[:, dl] * grad[:, dl], axis=1, keepdims=True)
    r["sq"][2] = jnp.broadcast_to(product, (rows, 128))
    product_in = twin(r["sq"].at[2], r["sq"].at[3], 7)
    back = r["full1"]

    def turned(h, g, sc, prod):
        return (-STEP_SIZE * h / sc - g * prod / (width * sc * sc * sc)).astype(BF)

    def wide_back():
        h, g = hsum[:, wide], grad[:, wide]
        prod = jnp.sum(-STEP_SIZE * h * g, axis=1, keepdims=True)
        back[own, wide] = turned(h, g, scale[0][:, :1], prod)

    def down_back():
        product_in.wait_recv()
        prod = (r["sq"][2] + r["sq"][3])[:, :1]
        back[own, dl] = turned(hsum[:, dl], grad[:, dl], scale[1][:, :1], prod)

    ag1 = all_gather(net, back, scratch_of("ag", 1), (wide_back, down_back))

    pq, tb, ec = r["pq"], r["tb"], r["ec"]
    pq[...] = dot_nt(xb[...], back[:, wide])
    ec[...] = dot(eb[...], back[:, dl])

    def t_rows(at):
        g, u = gu[at, gl], gu[at, ul]
        p, q = pq[at, gl], pq[at, ul]
        sig = jax.nn.sigmoid(g)
        tb[at, :] = (q * g * sig + p * u * sig * (1.0 + g * (1.0 - sig))).astype(BF)
    by_rows(every, 32, t_rows)
    sp, sr, sb = r["sp"], r["sr"], r["sb"]
    second_out = []
    for k, at in enumerate((mine, theirs)):
        sp[at, :] = dot_nt(ab[at, :], back[:, dl]) + dot(tb[at, :], r["cb"][...])
        second_out.append(twin(sp.at[at, :], sr.at[at, :], 8 + k))
    r["taT"][:, pl.ds(0, every)] = tb[...].T
    r["taT"][:, pl.ds(every, every)] = ab[...].T
    for copy, at in zip(second_out, (theirs, mine)):
        copy.wait_recv()
        sb[at, :] = (sp[at, :] + sr[at, :]).astype(BF)
    d_values[...] = -(sp[mine, :] + sr[mine, :])
    ec[...] += dot_nt(sb[...], r["cb"][...])
    gub = r["gub"]

    def pull_rows(at):
        g, u, d = gu[at, gl], gu[at, ul], da[at, :]
        p, q, back_a = pq[at, gl], pq[at, ul], ec[at, :]
        sig = jax.nn.sigmoid(g)
        sneg = 1.0 - sig
        h = g * sig
        slope = sig * (1.0 + g * sneg)
        bend = sig * sneg * (2.0 + g * (1.0 - 2.0 * sig))
        pd = p * d
        gub[at, gl] = (back_a * u * slope + pd * u * bend + q * d * slope).astype(BF)
        gub[at, ul] = (back_a * h + pd * slope).astype(BF)
    by_rows(every, 32, pull_rows)

    dsw, dloc = r["dsw"], r["dloc"]
    dloc[...] = (r["hdn"][...] + dot(r["taT"][:, pl.ds(0, every)], eb[...])
                 + dot(r["taT"][:, pl.ds(every, every)], sb[...])).astype(BF)
    swaps = []
    prow = 2 * rows
    for k in range(zs // 2):
        slot = (zs // 2) * c + k
        swaps.append(twin(dloc.at[block(2 * k + 1 - c, prow), :], dsw.at[slot], 10 + k))
        dsw[slot] = dloc[block(2 * k + c, prow), :]
    pay2 = r["pay2"]

    def last_block(zb, i):
        at = block(zb, zrows)
        pay2[at, wide] = (r["hp"][at, :] + dot(r["xT"][at, :], gub[...])).astype(BF)
        if i == 0:
            for copy in swaps:
                copy.wait_recv()
        for y in range(2):
            for x in range(2):
                pay2[block(4 * zb + 2 * y + x, rows), dl] = (
                    dsw[zb, y * rows:(y + 1) * rows, x * half:(x + 1) * half])

    def key_back():
        r["kp"][...] = dot(dgu[...], back[:, wide])

    def key_back_second():
        r["kp"][...] += dot_nt(gub[...], r["abb"][...])
        r["kin"] = twin(r["kp"].at[theirs, :], r["kr"], 10 + zs // 2)

    def query_out():
        r["qin"].wait_recv()
        d_queries[...] = (r["qp"][mine, :] + r["qr"][...]).astype(BF)

    last = r["last"]
    rs2 = reduce_scatter(net, pay2, scratch_of("rs", 2), last, last_block,
                         {0: key_back, 1: key_back_second, 2: query_out})
    fin = r["fin"]
    fin[block(net.g, rows), :] = last[...].astype(BF)
    s = scratch_of("ag", 2)
    own2, relay2 = {}, {}
    for p in range(2):
        own2[p] = spread_own(net, fin, 0, 0, p, s)
    for p in range(2):
        own2[p][0].wait_recv()
        relay2[p] = relay_side(net, fin, 0, 0, p, s)
    r["kin"].wait_recv()
    d_keys[...] = r["kp"][mine, :] + r["kr"][...]
    for p in range(2):
        own2[p][1].wait_recv()
        relay2[p].wait_recv()
    swap = twin(fin.at[block(1 - c, prow), wide], r["tw"], 11 + zs // 2)
    lanes = block(c, half)
    others = block(1 - c, half)
    d_gate[:, lanes] = fin[block(c, prow), gl].astype(F32) * inverse
    d_up[:, lanes] = fin[block(c, prow), ul].astype(F32) * inverse
    for y in range(2):
        for x in range(2):
            g = 2 * y + x
            d_down[y * rows:(y + 1) * rows, x * half:(x + 1) * half] = (
                fin[g * rows:(g + 1) * rows, width:].astype(F32) * inverse)
    swap.wait_recv()
    d_gate[:, others] = r["tw"][:, :half].astype(F32) * inverse
    d_up[:, others] = r["tw"][:, half:].astype(F32) * inverse
    drain(done + rs0 + ag0 + rs1 + ag1 + rs2)
    drain(own2[0] + own2[1] + list(relay2.values()))


def fused_step(queries, key_tokens, values, out_grad, w_gate, w_up, w_down, zs, inverse):
    toks, width = queries.shape
    half, every, rows = width // 2, 2 * toks, width // (4 * zs)
    total = width + half
    cut = 128 * ((total // 128 + 1) // 2)
    parts = (("a", cut), ("b", total - cut))
    names, shapes = [], []

    def add(name, spec):
        names.append(name)
        shapes.append(spec)

    for name, shape in (
        ("kf", (toks, width)), ("vf", (toks, width)), ("wab", (width, width)),
        ("wc", (half, width)), ("wabt", (width, width)), ("wct", (width, half)),
        ("gu", (every, width)), ("ep", (every, width)), ("er", (every, width)),
        ("da", (every, half)), ("grad", (rows, total)), ("hsum", (rows, total)),
        ("last", (rows, total)), ("sq", (4, rows, 128)), ("scale", (2, rows, 128)),
        ("hgu", (every, width)), ("dact", (every, half)), ("qp", (every, width)),
        ("qr", (toks, width)), ("hp", (width, width)), ("hdn", (half, width)),
        ("pq", (every, width)), ("ec", (every, half)), ("sp", (every, width)),
        ("sr", (every, width)), ("kp", (every, width)), ("kr", (toks, width)),
    ):
        add(name, VM(shape, F32))
    for name, shape in (
        ("xb", (every, width)), ("qb", (every, width)), ("ob", (every, width)),
        ("abb", (width, width)), ("cb", (half, width)), ("ab", (every, half)),
        ("eb", (every, width)), ("dgu", (every, width)), ("dguT", (width, every)),
        ("eT", (width, every)), ("oT", (width, every)), ("qT", (width, every)),
        ("xT", (width, every)), ("hd", (every, width)), ("hdT", (width, every)),
        ("hact", (every, half)), ("haT", (half, every)), ("tb", (every, half)),
        ("sb", (every, width)), ("taT", (half, 2 * every)), ("gub", (every, width)),
        ("dloc", (half, width)), ("dsw", (zs, 2 * rows, width)),
        ("pay0", (width, total)), ("pay1", (width, total)), ("pay2", (width, total)),
        ("full0", (width, total)), ("full1", (width, total)),
        ("fin", (4 * rows, total)), ("tw", (2 * rows, width)),
    ):
        add(name, VM(shape, BF))
    for k in range(3):
        for letter, size in parts:
            add("r1%s%d" % (letter, k), VM((zs, 2, rows, size), BF))
            add("r2%s%d" % (letter, k), VM((zs, rows, size), BF))
            add("zb%s%d" % (letter, k), VM((zs - 1, rows, size), BF))
            add("zr%s%d" % (letter, k), VM((zs - 1, rows, size), BF))
        for end in "sr":
            add("s1%s%d" % (end, k), DMA((zs, 2, 2)))
            add("s2%s%d" % (end, k), DMA((zs, 2)))
            add("s3%s%d" % (end, k), DMA((zs - 1, 2)))
    for k in range(3):
        for end in "sr":
            if k < 2:
                add("az%s%d" % (end, k), DMA((zs - 1, 2)))
            else:
                add("az%s%d" % (end, k), DMA((1, 2)))
            depth = zs if k < 2 else 1
            add("ao%s%d" % (end, k), DMA((depth, 2, 2)))
            add("af%s%d" % (end, k), DMA((depth, 2)))
    add("ld", DMA((7,)))
    add("ts", DMA((12 + zs // 2,)))
    add("tr", DMA((12 + zs // 2,)))
    all_names = ["in%d" % i for i in range(7)] + ["out%d" % i for i in range(6)] + names
    token = jax.ShapeDtypeStruct((toks, width), F32)
    weight = jax.ShapeDtypeStruct((2 * rows, width), F32)
    return pl.pallas_call(
        functools.partial(step_body, zs, all_names, inverse),
        out_shape=(jax.ShapeDtypeStruct((toks, width), BF), token, token, weight, weight, weight),
        in_specs=[pl.BlockSpec(memory_space=pl.ANY)] * 7,
        out_specs=[pl.BlockSpec(memory_space=VM)] * 6,
        scratch_shapes=shapes,
        compiler_params=pltpu.CompilerParams(
            collective_id=0, has_side_effects=True, vmem_limit_bytes=62 * 1024 * 1024),
    )(queries, key_tokens, values, out_grad, w_gate, w_up, w_down)


def matmul(left, right):
    return dot(left.astype(BF), right.astype(BF))


def key_grad(w_gate, w_up, w_down, key_rows, value_rows):
    hidden_gate = matmul(key_rows, w_gate)
    hidden_up = matmul(key_rows, w_up)
    sig = jax.nn.sigmoid(hidden_gate)
    active = hidden_gate * sig * hidden_up
    error = matmul(active, w_down) - value_rows
    d_active = matmul(error, w_down.T)
    d_hup = d_active * hidden_gate * sig
    d_hgate = d_active * hidden_up * sig * (1.0 + hidden_gate * (1.0 - sig))
    return (matmul(d_hgate.T, key_rows), matmul(d_hup.T, key_rows), matmul(error.T, active))


def query_grad(fast_t, query_rows, grad_rows):
    gate_t, up_t, down_t = fast_t
    hidden_gate = dot(query_rows, gate_t.T)
    hidden_up = dot(query_rows, up_t.T)
    sig = jax.nn.sigmoid(hidden_gate)
    active = (hidden_gate * sig * hidden_up).astype(BF)
    d_active = dot(grad_rows, down_t)
    d_hup = (d_active * hidden_gate * sig).astype(BF)
    d_hgate = (d_active * hidden_up * sig * (1.0 + hidden_gate * (1.0 - sig))).astype(BF)
    d_rows = (dot(d_hgate, gate_t) + dot(d_hup, up_t)).astype(BF)
    return (d_rows, active, d_hgate, d_hup)


def general_step(queries, key_tokens, values, out_grad, w_gate, w_up, w_down, inverse):
    gs, toks = lax.axis_size("grp"), lax.axis_size("tok")
    full_width = w_gate.shape[0]
    rows = 3 * full_width // (gs * toks)
    me = lax.axis_index("tok") * gs + lax.axis_index("grp")

    def reduce_units(x):
        y = x.reshape(toks, gs * rows, full_width)
        y = lax.psum_scatter(y, "tok", scatter_dimension=0, tiled=True)[0]
        return lax.psum_scatter(y.reshape(gs, rows, full_width), "grp", scatter_dimension=0, tiled=True)[0]

    def gather_units(y):
        full = lax.all_gather(lax.all_gather(y, "grp"), "tok").reshape(3, full_width, full_width)
        return full[0], full[1], full[2]

    local_grad, pullback = jax.vjp(key_grad, w_gate, w_up, w_down, key_tokens, values)
    grad = reduce_units(jnp.stack(local_grad))
    scale = jnp.sqrt(jnp.sum(grad * grad, axis=1, keepdims=True) / full_width + EPSILON)
    weights = jnp.concatenate((w_gate, w_up, w_down), axis=1)
    mine = lax.dynamic_slice_in_dim(weights, me * rows, rows, 1).T
    fast_t = gather_units((mine - STEP_SIZE * grad / scale).astype(BF))
    d_queries, active, d_hgate, d_hup = query_grad(fast_t, queries, out_grad)
    query_part = reduce_units(
        jnp.stack((dot(d_hgate.T, queries), dot(d_hup.T, queries), dot(out_grad.T, active))))
    product = jnp.sum(-STEP_SIZE * query_part * grad, axis=1, keepdims=True)
    cot = (
        -STEP_SIZE * query_part / scale - grad * product / (full_width * scale * scale * scale)
    ).astype(BF)
    second = pullback(tuple(item.astype(F32) for item in gather_units(cot)))
    plain = (dot(queries.T, d_hgate), dot(queries.T, d_hup), dot(active.T, out_grad))
    combined = jnp.stack(tuple(left + right for left, right in zip(plain, second[:3])))
    combined = combined.reshape(3, toks, full_width // toks, full_width).transpose(1, 0, 2, 3)
    summed = lax.all_gather(reduce_units(combined).astype(BF), "grp").astype(F32) * inverse
    summed = summed.reshape(3, full_width // toks, full_width)
    return (d_queries, second[3], second[4], summed[0], summed[1], summed[2])


def on_device(*arrays):
    gs, toks = lax.axis_size("grp"), lax.axis_size("tok")
    tokens, width = arrays[0].shape
    inverse = 1.0 / (tokens * gs * toks)
    zs = toks // 2
    fits = gs == 4 and toks % 4 == 0 and zs & (zs - 1) == 0
    if fits and width % (64 * zs) == 0 and width % 256 == 0 and tokens % 128 == 0:
        return fused_step(*arrays, zs, inverse)
    return general_step(*arrays, inverse)


def solution(mesh):
    token = P(("grp", "tok"), None)
    return jax.shard_map(
        on_device,
        mesh=mesh,
        in_specs=(token, token, token, token, P(), P(), P()),
        out_specs=(token, token, token, P("tok", None), P("tok", None), P("tok", None)),
        check_vma=False,
    )
```

```python
import functools

import jax
import jax.numpy as jnp
from jax import lax
from jax.experimental import pallas as pl
from jax.experimental.pallas import tpu as pltpu
from jax.sharding import PartitionSpec as P

STEP_SIZE = 0.02
EPSILON = 1e-06
MESH = pl.DeviceIdType.MESH
BF = jnp.bfloat16
F32 = jnp.float32
VM = pltpu.VMEM
DMA = pltpu.SemaphoreType.DMA


def dot(left, right):
    return jnp.dot(left, right, preferred_element_type=F32)


def dot_nt(left, right):
    return lax.dot_general(left, right, (((1,), (1,)), ((), ())), preferred_element_type=F32)


def block(index, size):
    return pl.ds(pl.multiple_of(index * size, size), size)


class Net:
    def __init__(self, zs, rows, width):
        g, t = lax.axis_index("grp"), lax.axis_index("tok")
        self.zs, self.rows = zs, rows
        self.g, self.z, self.c = g, t // 2, lax.rem(t, 2)
        self.y, self.x = g // 2, lax.rem(g, 2)
        self.t = t
        cut = 128 * ((width // 128 + 1) // 2)
        self.lanes = (pl.ds(0, cut), pl.ds(cut, width - cut))
        self.twin = (g, 2 * self.z + 1 - self.c)

    def flip(self, *directions):
        y, x = self.y, self.x
        for a in directions:
            if a == 0:
                x = 1 - x
            else:
                y = 1 - y
        return y, x

    def side(self, a):
        y, x = self.flip(a)
        return (2 * y + x, self.t)

    def at_z(self, z):
        return (self.g, 2 * z + self.c)

    def pick(self, table):
        value = table[0]
        for z in range(1, self.zs):
            value = jnp.where(self.z == z, table[z], value)
        return value

    def chunk(self, zb, yx):
        return block(4 * zb + 2 * yx[0] + yx[1], self.rows)

    def greet(self):
        barrier = pltpu.get_barrier_semaphore()
        peers = [self.twin, self.side(0), self.side(1)]
        for peer in peers:
            pl.semaphore_signal(barrier, inc=1, device_id=peer, device_id_type=MESH)
        for z in range(self.zs):
            near = [other for other in (z - 1, z + 1) if 0 <= other < self.zs]

            @pl.when(self.z == z)
            def _():
                for other in near:
                    pl.semaphore_signal(
                        barrier, inc=1, device_id=self.at_z(other), device_id_type=MESH)
                pl.semaphore_wait(barrier, len(peers) + len(near))


def send(src, dst, sems, at, peer, there=None):
    copy = pltpu.make_async_remote_copy(
        src_ref=src, dst_ref=dst, send_sem=sems[0].at[at],
        recv_sem=sems[1].at[at if there is None else there],
        device_id=peer, device_id_type=MESH,
    )
    copy.start()
    return copy


def await_copy(net, ref, sems, at, there=None):
    copy = pltpu.make_async_remote_copy(
        src_ref=ref, dst_ref=ref, send_sem=sems[0].at[at if there is None else there],
        recv_sem=sems[1].at[at], device_id=net.twin, device_id_type=MESH,
    )
    if there is None:
        copy.wait_recv()
    else:
        copy.wait_send()


def sum_order(zs, z):
    def key(zb):
        hops = z if zb > z else zs - 1 - z
        return (zb == z, hops, -abs(zb - z))
    return sorted(range(zs), key=key)


def spread_order(zs, z):
    return sorted(range(zs), key=lambda zb: (abs(zb - z), (zb > z) == (2 * z < zs)))


def reduce_scatter(net, pay, s, total, produce, fillers):
    zs = net.zs
    orders = [sum_order(zs, z) for z in range(zs)]
    blocks = [net.pick([orders[z][i] for z in range(zs)]) for i in range(zs)]
    first, second = {}, {}

    def start_first(i, k):
        for p in range(2):
            a = (p + i) % 2
            yx = net.flip(a, 1 - a) if k == 0 else net.flip(a)
            first[i, p, k] = send(
                pay.at[net.chunk(blocks[i], yx), net.lanes[p]], s["r1"][p].at[i, k],
                s["s1"], (i, p, k), net.side(a))

    def start_second(i):
        for p in range(2):
            a = (p + i) % 2
            first[i, p, 0].wait_recv()
            at = (net.chunk(blocks[i], net.flip(1 - a)), net.lanes[p])
            pay[at] = (pay[at].astype(F32) + s["r1"][p][i, 0].astype(F32)).astype(BF)
            second[i, p] = send(pay.at[at], s["r2"][p].at[i], s["s2"], (i, p), net.side(1 - a))

    def along(z, i):
        zb = orders[z][i]
        for p in range(2):
            first[i, p, 1].wait_recv()
            second[i, p].wait_recv()
            at = (net.chunk(zb, (net.y, net.x)), net.lanes[p])
            value = (pay[at].astype(F32) + s["r1"][p][i, 1].astype(F32)
                     + s["r2"][p][i].astype(F32))
            slots = []
            if zb >= z and z > 0:
                slots.append(i)
            if zb <= z and z < zs - 1:
                slots.append(i if zb < z else zs)
            for slot in slots:
                await_copy(net, s["zr"][p].at[slot], s["s3"], (slot, p))
                value = value + s["zr"][p][slot].astype(F32)
            if zb == z:
                total[:, net.lanes[p]] = value
            else:
                s["zb"][p][i] = value.astype(BF)
                nxt = z + 1 if zb > z else z - 1
                slot = orders[nxt].index(zb) if nxt != zb or zb > z else zs
                send(s["zb"][p].at[i], s["zr"][p].at[slot], s["s3"], (i, p), net.at_z(nxt),
                     (slot, p))

    last = 0
    steps = [{} for _ in range(zs)]
    for z in range(zs):
        for i, zb in enumerate(orders[z]):
            hops = 0 if zb == z else z if zb > z else zs - 1 - z
            when = max(i + 2 + hops, last if zb == z else 0)
            if zb == z:
                when = max([when] + list(steps[z]))
            steps[z].setdefault(when, []).append(i)
            last = max(last, when)
    for i in range(last + 1):
        if i < zs:
            produce(blocks[i], i)
            start_first(i, 0)
        if 1 <= i <= zs:
            start_second(i - 1)
        if i < zs:
            start_first(i, 1)
            if i in fillers:
                fillers[i]()
        for z in range(zs):
            if i in steps[z]:
                @pl.when(net.z == z)
                def _():
                    for k in steps[z][i]:
                        along(z, k)

    def finish():
        drain([*first.values(), *second.values()])
        for i in range(zs - 1):
            for p in range(2):
                await_copy(net, s["zb"][p].at[i], s["s3"], (i, p), (i, p))
    return finish


def spread_own(net, full, zb, i, p, s):
    a = (p + i) % 2
    at = (net.chunk(zb, (net.y, net.x)), net.lanes[p])
    return [send(full.at[at], full.at[at], s["o"], (i, p, k), net.side(d))
            for k, d in enumerate((a, 1 - a))]


def relay_side(net, full, zb, i, p, s):
    a = (p + i) % 2
    at = (net.chunk(zb, net.flip(a)), net.lanes[p])
    return send(full.at[at], full.at[at], s["f"], (i, p), net.side(1 - a))


def all_gather(net, full, s, parts):
    zs = net.zs

    def pass_on(z, zb, p):
        at = (net.chunk(zb, (net.y, net.x)), net.lanes[p])
        for k, other in enumerate((z - 1, z + 1)):
            if 0 <= other < zs and (zb == z or (zb > z) == (other < z)):
                send(full.at[at], full.at[at], s["z"], (zb, p, k), net.at_z(other), (zb, p, 0))

    def left(z, zb, p):
        at = (net.chunk(zb, (net.y, net.x)), net.lanes[p])
        for k, other in enumerate((z - 1, z + 1)):
            if 0 <= other < zs and (zb == z or (zb > z) == (other < z)):
                await_copy(net, full.at[at], s["z"], (zb, p, 0), (zb, p, k))

    def at_each(body):
        for z in range(zs):
            @pl.when(net.z == z)
            def _():
                body(z)

    for p in range(2):
        parts[p]()
        at_each(lambda z: pass_on(z, z, p))
        spread_own(net, full, net.z, 0, p, s)

    def rest(z):
        order = spread_order(zs, z)

        def forward(i):
            for p in range(2):
                at = (net.chunk(order[i], net.flip((p + i) % 2)), net.lanes[p])
                await_copy(net, full.at[at], s["o"], (i, p, 0))
                relay_side(net, full, order[i], i, p, s)

        for i in range(1, zs):
            for p in range(2):
                at = (net.chunk(order[i], (net.y, net.x)), net.lanes[p])
                await_copy(net, full.at[at], s["z"], (order[i], p, 0))
                pass_on(z, order[i], p)
                spread_own(net, full, order[i], i, p, s)
            forward(i - 1)
        forward(zs - 1)
        for i in range(zs):
            for p in range(2):
                a = (p + i) % 2
                at = (net.chunk(order[i], net.flip(1 - a)), net.lanes[p])
                await_copy(net, full.at[at], s["o"], (i, p, 1))
                at = (net.chunk(order[i], net.flip(0, 1)), net.lanes[p])
                await_copy(net, full.at[at], s["f"], (i, p))

    at_each(rest)

    def finish():
        def go(z):
            order = spread_order(zs, z)
            for i in range(zs):
                for p in range(2):
                    at = (net.chunk(order[i], (net.y, net.x)), net.lanes[p])
                    left(z, order[i], p)
                    for k in range(2):
                        await_copy(net, full.at[at], s["o"], (i, p, k), (i, p, k))
                    await_copy(net, full.at[at], s["f"], (i, p), (i, p))
        at_each(go)
    return finish


def drain(copies):
    for copy in copies:
        copy.wait_send()


def by_rows(count, step, body):
    def run(i, carry):
        body(pl.ds(pl.multiple_of(i * step, step), step))
        return carry
    lax.fori_loop(0, count // step, run, 0)


def step_body(zs, names, inverse, *refs):
    r = dict(zip(names, refs))
    (queries, keys, values, out_grad, w_gate, w_up, w_down) = refs[:7]
    (d_queries, d_keys, d_values, d_gate, d_up, d_down) = refs[7:13]
    toks, width = queries.shape
    half = width // 2
    every = 2 * toks
    rows = width // (4 * zs)
    zrows = 4 * rows
    net = Net(zs, rows, width + half)
    c = net.c
    mine, theirs = block(c, toks), block(1 - c, toks)
    gl, ul, dl = pl.ds(0, half), pl.ds(half, half), pl.ds(width, half)
    wide = pl.ds(0, width)
    hid = block(c, half)

    loads = {}
    for i, (name, src, dst) in enumerate((
        ("k", keys, r["kf"]),
        ("a", w_gate.at[:, hid], r["wab"].at[:, gl]),
        ("b", w_up.at[:, hid], r["wab"].at[:, ul]),
        ("c", w_down.at[hid, :], r["wc"]),
        ("v", values, r["vf"]),
        ("q", queries, r["qb"].at[mine, :]),
        ("o", out_grad, r["ob"].at[mine, :]),
    )):
        loads[name] = pltpu.make_async_copy(src, dst, r["ld"].at[i])
        loads[name].start()
    net.greet()
    tsem = (r["ts"], r["tr"])
    done = []

    def twin(src, dst, k):
        copy = send(src, dst, tsem, k, net.twin)
        done.append(copy)
        return copy

    def scratch_of(kind, k):
        if kind == "rs":
            return {
                "r1": (r["r1a%d" % k], r["r1b%d" % k]), "r2": (r["r2a%d" % k], r["r2b%d" % k]),
                "zb": (r["zba%d" % k], r["zbb%d" % k]), "zr": (r["zra%d" % k], r["zrb%d" % k]),
                "s1": (r["s1s%d" % k], r["s1r%d" % k]), "s2": (r["s2s%d" % k], r["s2r%d" % k]),
                "s3": (r["s3s%d" % k], r["s3r%d" % k]),
            }
        return {
            "z": (r["azs%d" % k], r["azr%d" % k]), "o": (r["aos%d" % k], r["aor%d" % k]),
            "f": (r["afs%d" % k], r["afr%d" % k]),
        }

    xb, gu, ab, eb = r["xb"], r["gu"], r["ab"], r["eb"]
    loads["k"].wait()
    xb[mine, :] = r["kf"][...].astype(BF)
    keys_in = twin(xb.at[mine, :], xb.at[mine, :], 0)
    loads["a"].wait()
    loads["b"].wait()
    r["abb"][...] = r["wab"][...].astype(BF)
    loads["c"].wait()
    r["cb"][...] = r["wc"][...].astype(BF)
    loads["q"].wait()
    queries_in = twin(r["qb"].at[mine, :], r["qb"].at[mine, :], 1)
    loads["o"].wait()
    grads_in = twin(r["ob"].at[mine, :], r["ob"].at[mine, :], 2)
    keys_in.wait_recv()
    gu[...] = dot(xb[...], r["abb"][...])

    def active_rows(at):
        g, u = gu[at, gl], gu[at, ul]
        ab[at, :] = (g * jax.nn.sigmoid(g) * u).astype(BF)
    by_rows(every, 32, active_rows)

    loads["v"].wait()
    ep, er = r["ep"], r["er"]
    ep[mine, :] = dot(ab[mine, :], r["cb"][...]) - r["vf"][...]
    e_out = [twin(ep.at[mine, :], er.at[mine, :], 3)]
    ep[theirs, :] = dot(ab[theirs, :], r["cb"][...])
    e_out.append(twin(ep.at[theirs, :], er.at[theirs, :], 4))
    for copy, at in zip(e_out, (theirs, mine)):
        copy.wait_recv()
        eb[at, :] = (ep[at, :] + er[at, :]).astype(BF)
    da, dgu = r["da"], r["dgu"]
    da[...] = dot_nt(eb[...], r["cb"][...])

    def d_rows(at):
        g, u, d = gu[at, gl], gu[at, ul], da[at, :]
        sig = jax.nn.sigmoid(g)
        dgu[at, ul] = (d * g * sig).astype(BF)
        dgu[at, gl] = (d * u * sig * (1.0 + g * (1.0 - sig))).astype(BF)
    by_rows(every, 32, d_rows)
    r["dguT"][...] = dgu[...].T
    r["eT"][...] = eb[...].T

    pay = r["pay0"]

    def key_block(zb, i):
        at = block(zb, zrows)
        pay[at, wide] = dot(r["dguT"][at, :], xb[...]).astype(BF)
        pay[at, dl] = dot(r["eT"][at, :], ab[...]).astype(BF)

    def turn_weights():
        r["wabt"][...] = r["wab"][...].T
        r["wct"][...] = r["wc"][...].T

    def turn_grads():
        grads_in.wait_recv()
        r["oT"][...] = r["ob"][...].T

    def turn_queries():
        queries_in.wait_recv()
        r["qT"][...] = r["qb"][...].T

    def turn_keys():
        r["xT"][...] = xb[...].T

    grad = r["grad"]
    rs0 = reduce_scatter(net, pay, scratch_of("rs", 0), grad, key_block,
                         {0: turn_grads, 1: turn_queries, 2: turn_keys, 3: turn_weights})

    own = net.chunk(net.z, (net.y, net.x))
    squares = jnp.sum(grad[:, dl] * grad[:, dl], axis=1, keepdims=True)
    r["sq"][0] = jnp.broadcast_to(squares, (rows, 128))
    norm_in = twin(r["sq"].at[0], r["sq"].at[1], 5)
    scale_of = lambda sq: jnp.sqrt(sq / width + EPSILON)
    full = r["full0"]
    scale = r["scale"]

    def wide_part():
        g = grad[:, wide]
        sc = scale_of(jnp.sum(g * g, axis=1, keepdims=True))
        scale[0] = jnp.broadcast_to(sc, (rows, 128))
        full[own, wide] = (r["wabt"][own, :] - STEP_SIZE * g / sc).astype(BF)

    def down_part():
        norm_in.wait_recv()
        sc = scale_of((r["sq"][0] + r["sq"][1])[:, :1])
        scale[1] = jnp.broadcast_to(sc, (rows, 128))
        full[own, dl] = (r["wct"][own, :] - STEP_SIZE * grad[:, dl] / sc).astype(BF)

    ag0 = all_gather(net, full, scratch_of("ag", 0), (wide_part, down_part))

    hgu, hd, hact, dact = r["hgu"], r["hd"], r["hact"], r["dact"]
    hgu[...] = dot_nt(r["qb"][...], full[:, wide])
    dact[...] = dot(r["ob"][...], full[:, dl])

    def query_rows(at):
        g, u, d = hgu[at, gl], hgu[at, ul], dact[at, :]
        sig = jax.nn.sigmoid(g)
        hact[at, :] = (g * sig * u).astype(BF)
        hd[at, ul] = (d * g * sig).astype(BF)
        hd[at, gl] = (d * u * sig * (1.0 + g * (1.0 - sig))).astype(BF)
    by_rows(every, 32, query_rows)
    r["hdT"][...] = hd[...].T
    pay1 = r["pay1"]

    def query_block(zb, i):
        at = block(zb, zrows)
        pay1[at, wide] = dot(r["hdT"][at, :], r["qb"][...]).astype(BF)
        pay1[at, dl] = dot(r["oT"][at, :], hact[...]).astype(BF)

    def query_back():
        r["qp"][...] = dot(hd[...], full[:, wide])
        r["qin"] = twin(r["qp"].at[theirs, :], r["qr"], 6)

    def plain_wide():
        r["hp"][...] = dot(r["qT"][...], hd[...])

    def plain_down():
        r["haT"][...] = hact[...].T
        r["hdn"][...] = dot(r["haT"][...], r["ob"][...])

    hsum = r["hsum"]
    rs1 = reduce_scatter(net, pay1, scratch_of("rs", 1), hsum, query_block,
                         {0: query_back, 1: plain_wide, 2: plain_down})

    product = jnp.sum(-STEP_SIZE * hsum[:, dl] * grad[:, dl], axis=1, keepdims=True)
    r["sq"][2] = jnp.broadcast_to(product, (rows, 128))
    product_in = twin(r["sq"].at[2], r["sq"].at[3], 7)
    back = r["full1"]

    def turned(h, g, sc, prod):
        return (-STEP_SIZE * h / sc - g * prod / (width * sc * sc * sc)).astype(BF)

    def wide_back():
        h, g = hsum[:, wide], grad[:, wide]
        prod = jnp.sum(-STEP_SIZE * h * g, axis=1, keepdims=True)
        back[own, wide] = turned(h, g, scale[0][:, :1], prod)

    def down_back():
        product_in.wait_recv()
        prod = (r["sq"][2] + r["sq"][3])[:, :1]
        back[own, dl] = turned(hsum[:, dl], grad[:, dl], scale[1][:, :1], prod)

    ag1 = all_gather(net, back, scratch_of("ag", 1), (wide_back, down_back))

    pq, tb, ec = r["pq"], r["tb"], r["ec"]
    pq[...] = dot_nt(xb[...], back[:, wide])
    ec[...] = dot(eb[...], back[:, dl])

    def t_rows(at):
        g, u = gu[at, gl], gu[at, ul]
        p, q = pq[at, gl], pq[at, ul]
        sig = jax.nn.sigmoid(g)
        tb[at, :] = (q * g * sig + p * u * sig * (1.0 + g * (1.0 - sig))).astype(BF)
    by_rows(every, 32, t_rows)
    sp, sr, sb = r["sp"], r["sr"], r["sb"]
    second_out = []
    for k, at in enumerate((mine, theirs)):
        sp[at, :] = dot_nt(ab[at, :], back[:, dl]) + dot(tb[at, :], r["cb"][...])
        second_out.append(twin(sp.at[at, :], sr.at[at, :], 8 + k))
    r["taT"][:, pl.ds(0, every)] = tb[...].T
    r["taT"][:, pl.ds(every, every)] = ab[...].T
    for copy, at in zip(second_out, (theirs, mine)):
        copy.wait_recv()
        sb[at, :] = (sp[at, :] + sr[at, :]).astype(BF)
    d_values[...] = -(sp[mine, :] + sr[mine, :])
    ec[...] += dot_nt(sb[...], r["cb"][...])
    gub = r["gub"]

    def pull_rows(at):
        g, u, d = gu[at, gl], gu[at, ul], da[at, :]
        p, q, back_a = pq[at, gl], pq[at, ul], ec[at, :]
        sig = jax.nn.sigmoid(g)
        sneg = 1.0 - sig
        h = g * sig
        slope = sig * (1.0 + g * sneg)
        bend = sig * sneg * (2.0 + g * (1.0 - 2.0 * sig))
        pd = p * d
        gub[at, gl] = (back_a * u * slope + pd * u * bend + q * d * slope).astype(BF)
        gub[at, ul] = (back_a * h + pd * slope).astype(BF)
    by_rows(every, 32, pull_rows)

    dsw, dloc = r["dsw"], r["dloc"]
    dloc[...] = (r["hdn"][...] + dot(r["taT"][:, pl.ds(0, every)], eb[...])
                 + dot(r["taT"][:, pl.ds(every, every)], sb[...])).astype(BF)
    swaps = []
    prow = 2 * rows
    for k in range(zs // 2):
        slot = (zs // 2) * c + k
        swaps.append(twin(dloc.at[block(2 * k + 1 - c, prow), :], dsw.at[slot], 10 + k))
        dsw[slot] = dloc[block(2 * k + c, prow), :]
    pay2 = r["pay2"]

    def last_block(zb, i):
        at = block(zb, zrows)
        pay2[at, wide] = (r["hp"][at, :] + dot(r["xT"][at, :], gub[...])).astype(BF)
        if i == 0:
            for copy in swaps:
                copy.wait_recv()
        for y in range(2):
            for x in range(2):
                pay2[block(4 * zb + 2 * y + x, rows), dl] = (
                    dsw[zb, y * rows:(y + 1) * rows, x * half:(x + 1) * half])

    def key_back():
        r["kp"][...] = dot(dgu[...], back[:, wide])

    def key_back_second():
        r["kp"][...] += dot_nt(gub[...], r["abb"][...])
        r["kin"] = twin(r["kp"].at[theirs, :], r["kr"], 10 + zs // 2)

    def query_out():
        r["qin"].wait_recv()
        d_queries[...] = (r["qp"][mine, :] + r["qr"][...]).astype(BF)

    last = r["last"]
    rs2 = reduce_scatter(net, pay2, scratch_of("rs", 2), last, last_block,
                         {0: key_back, 1: key_back_second, 2: query_out})
    fin = r["fin"]
    fin[block(net.g, rows), :] = last[...].astype(BF)
    s = scratch_of("ag", 2)
    own2, relay2 = {}, {}
    for p in range(2):
        own2[p] = spread_own(net, fin, 0, 0, p, s)
    for p in range(2):
        own2[p][0].wait_recv()
        relay2[p] = relay_side(net, fin, 0, 0, p, s)
    r["kin"].wait_recv()
    d_keys[...] = r["kp"][mine, :] + r["kr"][...]
    for p in range(2):
        own2[p][1].wait_recv()
        relay2[p].wait_recv()
    swap = twin(fin.at[block(1 - c, prow), wide], r["tw"], 11 + zs // 2)
    lanes = block(c, half)
    others = block(1 - c, half)
    d_gate[:, lanes] = fin[block(c, prow), gl].astype(F32) * inverse
    d_up[:, lanes] = fin[block(c, prow), ul].astype(F32) * inverse
    for y in range(2):
        for x in range(2):
            g = 2 * y + x
            d_down[y * rows:(y + 1) * rows, x * half:(x + 1) * half] = (
                fin[g * rows:(g + 1) * rows, width:].astype(F32) * inverse)
    swap.wait_recv()
    d_gate[:, others] = r["tw"][:, :half].astype(F32) * inverse
    d_up[:, others] = r["tw"][:, half:].astype(F32) * inverse
    drain(done)
    for finish in (rs0, ag0, rs1, ag1, rs2):
        finish()
    drain(own2[0] + own2[1] + list(relay2.values()))


def hand_over(*refs):
    for src, dst in zip(refs[:6], refs[6:]):
        dst[...] = src[...]


def fused_step(queries, key_tokens, values, out_grad, w_gate, w_up, w_down, zs, inverse):
    toks, width = queries.shape
    half, every, rows = width // 2, 2 * toks, width // (4 * zs)
    total = width + half
    cut = 128 * ((total // 128 + 1) // 2)
    parts = (("a", cut), ("b", total - cut))
    names, shapes = [], []

    def add(name, spec):
        names.append(name)
        shapes.append(spec)

    for name, shape in (
        ("kf", (toks, width)), ("vf", (toks, width)), ("wab", (width, width)),
        ("wc", (half, width)), ("wabt", (width, width)), ("wct", (width, half)),
        ("gu", (every, width)), ("ep", (every, width)), ("er", (every, width)),
        ("da", (every, half)), ("grad", (rows, total)), ("hsum", (rows, total)),
        ("last", (rows, total)), ("sq", (4, rows, 128)), ("scale", (2, rows, 128)),
        ("hgu", (every, width)), ("dact", (every, half)), ("qp", (every, width)),
        ("qr", (toks, width)), ("hp", (width, width)), ("hdn", (half, width)),
        ("pq", (every, width)), ("ec", (every, half)), ("sp", (every, width)),
        ("sr", (every, width)), ("kp", (every, width)), ("kr", (toks, width)),
    ):
        add(name, VM(shape, F32))
    for name, shape in (
        ("xb", (every, width)), ("qb", (every, width)), ("ob", (every, width)),
        ("abb", (width, width)), ("cb", (half, width)), ("ab", (every, half)),
        ("eb", (every, width)), ("dgu", (every, width)), ("dguT", (width, every)),
        ("eT", (width, every)), ("oT", (width, every)), ("qT", (width, every)),
        ("xT", (width, every)), ("hd", (every, width)), ("hdT", (width, every)),
        ("hact", (every, half)), ("haT", (half, every)), ("tb", (every, half)),
        ("sb", (every, width)), ("taT", (half, 2 * every)), ("gub", (every, width)),
        ("dloc", (half, width)), ("dsw", (zs, 2 * rows, width)),
        ("pay0", (width, total)), ("pay1", (width, total)), ("pay2", (width, total)),
        ("full0", (width, total)), ("full1", (width, total)),
        ("fin", (4 * rows, total)), ("tw", (2 * rows, width)),
    ):
        add(name, VM(shape, BF))
    for k in range(3):
        for letter, size in parts:
            add("r1%s%d" % (letter, k), VM((zs, 2, rows, size), BF))
            add("r2%s%d" % (letter, k), VM((zs, rows, size), BF))
            add("zb%s%d" % (letter, k), VM((zs - 1, rows, size), BF))
            add("zr%s%d" % (letter, k), VM((zs + 1, rows, size), BF))
        for end in "sr":
            add("s1%s%d" % (end, k), DMA((zs, 2, 2)))
            add("s2%s%d" % (end, k), DMA((zs, 2)))
            add("s3%s%d" % (end, k), DMA((zs + 1, 2)))
    for k in range(3):
        for end in "sr":
            if k < 2:
                add("az%s%d" % (end, k), DMA((zs, 2, 2)))
            else:
                add("az%s%d" % (end, k), DMA((1, 2, 2)))
            depth = zs if k < 2 else 1
            add("ao%s%d" % (end, k), DMA((depth, 2, 2)))
            add("af%s%d" % (end, k), DMA((depth, 2)))
    add("ld", DMA((7,)))
    add("ts", DMA((12 + zs // 2,)))
    add("tr", DMA((12 + zs // 2,)))
    all_names = ["in%d" % i for i in range(7)] + ["out%d" % i for i in range(6)] + names
    token = jax.ShapeDtypeStruct((toks, width), F32)
    weight = jax.ShapeDtypeStruct((2 * rows, width), F32)
    results = pl.pallas_call(
        functools.partial(step_body, zs, all_names, inverse),
        out_shape=(jax.ShapeDtypeStruct((toks, width), BF), token, token, weight, weight, weight),
        in_specs=[pl.BlockSpec(memory_space=pltpu.HBM)] * 7,
        out_specs=[pl.BlockSpec(memory_space=VM)] * 6,
        scratch_shapes=shapes,
        compiler_params=pltpu.CompilerParams(
            collective_id=0, has_side_effects=True, vmem_limit_bytes=50 * 1024 * 1024),
    )(*(pltpu.with_memory_space_constraint(x, pltpu.HBM) for x in (
        queries, key_tokens, values, out_grad, w_gate, w_up, w_down)))
    return pl.pallas_call(
        hand_over,
        out_shape=tuple(jax.ShapeDtypeStruct(item.shape, item.dtype) for item in results),
        in_specs=[pl.BlockSpec(memory_space=VM)] * 6,
        out_specs=[pl.BlockSpec(memory_space=VM)] * 6,
        compiler_params=pltpu.CompilerParams(vmem_limit_bytes=8 * 1024 * 1024),
    )(*results)


def matmul(left, right):
    return dot(left.astype(BF), right.astype(BF))


def key_grad(w_gate, w_up, w_down, key_rows, value_rows):
    hidden_gate = matmul(key_rows, w_gate)
    hidden_up = matmul(key_rows, w_up)
    sig = jax.nn.sigmoid(hidden_gate)
    active = hidden_gate * sig * hidden_up
    error = matmul(active, w_down) - value_rows
    d_active = matmul(error, w_down.T)
    d_hup = d_active * hidden_gate * sig
    d_hgate = d_active * hidden_up * sig * (1.0 + hidden_gate * (1.0 - sig))
    return (matmul(d_hgate.T, key_rows), matmul(d_hup.T, key_rows), matmul(error.T, active))


def query_grad(fast_t, query_rows, grad_rows):
    gate_t, up_t, down_t = fast_t
    hidden_gate = dot(query_rows, gate_t.T)
    hidden_up = dot(query_rows, up_t.T)
    sig = jax.nn.sigmoid(hidden_gate)
    active = (hidden_gate * sig * hidden_up).astype(BF)
    d_active = dot(grad_rows, down_t)
    d_hup = (d_active * hidden_gate * sig).astype(BF)
    d_hgate = (d_active * hidden_up * sig * (1.0 + hidden_gate * (1.0 - sig))).astype(BF)
    d_rows = (dot(d_hgate, gate_t) + dot(d_hup, up_t)).astype(BF)
    return (d_rows, active, d_hgate, d_hup)


def general_step(queries, key_tokens, values, out_grad, w_gate, w_up, w_down, inverse):
    gs, toks = lax.axis_size("grp"), lax.axis_size("tok")
    full_width = w_gate.shape[0]
    rows = 3 * full_width // (gs * toks)
    me = lax.axis_index("tok") * gs + lax.axis_index("grp")

    def reduce_units(x):
        y = x.reshape(toks, gs * rows, full_width)
        y = lax.psum_scatter(y, "tok", scatter_dimension=0, tiled=True)[0]
        return lax.psum_scatter(y.reshape(gs, rows, full_width), "grp", scatter_dimension=0, tiled=True)[0]

    def gather_units(y):
        full = lax.all_gather(lax.all_gather(y, "grp"), "tok").reshape(3, full_width, full_width)
        return full[0], full[1], full[2]

    local_grad, pullback = jax.vjp(key_grad, w_gate, w_up, w_down, key_tokens, values)
    grad = reduce_units(jnp.stack(local_grad))
    scale = jnp.sqrt(jnp.sum(grad * grad, axis=1, keepdims=True) / full_width + EPSILON)
    weights = jnp.concatenate((w_gate, w_up, w_down), axis=1)
    mine = lax.dynamic_slice_in_dim(weights, me * rows, rows, 1).T
    fast_t = gather_units((mine - STEP_SIZE * grad / scale).astype(BF))
    d_queries, active, d_hgate, d_hup = query_grad(fast_t, queries, out_grad)
    query_part = reduce_units(
        jnp.stack((dot(d_hgate.T, queries), dot(d_hup.T, queries), dot(out_grad.T, active))))
    product = jnp.sum(-STEP_SIZE * query_part * grad, axis=1, keepdims=True)
    cot = (
        -STEP_SIZE * query_part / scale - grad * product / (full_width * scale * scale * scale)
    ).astype(BF)
    second = pullback(tuple(item.astype(F32) for item in gather_units(cot)))
    plain = (dot(queries.T, d_hgate), dot(queries.T, d_hup), dot(active.T, out_grad))
    combined = jnp.stack(tuple(left + right for left, right in zip(plain, second[:3])))
    combined = combined.reshape(3, toks, full_width // toks, full_width).transpose(1, 0, 2, 3)
    summed = lax.all_gather(reduce_units(combined).astype(BF), "grp").astype(F32) * inverse
    summed = summed.reshape(3, full_width // toks, full_width)
    return (d_queries, second[3], second[4], summed[0], summed[1], summed[2])


def on_device(*arrays):
    gs, toks = lax.axis_size("grp"), lax.axis_size("tok")
    tokens, width = arrays[0].shape
    inverse = 1.0 / (tokens * gs * toks)
    zs = toks // 2
    fits = gs == 4 and toks % 4 == 0 and zs <= 4
    if fits and width % (64 * zs) == 0 and width % 256 == 0 and tokens % 128 == 0:
        return fused_step(*arrays, zs, inverse)
    return general_step(*arrays, inverse)


def solution(mesh):
    token = P(("grp", "tok"), None)
    return jax.shard_map(
        on_device,
        mesh=mesh,
        in_specs=(token, token, token, token, P(), P(), P()),
        out_specs=(token, token, token, P("tok", None), P("tok", None), P("tok", None)),
        check_vma=False,
    )
```

```python
import functools

import jax
import jax.numpy as jnp
from jax import lax
from jax.experimental import pallas as pl
from jax.experimental.pallas import tpu as pltpu
from jax.sharding import PartitionSpec as P

STEP_SIZE = 0.02
EPSILON = 1e-06
MESH = pl.DeviceIdType.MESH
BF = jnp.bfloat16
F32 = jnp.float32
VM = pltpu.VMEM
DMA = pltpu.SemaphoreType.DMA


def dot(left, right):
    return jnp.dot(left, right, preferred_element_type=F32)


def dot_nt(left, right):
    return lax.dot_general(left, right, (((1,), (1,)), ((), ())), preferred_element_type=F32)


def block(index, size):
    return pl.ds(pl.multiple_of(index * size, size), size)


class Net:
    def __init__(self, zs, rows, width):
        g, t = lax.axis_index("grp"), lax.axis_index("tok")
        self.zs, self.rows = zs, rows
        self.g, self.z, self.c = g, t // 2, lax.rem(t, 2)
        self.y, self.x = g // 2, lax.rem(g, 2)
        self.t = t
        cut = 128 * ((width // 128 + 1) // 2)
        self.lanes = (pl.ds(0, cut), pl.ds(cut, width - cut))
        self.twin = (g, 2 * self.z + 1 - self.c)

    def flip(self, *directions):
        y, x = self.y, self.x
        for a in directions:
            if a == 0:
                x = 1 - x
            else:
                y = 1 - y
        return y, x

    def side(self, a):
        y, x = self.flip(a)
        return (2 * y + x, self.t)

    def across(self):
        y, x = self.flip(0, 1)
        return (2 * y + x, self.t)

    def at_z(self, z):
        return (self.g, 2 * z + self.c)

    def pick(self, table):
        value = table[0]
        for z in range(1, self.zs):
            value = jnp.where(self.z == z, table[z], value)
        return value

    def chunk(self, zb, yx):
        return block(4 * zb + 2 * yx[0] + yx[1], self.rows)

    def greet(self):
        barrier = pltpu.get_barrier_semaphore()
        peers = [self.twin, self.side(0), self.side(1), self.across()]
        for peer in peers:
            pl.semaphore_signal(barrier, inc=1, device_id=peer, device_id_type=MESH)
        for z in range(self.zs):
            near = [other for other in (z - 1, z + 1) if 0 <= other < self.zs]

            @pl.when(self.z == z)
            def _():
                for other in near:
                    pl.semaphore_signal(
                        barrier, inc=1, device_id=self.at_z(other), device_id_type=MESH)
                pl.semaphore_wait(barrier, len(peers) + len(near))


def send(src, dst, sems, at, peer, there=None):
    copy = pltpu.make_async_remote_copy(
        src_ref=src, dst_ref=dst, send_sem=sems[0].at[at],
        recv_sem=sems[1].at[at if there is None else there],
        device_id=peer, device_id_type=MESH,
    )
    copy.start()
    return copy


def await_copy(net, ref, sems, at, there=None):
    copy = pltpu.make_async_remote_copy(
        src_ref=ref, dst_ref=ref, send_sem=sems[0].at[at if there is None else there],
        recv_sem=sems[1].at[at], device_id=net.twin, device_id_type=MESH,
    )
    if there is None:
        copy.wait_recv()
    else:
        copy.wait_send()


def sum_order(zs, z):
    def key(zb):
        hops = z if zb > z else zs - 1 - z
        return (zb == z, hops, -abs(zb - z))
    return sorted(range(zs), key=key)


def spread_order(zs, z):
    return sorted(range(zs), key=lambda zb: (abs(zb - z), (zb > z) == (2 * z < zs)))


def reduce_scatter(net, pay, s, total, produce, fillers):
    zs = net.zs
    orders = [sum_order(zs, z) for z in range(zs)]
    blocks = [net.pick([orders[z][i] for z in range(zs)]) for i in range(zs)]
    first, second = {}, {}

    def start_first(i, k):
        for p in range(2):
            a = (p + i) % 2
            yx = net.flip(a, 1 - a) if k == 0 else net.flip(a)
            first[i, p, k] = send(
                pay.at[net.chunk(blocks[i], yx), net.lanes[p]], s["r1"][p].at[i, k],
                s["s1"], (i, p, k), net.side(a))

    def start_second(i):
        for p in range(2):
            a = (p + i) % 2
            first[i, p, 0].wait_recv()
            at = (net.chunk(blocks[i], net.flip(1 - a)), net.lanes[p])
            pay[at] = (pay[at].astype(F32) + s["r1"][p][i, 0].astype(F32)).astype(BF)
            second[i, p] = send(pay.at[at], s["r2"][p].at[i], s["s2"], (i, p), net.side(1 - a))

    def along(z, i):
        zb = orders[z][i]
        for p in range(2):
            first[i, p, 1].wait_recv()
            second[i, p].wait_recv()
            at = (net.chunk(zb, (net.y, net.x)), net.lanes[p])
            value = (pay[at].astype(F32) + s["r1"][p][i, 1].astype(F32)
                     + s["r2"][p][i].astype(F32))
            slots = []
            if zb >= z and z > 0:
                slots.append(i)
            if zb <= z and z < zs - 1:
                slots.append(i if zb < z else zs)
            for slot in slots:
                await_copy(net, s["zr"][p].at[slot], s["s3"], (slot, p))
                value = value + s["zr"][p][slot].astype(F32)
            if zb == z:
                total[:, net.lanes[p]] = value
            else:
                s["zb"][p][i] = value.astype(BF)
                nxt = z + 1 if zb > z else z - 1
                slot = orders[nxt].index(zb) if nxt != zb or zb > z else zs
                send(s["zb"][p].at[i], s["zr"][p].at[slot], s["s3"], (i, p), net.at_z(nxt),
                     (slot, p))

    last = 0
    steps = [{} for _ in range(zs)]
    for z in range(zs):
        for i, zb in enumerate(orders[z]):
            hops = 0 if zb == z else z if zb > z else zs - 1 - z
            when = max(i + 2 + hops, last if zb == z else 0)
            if zb == z:
                when = max([when] + list(steps[z]))
            steps[z].setdefault(when, []).append(i)
            last = max(last, when)
    for i in range(last + 1):
        if i < zs:
            produce(blocks[i], i)
            start_first(i, 0)
        if 1 <= i <= zs:
            start_second(i - 1)
        if i < zs:
            start_first(i, 1)
            if i in fillers:
                fillers[i]()
        for z in range(zs):
            if i in steps[z]:
                @pl.when(net.z == z)
                def _():
                    for k in steps[z][i]:
                        along(z, k)

    def finish():
        drain([*first.values(), *second.values()])
        for i in range(zs - 1):
            for p in range(2):
                await_copy(net, s["zb"][p].at[i], s["s3"], (i, p), (i, p))
    return finish


def plane_own(net, ref, at, i, p, s):
    a = (p + i) % 2
    ref = ref.at[at((net.y, net.x), p)]
    return [send(ref, ref, s["o"], (i, p, k), net.side(d)) for k, d in enumerate((a, 1 - a))]


def plane_relay(net, ref, at, i, p, s):
    a = (p + i) % 2
    ref = ref.at[at(net.flip(a), p)]
    await_copy(net, ref, s["o"], (i, p, 0))
    return send(ref, ref, s["f"], (i, p), net.side(1 - a))


def plane_rest(net, ref, at, i, p, s):
    a = (p + i) % 2
    await_copy(net, ref.at[at(net.flip(1 - a), p)], s["o"], (i, p, 1))
    await_copy(net, ref.at[at(net.flip(0, 1), p)], s["f"], (i, p))


def plane_drain(net, ref, at, i, p, s):
    ref = ref.at[at((net.y, net.x), p)]
    for k in range(2):
        await_copy(net, ref, s["o"], (i, p, k), (i, p, k))
    await_copy(net, ref, s["f"], (i, p), (i, p))


def at_each(net, body):
    for z in range(net.zs):
        @pl.when(net.z == z)
        def _():
            body(z)


def onward(zs, z, zb):
    return [(k, other) for k, other in enumerate((z - 1, z + 1))
            if 0 <= other < zs and (zb == z or (zb > z) == (other < z))]


def pass_on(net, z, zb, p, ref, s):
    for k, other in onward(net.zs, z, zb):
        send(ref, ref, s["z"], (zb, p, k), net.at_z(other), (zb, p, 0))


def pass_drain(net, z, zb, p, ref, s):
    for k, other in onward(net.zs, z, zb):
        await_copy(net, ref, s["z"], (zb, p, 0), (zb, p, k))


def all_gather(net, full, s, parts):
    zs = net.zs
    place = lambda zb: lambda yx, p: (net.chunk(zb, yx), net.lanes[p])
    mine = lambda zb, p: full.at[place(zb)((net.y, net.x), p)]

    for p in range(2):
        parts[p]()
        at_each(net, lambda z: pass_on(net, z, z, p, mine(z, p), s))
        plane_own(net, full, place(net.z), 0, p, s)

    def rest(z):
        order = spread_order(zs, z)
        for i in range(1, zs):
            for p in range(2):
                await_copy(net, mine(order[i], p), s["z"], (order[i], p, 0))
                pass_on(net, z, order[i], p, mine(order[i], p), s)
                plane_own(net, full, place(order[i]), i, p, s)
            for p in range(2):
                plane_relay(net, full, place(order[i - 1]), i - 1, p, s)
        for p in range(2):
            plane_relay(net, full, place(order[zs - 1]), zs - 1, p, s)
        for i in range(zs):
            for p in range(2):
                plane_rest(net, full, place(order[i]), i, p, s)
    at_each(net, rest)

    def finish():
        def go(z):
            order = spread_order(zs, z)
            for i in range(zs):
                for p in range(2):
                    pass_drain(net, z, order[i], p, mine(order[i], p), s)
                    plane_drain(net, full, place(order[i]), i, p, s)
        at_each(net, go)
    return finish


class PlaneSum:
    def __init__(self, net, ref, at, s):
        self.net, self.ref, self.at, self.s = net, ref, at, s
        self.copies = []

    def first(self):
        net, s = self.net, self.s
        for k in range(2):
            for p in range(2):
                yx = net.flip(p, 1 - p) if k == 0 else net.flip(p)
                self.copies.append(send(self.ref.at[self.at(yx, p)], s["r1"].at[p, k], s["s1"],
                                        (p, k), net.side(p)))

    def second(self):
        net, s = self.net, self.s
        for p in range(2):
            await_copy(net, s["r1"].at[p, 0], s["s1"], (p, 0))
            at = self.at(net.flip(1 - p), p)
            self.ref[at] = (self.ref[at].astype(F32) + s["r1"][p, 0].astype(F32)).astype(BF)
            self.copies.append(send(self.ref.at[at], s["r2"].at[p], s["s2"], (p,), net.side(1 - p)))

    def last(self, done):
        net, s = self.net, self.s
        for p in range(2):
            await_copy(net, s["r1"].at[p, 1], s["s1"], (p, 1))
            await_copy(net, s["r2"].at[p], s["s2"], (p,))
            value = self.ref[self.at((net.y, net.x), p)].astype(F32)
            done(p, value + s["r1"][p, 1].astype(F32) + s["r2"][p].astype(F32))


class LineSum:
    def __init__(self, net, pieces, sems):
        self.net, self.pieces, self.sems = net, pieces, sems
        self.orders = [sum_order(net.zs, z) for z in range(net.zs)]

    def hops(self, z, i):
        zb = self.orders[z][i]
        return self.net.zs if zb == z else z if zb > z else self.net.zs - 1 - z

    def move(self, z, i, p):
        net, zs = self.net, self.net.zs
        cut, out, inn, own = self.pieces[p]
        zb = self.orders[z][i]
        value = cut(zb)
        slots = []
        if zb >= z and z > 0:
            slots.append(i)
        if zb <= z and z < zs - 1:
            slots.append(i if zb < z else zs)
        for slot in slots:
            await_copy(net, inn.at[slot], self.sems, (slot, p))
            value = value + inn[slot].astype(F32)
        if zb == z:
            own(value)
            return
        out[i] = value.astype(BF)
        nxt = z + 1 if zb > z else z - 1
        slot = self.orders[nxt].index(zb) if nxt != zb or zb > z else zs
        send(out.at[i], inn.at[slot], self.sems, (i, p), net.at_z(nxt), (slot, p))

    def run(self, chosen):
        def go(z):
            for i in range(self.net.zs):
                for p in range(len(self.pieces)):
                    if chosen(i, p, self.hops(z, i)):
                        self.move(z, i, p)
        at_each(self.net, go)

    def finish(self):
        for i in range(self.net.zs - 1):
            for p, piece in enumerate(self.pieces):
                await_copy(self.net, piece[1].at[i], self.sems, (i, p), (i, p))


def drain(copies):
    for copy in copies:
        copy.wait_send()


def by_rows(count, step, body):
    def run(i, carry):
        body(pl.ds(pl.multiple_of(i * step, step), step))
        return carry
    lax.fori_loop(0, count // step, run, 0)


def step_body(zs, names, inverse, *refs):
    r = dict(zip(names, refs))
    (queries, keys, values, out_grad, w_gate, w_up, w_down) = refs[:7]
    (d_queries, d_keys, d_values, d_gate, d_up, d_down) = refs[7:13]
    toks, width = queries.shape
    half = width // 2
    every = 2 * toks
    rows = width // (4 * zs)
    zrows = 4 * rows
    net = Net(zs, rows, width + half)
    c = net.c
    mine, theirs = block(c, toks), block(1 - c, toks)
    gl, ul, dl = pl.ds(0, half), pl.ds(half, half), pl.ds(width, half)
    wide = pl.ds(0, width)
    hid = block(c, half)

    token_at = lambda yx, p: (block(2 * (2 * yx[0] + yx[1]) + c, toks), block(p, half))
    spot = block(2 * net.g + c, toks)
    loads = {}
    for i, (name, src, dst) in enumerate((
        ("k", keys, r["kf"]),
        ("a", w_gate.at[:, hid], r["wab"].at[:, gl]),
        ("b", w_up.at[:, hid], r["wab"].at[:, ul]),
        ("c", w_down.at[hid, :], r["wc"]),
        ("v", values, r["vf"]),
        ("q", queries, r["qa"].at[spot, :]),
        ("o", out_grad, r["oa"].at[spot, :]),
    )):
        loads[name] = pltpu.make_async_copy(src, dst, r["ld"].at[i])
        loads[name].start()
    net.greet()
    tsem = (r["ts"], r["tr"])
    done = []

    def twin(src, dst, k):
        copy = send(src, dst, tsem, k, net.twin)
        done.append(copy)
        return copy

    def scratch_of(kind, k):
        if kind == "rs":
            return {
                "r1": (r["r1a%d" % k], r["r1b%d" % k]), "r2": (r["r2a%d" % k], r["r2b%d" % k]),
                "zb": (r["zba%d" % k], r["zbb%d" % k]), "zr": (r["zra%d" % k], r["zrb%d" % k]),
                "s1": (r["s1s%d" % k], r["s1r%d" % k]), "s2": (r["s2s%d" % k], r["s2r%d" % k]),
                "s3": (r["s3s%d" % k], r["s3r%d" % k]),
            }
        return {
            "z": (r["azs%d" % k], r["azr%d" % k]), "o": (r["aos%d" % k], r["aor%d" % k]),
            "f": (r["afs%d" % k], r["afr%d" % k]),
        }

    xb, gu, ab, eb = r["xb"], r["gu"], r["ab"], r["eb"]
    loads["k"].wait()
    xb[mine, :] = r["kf"][...].astype(BF)
    keys_in = twin(xb.at[mine, :], xb.at[mine, :], 0)
    qa, oa = r["qa"], r["oa"]
    sq_q = {"o": (r["qos"], r["qor"]), "f": (r["qfs"], r["qfr"])}
    sq_o = {"o": (r["oos"], r["oor"]), "f": (r["ofs"], r["ofr"])}
    loads["q"].wait()
    for p in range(2):
        plane_own(net, qa, token_at, 0, p, sq_q)
    loads["a"].wait()
    loads["b"].wait()
    r["abb"][...] = r["wab"][...].astype(BF)
    loads["c"].wait()
    r["cb"][...] = r["wc"][...].astype(BF)
    keys_in.wait_recv()
    gu[...] = dot(xb[...], r["abb"][...])

    def active_rows(at):
        g, u = gu[at, gl], gu[at, ul]
        ab[at, :] = (g * jax.nn.sigmoid(g) * u).astype(BF)
    by_rows(every, 32, active_rows)

    for p in range(2):
        plane_relay(net, qa, token_at, 0, p, sq_q)
    loads["v"].wait()
    ep, er = r["ep"], r["er"]
    ep[mine, :] = dot(ab[mine, :], r["cb"][...]) - r["vf"][...]
    e_out = [twin(ep.at[mine, :], er.at[mine, :], 3)]
    ep[theirs, :] = dot(ab[theirs, :], r["cb"][...])
    e_out.append(twin(ep.at[theirs, :], er.at[theirs, :], 4))
    for copy, at in zip(e_out, (theirs, mine)):
        copy.wait_recv()
        eb[at, :] = (ep[at, :] + er[at, :]).astype(BF)
    da, dgu = r["da"], r["dgu"]
    da[...] = dot_nt(eb[...], r["cb"][...])

    def d_rows(at):
        g, u, d = gu[at, gl], gu[at, ul], da[at, :]
        sig = jax.nn.sigmoid(g)
        dgu[at, ul] = (d * g * sig).astype(BF)
        dgu[at, gl] = (d * u * sig * (1.0 + g * (1.0 - sig))).astype(BF)
    by_rows(every, 32, d_rows)
    r["dguT"][...] = dgu[...].T
    r["eT"][...] = eb[...].T

    pay = r["pay0"]

    def key_block(zb, i):
        at = block(zb, zrows)
        pay[at, wide] = dot(r["dguT"][at, :], xb[...]).astype(BF)
        pay[at, dl] = dot(r["eT"][at, :], ab[...]).astype(BF)

    def turn_weights():
        r["wabt"][...] = r["wab"][...].T
        r["wct"][...] = r["wc"][...].T

    def to_twin(ref, k):
        return [twin(ref.at[block(2 * g + c, toks), :], ref.at[block(2 * g + c, toks), :], k + g)
                for g in range(4)]

    def share_queries():
        for p in range(2):
            plane_rest(net, qa, token_at, 0, p, sq_q)
        r["q_in"] = to_twin(qa, 20)

    def select_lanes():
        h = lax.broadcasted_iota(jnp.int32, (half, 512), 0)
        lane = lax.broadcasted_iota(jnp.int32, (half, 512), 1)
        g, l = lane // 128, lane % 128
        hit = (h == (half // 2) * (l // rows) + rows * g + l % rows) & (l < 2 * rows)
        r["sel"][...] = jnp.where(hit, 1.0, 0.0).astype(BF)
        r["wgu"][...] = jnp.zeros((256, width), BF)

    def turn_keys():
        r["xT"][...] = xb[...].T

    grad = r["grad"]
    rs0 = reduce_scatter(net, pay, scratch_of("rs", 0), grad, key_block,
                         {0: turn_keys, 1: share_queries, 2: select_lanes, 3: turn_weights})

    own = net.chunk(net.z, (net.y, net.x))
    squares = jnp.sum(grad[:, dl] * grad[:, dl], axis=1, keepdims=True)
    r["sq"][0] = jnp.broadcast_to(squares, (rows, 128))
    norm_in = twin(r["sq"].at[0], r["sq"].at[1], 5)
    scale_of = lambda sq: jnp.sqrt(sq / width + EPSILON)
    scale = r["scale"]
    loads["o"].wait()
    for p in range(2):
        plane_own(net, oa, token_at, 0, p, sq_o)

    gz, rz = r["gz"], r["rz"]
    line = {"z": (r["lzs"], r["lzr"])}
    gz_at = lambda zb: gz.at[pl.ds(rows * zb, rows), :]
    rz_at = lambda zb: rz.at[pl.ds(zrows * zb, zrows), :]
    g = grad[:, wide]
    sc = scale_of(jnp.sum(g * g, axis=1, keepdims=True))
    scale[0] = jnp.broadcast_to(sc, (rows, 128))
    gz[block(net.z, rows), :] = (r["wabt"][own, :] - STEP_SIZE * g / sc).astype(BF)
    at_each(net, lambda z: pass_on(net, z, z, 0, gz_at(z), line))
    norm_in.wait_recv()
    sc = scale_of((r["sq"][0] + r["sq"][1])[:, :1])
    scale[1] = jnp.broadcast_to(sc, (rows, 128))
    down = (r["wct"][own, :] - STEP_SIZE * grad[:, dl] / sc).astype(BF)
    r["dsl"][...] = dot(down, r["sel"][...]).astype(BF)
    ssem = (r["sls"], r["slr"])
    near = [net.flip(0), net.flip(1), net.flip(0, 1)]
    near_at = [net.side(0), net.side(1), net.across()]
    lane_of = lambda yx: block(2 * yx[0] + yx[1], 128)
    rz[own, :] = r["dsl"][:, lane_of((net.y, net.x))]
    slices = [send(r["dsl"].at[:, lane_of(yx)], rz.at[own, :], ssem, k, peer)
              for k, (yx, peer) in enumerate(zip(near, near_at))]
    for p in range(2):
        plane_relay(net, oa, token_at, 0, p, sq_o)
    for copy in slices:
        copy.wait_recv()
    at_each(net, lambda z: pass_on(net, z, z, 1, rz_at(z), line))

    def gather_line(first, last):
        def go(z):
            for zb in spread_order(zs, z)[first:last]:
                for p, at in enumerate((gz_at, rz_at)):
                    await_copy(net, at(zb), line["z"], (zb, p, 0))
                    pass_on(net, z, zb, p, at(zb), line)
        at_each(net, go)

    gather_line(1, 2)
    for p in range(2):
        plane_rest(net, oa, token_at, 0, p, sq_o)
    o_in = to_twin(oa, 24)
    for copy in r["q_in"]:
        copy.wait_recv()
    gather_line(2, zs)

    wgu, hgu, dact, hd, hact = r["wgu"], r["hgu"], r["dact"], r["hd"], r["hact"]
    wgu[:2 * rows, :] = gz[:2 * rows, :]
    wgu[128:128 + 2 * rows, :] = gz[2 * rows:, :]
    low, high = pl.ds(0, 128), pl.ds(128, 128)
    plane = 4 * every
    hgu[...] = dot_nt(qa[...], wgu[...])
    for copy in o_in:
        copy.wait_recv()
    dact[...] = dot(oa[...], rz[...])

    def query_rows(at):
        g, u, d = hgu[at, low], hgu[at, high], dact[at, :]
        sig = jax.nn.sigmoid(g)
        hact[at, :] = (g * sig * u).astype(BF)
        hd[at, high] = (d * g * sig).astype(BF)
        hd[at, low] = (d * u * sig * (1.0 + g * (1.0 - sig))).astype(BF)
    by_rows(plane, 64, query_rows)
    hsum = r["hsum"]
    hdn8, hgu8 = r["hdn8"], r["hgu8"]
    r["haT"][...] = hact[...].T
    hdn8[...] = dot(r["haT"][...], oa[...])
    r["pd"][...] = hdn8[...].T
    r["hdT"][...] = hd[...].T

    def own_down(value):
        r["dout"][...] = value.astype(BF)

    def own_wide(value):
        hsum[:, wide] = value

    pieces = (
        (lambda zb: r["pd"][zrows * zb:zrows * (zb + 1), :], r["ldo"], r["ldi"], own_down),
        (lambda zb: hgu8[pl.ds(rows * zb + (128 - 2 * rows) * (zb // 2), rows), :],
         r["lgo"], r["lgi"], own_wide),
    )
    summing = LineSum(net, pieces, (r["lss"], r["lsr"]))
    summing.run(lambda i, p, hops: hops == 0 and p == 0)
    hgu8[...] = dot(r["hdT"][...], qa[...])
    summing.run(lambda i, p, hops: hops == 0 and p == 1)
    dqs, dqm, dqt = r["dqs"], r["dqm"], r["dqt"]
    dq_in = []
    for g in range(4):
        at = block(g, toks)
        dqs[at, :] = dot(hd[block(2 * g + 1 - c, toks), :], wgu[...]).astype(BF)
        dq_in.append(twin(dqs.at[at, :], dqt.at[at, :], 28 + g))
    summing.run(lambda i, p, hops: hops == 1)
    for g in range(4):
        at = block(g, toks)
        mid = dot(hd[block(2 * g + c, toks), :], wgu[...])
        dq_in[g].wait_recv()
        dqm[at, :] = (mid + dqt[at, :].astype(F32)).astype(BF)
    query_sum = PlaneSum(net, dqm, lambda yx, p: (block(2 * yx[0] + yx[1], toks), block(p, half)), {
        "r1": r["dq1"], "r2": r["dq2"], "s1": (r["d1s"], r["d1r"]), "s2": (r["d2s"], r["d2r"])})
    query_sum.first()
    summing.run(lambda i, p, hops: 1 < hops < zs)
    query_sum.second()
    summing.run(lambda i, p, hops: hops == zs and p == 0)
    dout, din = r["dout"], r["din"]
    mine_at = lambda yx: block(2 * yx[0] + yx[1], rows)
    usem = (r["uls"], r["ulr"])
    units = [send(dout.at[mine_at(yx), :], din.at[:, lane_of((net.y, net.x))], usem, k, peer)
             for k, (yx, peer) in enumerate(zip(near, near_at))]
    din[:, lane_of((net.y, net.x))] = dout[mine_at((net.y, net.x)), :]
    summing.run(lambda i, p, hops: hops == zs and p == 1)
    for copy in units:
        copy.wait_recv()
    hsum[:, dl] = dot_nt(din[...], r["sel"][...])

    def query_done(p, value):
        d_queries[:, p * half:(p + 1) * half] = value.astype(BF)
    query_sum.last(query_done)

    product = jnp.sum(-STEP_SIZE * hsum[:, dl] * grad[:, dl], axis=1, keepdims=True)
    r["sq"][2] = jnp.broadcast_to(product, (rows, 128))
    product_in = twin(r["sq"].at[2], r["sq"].at[3], 7)
    back = r["full1"]

    def turned(h, g, sc, prod):
        return (-STEP_SIZE * h / sc - g * prod / (width * sc * sc * sc)).astype(BF)

    def wide_back():
        h, g = hsum[:, wide], grad[:, wide]
        prod = jnp.sum(-STEP_SIZE * h * g, axis=1, keepdims=True)
        back[own, wide] = turned(h, g, scale[0][:, :1], prod)

    def down_back():
        product_in.wait_recv()
        prod = (r["sq"][2] + r["sq"][3])[:, :1]
        back[own, dl] = turned(hsum[:, dl], grad[:, dl], scale[1][:, :1], prod)

    ag1 = all_gather(net, back, scratch_of("ag", 1), (wide_back, down_back))

    pq, tb, ec = r["pq"], r["tb"], r["ec"]
    pq[...] = dot_nt(xb[...], back[:, wide])
    ec[...] = dot(eb[...], back[:, dl])

    def t_rows(at):
        g, u = gu[at, gl], gu[at, ul]
        p, q = pq[at, gl], pq[at, ul]
        sig = jax.nn.sigmoid(g)
        tb[at, :] = (q * g * sig + p * u * sig * (1.0 + g * (1.0 - sig))).astype(BF)
    by_rows(every, 32, t_rows)
    sp, sr, sb = r["sp"], r["sr"], r["sb"]
    second_out = []
    for k, at in enumerate((mine, theirs)):
        sp[at, :] = dot_nt(ab[at, :], back[:, dl]) + dot(tb[at, :], r["cb"][...])
        second_out.append(twin(sp.at[at, :], sr.at[at, :], 8 + k))
    placed, hp, hdn = r["placed"], r["hp"], r["hdn"]
    placed[...] = jnp.zeros_like(placed)
    hdn[...] = jnp.zeros_like(hdn)
    for k in range(2):
        to = pl.ds(pl.multiple_of((half // 2) * k + rows * net.g, rows), rows)
        to_up = pl.ds(pl.multiple_of(half + (half // 2) * k + rows * net.g, rows), rows)
        placed[to, :] = hgu8[k * rows:(k + 1) * rows, :]
        placed[to_up, :] = hgu8[128 + k * rows:128 + (k + 1) * rows, :]
        hdn[to, :] = hdn8[k * rows:(k + 1) * rows, :]
    hp[...] = placed[...].T
    r["taT"][:, pl.ds(0, every)] = tb[...].T
    r["taT"][:, pl.ds(every, every)] = ab[...].T
    for copy, at in zip(second_out, (theirs, mine)):
        copy.wait_recv()
        sb[at, :] = (sp[at, :] + sr[at, :]).astype(BF)
    d_values[...] = -(sp[mine, :] + sr[mine, :])
    ec[...] += dot_nt(sb[...], r["cb"][...])
    gub = r["gub"]

    def pull_rows(at):
        g, u, d = gu[at, gl], gu[at, ul], da[at, :]
        p, q, back_a = pq[at, gl], pq[at, ul], ec[at, :]
        sig = jax.nn.sigmoid(g)
        sneg = 1.0 - sig
        h = g * sig
        slope = sig * (1.0 + g * sneg)
        bend = sig * sneg * (2.0 + g * (1.0 - 2.0 * sig))
        pd = p * d
        gub[at, gl] = (back_a * u * slope + pd * u * bend + q * d * slope).astype(BF)
        gub[at, ul] = (back_a * h + pd * slope).astype(BF)
    by_rows(every, 32, pull_rows)

    dsw, dloc = r["dsw"], r["dloc"]
    dloc[...] = (r["hdn"][...] + dot(r["taT"][:, pl.ds(0, every)], eb[...])
                 + dot(r["taT"][:, pl.ds(every, every)], sb[...])).astype(BF)
    swaps = []
    prow = 2 * rows
    for k in range(zs // 2):
        slot = (zs // 2) * c + k
        swaps.append(twin(dloc.at[block(2 * k + 1 - c, prow), :], dsw.at[slot], 10 + k))
        dsw[slot] = dloc[block(2 * k + c, prow), :]
    pay2 = r["pay2"]

    def last_block(zb, i):
        at = block(zb, zrows)
        pay2[at, wide] = (r["hp"][at, :] + dot(r["xT"][at, :], gub[...])).astype(BF)
        if i == 0:
            for copy in swaps:
                copy.wait_recv()
        for y in range(2):
            for x in range(2):
                pay2[block(4 * zb + 2 * y + x, rows), dl] = (
                    dsw[zb, y * rows:(y + 1) * rows, x * half:(x + 1) * half])

    def key_back():
        r["kp"][...] = dot(dgu[...], back[:, wide])

    def key_back_second():
        r["kp"][...] += dot_nt(gub[...], r["abb"][...])
        r["kin"] = twin(r["kp"].at[theirs, :], r["kr"], 10 + zs // 2)

    last = r["last"]
    rs2 = reduce_scatter(net, pay2, scratch_of("rs", 2), last, last_block,
                         {0: key_back, 1: key_back_second})
    fin = r["fin"]
    fin[block(net.g, rows), :] = last[...].astype(BF)
    s = scratch_of("ag", 2)
    fin_at = lambda yx, p: (block(2 * yx[0] + yx[1], rows), net.lanes[p])
    for p in range(2):
        plane_own(net, fin, fin_at, 0, p, s)
    for p in range(2):
        plane_relay(net, fin, fin_at, 0, p, s)
    r["kin"].wait_recv()
    d_keys[...] = r["kp"][mine, :] + r["kr"][...]
    for p in range(2):
        plane_rest(net, fin, fin_at, 0, p, s)
    swap = twin(fin.at[block(1 - c, prow), wide], r["tw"], 11 + zs // 2)
    lanes = block(c, half)
    others = block(1 - c, half)
    d_gate[:, lanes] = fin[block(c, prow), gl].astype(F32) * inverse
    d_up[:, lanes] = fin[block(c, prow), ul].astype(F32) * inverse
    for y in range(2):
        for x in range(2):
            g = 2 * y + x
            d_down[y * rows:(y + 1) * rows, x * half:(x + 1) * half] = (
                fin[g * rows:(g + 1) * rows, width:].astype(F32) * inverse)
    swap.wait_recv()
    d_gate[:, others] = r["tw"][:, :half].astype(F32) * inverse
    d_up[:, others] = r["tw"][:, half:].astype(F32) * inverse
    drain(done + slices + units + query_sum.copies)
    for finish in (rs0, ag1, rs2, summing.finish):
        finish()
    for p in range(2):
        plane_drain(net, qa, token_at, 0, p, sq_q)
        plane_drain(net, oa, token_at, 0, p, sq_o)
        plane_drain(net, fin, fin_at, 0, p, s)

    def drain_line(z):
        for zb in range(zs):
            for p, at in enumerate((gz_at, rz_at)):
                pass_drain(net, z, zb, p, at(zb), line)
    at_each(net, drain_line)


def hand_over(*refs):
    for src, dst in zip(refs[:6], refs[6:]):
        dst[...] = src[...]


def fused_step(queries, key_tokens, values, out_grad, w_gate, w_up, w_down, zs, inverse):
    toks, width = queries.shape
    half, every, rows = width // 2, 2 * toks, width // (4 * zs)
    plane = 4 * every
    total = width + half
    cut = 128 * ((total // 128 + 1) // 2)
    parts = (("a", cut), ("b", total - cut))
    names, shapes = [], []

    def add(name, spec):
        names.append(name)
        shapes.append(spec)

    for name, shape in (
        ("kf", (toks, width)), ("vf", (toks, width)), ("wab", (width, width)),
        ("wc", (half, width)), ("wabt", (width, width)), ("wct", (width, half)),
        ("gu", (every, width)), ("ep", (every, width)), ("er", (every, width)),
        ("da", (every, half)), ("grad", (rows, total)), ("hsum", (rows, total)),
        ("last", (rows, total)), ("sq", (4, rows, 128)), ("scale", (2, rows, 128)),
        ("hgu", (plane, 256)), ("dact", (plane, 128)), ("hdn8", (128, width)),
        ("hgu8", (256, width)), ("pd", (width, 128)), ("placed", (width, width)),
        ("hp", (width, width)), ("hdn", (half, width)),
        ("pq", (every, width)), ("ec", (every, half)), ("sp", (every, width)),
        ("sr", (every, width)), ("kp", (every, width)), ("kr", (toks, width)),
    ):
        add(name, VM(shape, F32))
    for name, shape in (
        ("xb", (every, width)), ("qa", (plane, width)), ("oa", (plane, width)),
        ("abb", (width, width)), ("cb", (half, width)), ("ab", (every, half)),
        ("eb", (every, width)), ("dgu", (every, width)), ("dguT", (width, every)),
        ("eT", (width, every)), ("xT", (width, every)), ("hd", (plane, 256)),
        ("hdT", (256, plane)), ("hact", (plane, 128)), ("haT", (128, plane)),
        ("tb", (every, half)), ("sel", (half, 512)), ("wgu", (256, width)),
        ("gz", (zs * rows, width)), ("rz", (width, 128)), ("dsl", (rows, 512)),
        ("dout", (4 * rows, 128)), ("din", (rows, 512)), ("dqs", (4 * toks, width)),
        ("dqm", (4 * toks, width)), ("dqt", (4 * toks, width)),
        ("dq1", (2, 2, toks, half)), ("dq2", (2, toks, half)),
        ("ldo", (zs - 1, 4 * rows, 128)), ("ldi", (zs + 1, 4 * rows, 128)),
        ("lgo", (zs - 1, rows, width)), ("lgi", (zs + 1, rows, width)),
        ("sb", (every, width)), ("taT", (half, 2 * every)), ("gub", (every, width)),
        ("dloc", (half, width)), ("dsw", (zs, 2 * rows, width)),
        ("pay0", (width, total)), ("pay2", (width, total)), ("full1", (width, total)),
        ("fin", (4 * rows, total)), ("tw", (2 * rows, width)),
    ):
        add(name, VM(shape, BF))
    for k in (0, 2):
        for letter, size in parts:
            add("r1%s%d" % (letter, k), VM((zs, 2, rows, size), BF))
            add("r2%s%d" % (letter, k), VM((zs, rows, size), BF))
            add("zb%s%d" % (letter, k), VM((zs - 1, rows, size), BF))
            add("zr%s%d" % (letter, k), VM((zs + 1, rows, size), BF))
        for end in "sr":
            add("s1%s%d" % (end, k), DMA((zs, 2, 2)))
            add("s2%s%d" % (end, k), DMA((zs, 2)))
            add("s3%s%d" % (end, k), DMA((zs + 1, 2)))
    for end in "sr":
        add("az%s1" % end, DMA((zs, 2, 2)))
        add("az%s2" % end, DMA((1, 2, 2)))
        for k, depth in ((1, zs), (2, 1)):
            add("ao%s%d" % (end, k), DMA((depth, 2, 2)))
            add("af%s%d" % (end, k), DMA((depth, 2)))
        for name in "qo":
            add("%so%s" % (name, end), DMA((1, 2, 2)))
            add("%sf%s" % (name, end), DMA((1, 2)))
        add("lz%s" % end, DMA((zs, 2, 2)))
        add("ls%s" % end, DMA((zs + 1, 2)))
        add("sl%s" % end, DMA((3,)))
        add("ul%s" % end, DMA((3,)))
        add("d1%s" % end, DMA((2, 2)))
        add("d2%s" % end, DMA((2,)))
    add("ld", DMA((7,)))
    add("ts", DMA((32,)))
    add("tr", DMA((32,)))
    all_names = ["in%d" % i for i in range(7)] + ["out%d" % i for i in range(6)] + names
    token = jax.ShapeDtypeStruct((toks, width), F32)
    weight = jax.ShapeDtypeStruct((2 * rows, width), F32)
    results = pl.pallas_call(
        functools.partial(step_body, zs, all_names, inverse),
        out_shape=(jax.ShapeDtypeStruct((toks, width), BF), token, token, weight, weight, weight),
        in_specs=[pl.BlockSpec(memory_space=pltpu.HBM)] * 7,
        out_specs=[pl.BlockSpec(memory_space=VM)] * 6,
        scratch_shapes=shapes,
        compiler_params=pltpu.CompilerParams(
            collective_id=0, has_side_effects=True, vmem_limit_bytes=50 * 1024 * 1024),
    )(*(pltpu.with_memory_space_constraint(x, pltpu.HBM) for x in (
        queries, key_tokens, values, out_grad, w_gate, w_up, w_down)))
    return pl.pallas_call(
        hand_over,
        out_shape=tuple(jax.ShapeDtypeStruct(item.shape, item.dtype) for item in results),
        in_specs=[pl.BlockSpec(memory_space=VM)] * 6,
        out_specs=[pl.BlockSpec(memory_space=VM)] * 6,
        compiler_params=pltpu.CompilerParams(vmem_limit_bytes=8 * 1024 * 1024),
    )(*results)


def matmul(left, right):
    return dot(left.astype(BF), right.astype(BF))


def key_grad(w_gate, w_up, w_down, key_rows, value_rows):
    hidden_gate = matmul(key_rows, w_gate)
    hidden_up = matmul(key_rows, w_up)
    sig = jax.nn.sigmoid(hidden_gate)
    active = hidden_gate * sig * hidden_up
    error = matmul(active, w_down) - value_rows
    d_active = matmul(error, w_down.T)
    d_hup = d_active * hidden_gate * sig
    d_hgate = d_active * hidden_up * sig * (1.0 + hidden_gate * (1.0 - sig))
    return (matmul(d_hgate.T, key_rows), matmul(d_hup.T, key_rows), matmul(error.T, active))


def query_grad(fast_t, query_rows, grad_rows):
    gate_t, up_t, down_t = fast_t
    hidden_gate = dot(query_rows, gate_t.T)
    hidden_up = dot(query_rows, up_t.T)
    sig = jax.nn.sigmoid(hidden_gate)
    active = (hidden_gate * sig * hidden_up).astype(BF)
    d_active = dot(grad_rows, down_t)
    d_hup = (d_active * hidden_gate * sig).astype(BF)
    d_hgate = (d_active * hidden_up * sig * (1.0 + hidden_gate * (1.0 - sig))).astype(BF)
    d_rows = (dot(d_hgate, gate_t) + dot(d_hup, up_t)).astype(BF)
    return (d_rows, active, d_hgate, d_hup)


def general_step(queries, key_tokens, values, out_grad, w_gate, w_up, w_down, inverse):
    gs, toks = lax.axis_size("grp"), lax.axis_size("tok")
    full_width = w_gate.shape[0]
    rows = 3 * full_width // (gs * toks)
    me = lax.axis_index("tok") * gs + lax.axis_index("grp")

    def reduce_units(x):
        y = x.reshape(toks, gs * rows, full_width)
        y = lax.psum_scatter(y, "tok", scatter_dimension=0, tiled=True)[0]
        return lax.psum_scatter(y.reshape(gs, rows, full_width), "grp", scatter_dimension=0, tiled=True)[0]

    def gather_units(y):
        full = lax.all_gather(lax.all_gather(y, "grp"), "tok").reshape(3, full_width, full_width)
        return full[0], full[1], full[2]

    local_grad, pullback = jax.vjp(key_grad, w_gate, w_up, w_down, key_tokens, values)
    grad = reduce_units(jnp.stack(local_grad))
    scale = jnp.sqrt(jnp.sum(grad * grad, axis=1, keepdims=True) / full_width + EPSILON)
    weights = jnp.concatenate((w_gate, w_up, w_down), axis=1)
    mine = lax.dynamic_slice_in_dim(weights, me * rows, rows, 1).T
    fast_t = gather_units((mine - STEP_SIZE * grad / scale).astype(BF))
    d_queries, active, d_hgate, d_hup = query_grad(fast_t, queries, out_grad)
    query_part = reduce_units(
        jnp.stack((dot(d_hgate.T, queries), dot(d_hup.T, queries), dot(out_grad.T, active))))
    product = jnp.sum(-STEP_SIZE * query_part * grad, axis=1, keepdims=True)
    cot = (
        -STEP_SIZE * query_part / scale - grad * product / (full_width * scale * scale * scale)
    ).astype(BF)
    second = pullback(tuple(item.astype(F32) for item in gather_units(cot)))
    plain = (dot(queries.T, d_hgate), dot(queries.T, d_hup), dot(active.T, out_grad))
    combined = jnp.stack(tuple(left + right for left, right in zip(plain, second[:3])))
    combined = combined.reshape(3, toks, full_width // toks, full_width).transpose(1, 0, 2, 3)
    summed = lax.all_gather(reduce_units(combined).astype(BF), "grp").astype(F32) * inverse
    summed = summed.reshape(3, full_width // toks, full_width)
    return (d_queries, second[3], second[4], summed[0], summed[1], summed[2])


def on_device(*arrays):
    gs, toks = lax.axis_size("grp"), lax.axis_size("tok")
    tokens, width = arrays[0].shape
    inverse = 1.0 / (tokens * gs * toks)
    zs = toks // 2
    fits = gs == 4 and toks % 4 == 0 and zs <= 4
    if fits and width % (64 * zs) == 0 and 2 * width <= 512 * zs and width % 256 == 0 and tokens % 128 == 0:
        return fused_step(*arrays, zs, inverse)
    return general_step(*arrays, inverse)


def solution(mesh):
    token = P(("grp", "tok"), None)
    return jax.shard_map(
        on_device,
        mesh=mesh,
        in_specs=(token, token, token, token, P(), P(), P()),
        out_specs=(token, token, token, P("tok", None), P("tok", None), P("tok", None)),
        check_vma=False,
    )
```

```python
import functools
from types import SimpleNamespace as Names

import jax
import jax.numpy as jnp
from jax import lax
from jax.experimental import pallas as pl
from jax.experimental.pallas import tpu as pltpu
from jax.sharding import PartitionSpec as P

STEP_SIZE = 0.02
EPSILON = 1e-06
MESH = pl.DeviceIdType.MESH
BF = jnp.bfloat16
F32 = jnp.float32
VM = pltpu.VMEM
DMA = pltpu.SemaphoreType.DMA


def dot(left, right):
    return jnp.dot(left, right, preferred_element_type=F32)


def dot_nt(left, right):
    return lax.dot_general(left, right, (((1,), (1,)), ((), ())), preferred_element_type=F32)


def block(index, size):
    return pl.ds(pl.multiple_of(index * size, size), size)


def lane_parts(width):
    unit = 128 * max(1, width // 1152)
    cut = width - 128 * ((width // 128 - 2 * (unit // 128)) // 2)
    return ((pl.ds(0, unit), pl.ds(unit, unit)),
            (pl.ds(2 * unit, cut - 2 * unit), pl.ds(cut, width - cut)))


class Net:
    def __init__(self, zs, rows, width):
        g, t = lax.axis_index("grp"), lax.axis_index("tok")
        self.zs, self.rows = zs, rows
        self.g, self.z, self.c = g, t // 2, lax.rem(t, 2)
        self.y, self.x = g // 2, lax.rem(g, 2)
        self.t = t
        self.outer, self.lanes = lane_parts(width)
        cut = 128 * ((width // 128 + 1) // 2)
        self.parts = (pl.ds(0, cut), pl.ds(cut, width - cut))
        self.twin = (g, 2 * self.z + 1 - self.c)

    def flip(self, *directions):
        y, x = self.y, self.x
        for a in directions:
            if a == 0:
                x = 1 - x
            else:
                y = 1 - y
        return y, x

    def side(self, a):
        y, x = self.flip(a)
        return (2 * y + x, self.t)

    def across(self):
        y, x = self.flip(0, 1)
        return (2 * y + x, self.t)

    def at_z(self, z):
        return (self.g, 2 * z + self.c)

    def pick(self, table):
        value = table[0]
        for z in range(1, self.zs):
            value = jnp.where(self.z == z, table[z], value)
        return value

    def chunk(self, zb, yx):
        return block(4 * zb + 2 * yx[0] + yx[1], self.rows)

    def greet(self):
        barrier = pltpu.get_barrier_semaphore()
        peers = [self.twin, self.side(0), self.side(1), self.across()]
        for d in range(1, self.zs):
            peers.append(self.at_z(lax.rem(self.z + d, self.zs)))
        for peer in peers:
            pl.semaphore_signal(barrier, inc=1, device_id=peer, device_id_type=MESH)
        pl.semaphore_wait(barrier, len(peers))


def send(src, dst, sems, at, peer, there=None):
    copy = pltpu.make_async_remote_copy(
        src_ref=src, dst_ref=dst, send_sem=sems[0].at[at],
        recv_sem=sems[1].at[at if there is None else there],
        device_id=peer, device_id_type=MESH,
    )
    copy.start()
    return copy


def await_copy(net, ref, sems, at, there=None):
    copy = pltpu.make_async_remote_copy(
        src_ref=ref, dst_ref=ref, send_sem=sems[0].at[at if there is None else there],
        recv_sem=sems[1].at[at], device_id=net.twin, device_id_type=MESH,
    )
    if there is None:
        copy.wait_recv()
    else:
        copy.wait_send()


def sum_order(zs, z):
    def key(zb):
        hops = z if zb > z else zs - 1 - z
        return (zb == z, hops, -abs(zb - z))
    return sorted(range(zs), key=key)


def spread_order(zs, z):
    return sorted(range(zs), key=lambda zb: (abs(zb - z), (zb > z) == (2 * z < zs)))


def reduce_scatter(net, pay, s, total, produce, fillers):
    zs = net.zs
    orders = [sum_order(zs, z) for z in range(zs)]
    blocks = [net.pick([orders[z][i] for z in range(zs)]) for i in range(zs)]
    first, second = {}, {}
    unit = s.pb.shape[-1] // 2

    def line_piece(p):
        def cut(zb):
            return pay[pl.ds(4 * net.rows * zb, 4 * net.rows), net.outer[p]]

        def own(value):
            s.pb[:, unit * p:unit * (p + 1)] = value.astype(BF)
        return cut, s.lo[p], s.li[p], own

    line = LineSum(net, (line_piece(0), line_piece(1)), s.ls)
    plane = PlaneSum(net, s.pb, lambda yx, p: (
        block(2 * yx[0] + yx[1], net.rows), pl.ds(unit * p, unit)), s.ps)

    def start_first(i, k):
        for p in range(2):
            a = (p + i) % 2
            yx = net.flip(a, 1 - a) if k == 0 else net.flip(a)
            first[i, p, k] = send(
                pay.at[net.chunk(blocks[i], yx), net.lanes[p]], s.r1[p].at[i, k],
                s.s1, (i, p, k), net.side(a))

    def start_second(i):
        for p in range(2):
            a = (p + i) % 2
            first[i, p, 0].wait_recv()
            at = (net.chunk(blocks[i], net.flip(1 - a)), net.lanes[p])
            pay[at] = (pay[at].astype(F32) + s.r1[p][i, 0].astype(F32)).astype(BF)
            second[i, p] = send(pay.at[at], s.r2[p].at[i], s.s2, (i, p), net.side(1 - a))

    def along(z, i):
        zb = orders[z][i]
        for p in range(2):
            first[i, p, 1].wait_recv()
            second[i, p].wait_recv()
            at = (net.chunk(zb, (net.y, net.x)), net.lanes[p])
            value = (pay[at].astype(F32) + s.r1[p][i, 1].astype(F32)
                     + s.r2[p][i].astype(F32))
            slots = []
            if zb >= z and z > 0:
                slots.append(i)
            if zb <= z and z < zs - 1:
                slots.append(i if zb < z else zs)
            for slot in slots:
                await_copy(net, s.zr[p].at[slot], s.s3, (slot, p))
                value = value + s.zr[p][slot].astype(F32)
            if zb == z:
                total[:, net.lanes[p]] = value
            else:
                s.zb[p][i] = value.astype(BF)
                nxt = z + 1 if zb > z else z - 1
                slot = orders[nxt].index(zb) if nxt != zb or zb > z else zs
                send(s.zb[p].at[i], s.zr[p].at[slot], s.s3, (i, p), net.at_z(nxt),
                     (slot, p))

    last = 0
    steps = [{} for _ in range(zs)]
    for z in range(zs):
        for i, zb in enumerate(orders[z]):
            hops = 0 if zb == z else z if zb > z else zs - 1 - z
            when = zs + 2 if zb == z else i + 2 + min(hops, 1)
            steps[z].setdefault(when, []).append(i)
            last = max(last, when)
    for i in range(last + 1):
        if i < zs:
            produce(blocks[i], i)
            start_first(i, 0)
        if 1 <= i <= zs:
            start_second(i - 1)
        if i < zs:
            start_first(i, 1)
        line.run(lambda n, p, hops: hops < zs and n + min(hops, 1) == i)
        if i == zs:
            line.run(lambda n, p, hops: hops == zs)
            plane.first()
        for z in range(zs):
            if i in steps[z]:
                @pl.when(net.z == z)
                def _():
                    for k in steps[z][i]:
                        along(z, k)
        if i == zs + 1:
            plane.second()
        if i in fillers:
            fillers[i]()
    def plane_done(p, value):
        total[:, net.outer[p]] = value
    plane.last(plane_done)

    def finish():
        drain([*first.values(), *second.values(), *plane.copies])
        line.finish()
        for i in range(zs - 1):
            for p in range(2):
                await_copy(net, s.zb[p].at[i], s.s3, (i, p), (i, p))
    return finish


def plane_own(net, ref, at, i, p, k, s):
    ref = ref.at[at((net.y, net.x), p)]
    return send(ref, ref, s.o, (i, p, k), net.side((p + i + k) % 2))


def plane_relay(net, ref, at, i, p, s):
    a = (p + i) % 2
    ref = ref.at[at(net.flip(a), p)]
    await_copy(net, ref, s.o, (i, p, 0))
    return send(ref, ref, s.f, (i, p), net.side(1 - a))


def plane_rest(net, ref, at, i, p, s):
    a = (p + i) % 2
    await_copy(net, ref.at[at(net.flip(1 - a), p)], s.o, (i, p, 1))
    await_copy(net, ref.at[at(net.flip(0, 1), p)], s.f, (i, p))


def plane_drain(net, ref, at, i, p, s):
    ref = ref.at[at((net.y, net.x), p)]
    for k in range(2):
        await_copy(net, ref, s.o, (i, p, k), (i, p, k))
    await_copy(net, ref, s.f, (i, p), (i, p))


def at_each(net, body):
    for z in range(net.zs):
        @pl.when(net.z == z)
        def _():
            body(z)


def onward(zs, z, zb):
    return [(k, other) for k, other in enumerate((z - 1, z + 1))
            if 0 <= other < zs and (zb == z or (zb > z) == (other < z))]


def pass_on(net, z, zb, p, ref, s):
    for k, other in onward(net.zs, z, zb):
        send(ref, ref, s.z, (zb, p, k), net.at_z(other), (zb, p, 0))


def pass_drain(net, z, zb, p, ref, s):
    for k, other in onward(net.zs, z, zb):
        await_copy(net, ref, s.z, (zb, p, 0), (zb, p, k))


def all_gather(net, full, s, parts):
    zs = net.zs
    place = lambda zb: lambda yx, p: (net.chunk(zb, yx), net.parts[p])
    mine = lambda zb, p: full.at[place(zb)((net.y, net.x), p)]

    for p in range(2):
        parts[p]()
        at_each(net, lambda z: pass_on(net, z, z, p, mine(z, p), s))
        plane_own(net, full, place(net.z), 0, p, 0, s)
    for p in range(2):
        plane_own(net, full, place(net.z), 0, p, 1, s)

    def rest(z):
        order = spread_order(zs, z)
        for i in range(1, zs):
            for p in range(2):
                await_copy(net, mine(order[i], p), s.z, (order[i], p, 0))
                pass_on(net, z, order[i], p, mine(order[i], p), s)
                plane_own(net, full, place(order[i]), i, p, 0, s)
            for p in range(2):
                plane_relay(net, full, place(order[i - 1]), i - 1, p, s)
            for p in range(2):
                plane_own(net, full, place(order[i]), i, p, 1, s)
        for p in range(2):
            plane_relay(net, full, place(order[zs - 1]), zs - 1, p, s)
        for i in range(zs):
            for p in range(2):
                plane_rest(net, full, place(order[i]), i, p, s)
    at_each(net, rest)

    def finish():
        def go(z):
            order = spread_order(zs, z)
            for i in range(zs):
                for p in range(2):
                    pass_drain(net, z, order[i], p, mine(order[i], p), s)
                    plane_drain(net, full, place(order[i]), i, p, s)
        at_each(net, go)
    return finish


class PlaneSum:
    def __init__(self, net, ref, at, s):
        self.net, self.ref, self.at, self.s = net, ref, at, s
        self.copies = []

    def first(self):
        net, s = self.net, self.s
        for k in range(2):
            for p in range(2):
                yx = net.flip(p, 1 - p) if k == 0 else net.flip(p)
                self.copies.append(send(self.ref.at[self.at(yx, p)], s.r1.at[p, k], s.s1,
                                        (p, k), net.side(p)))

    def second(self):
        net, s = self.net, self.s
        for p in range(2):
            await_copy(net, s.r1.at[p, 0], s.s1, (p, 0))
            at = self.at(net.flip(1 - p), p)
            self.ref[at] = (self.ref[at].astype(F32) + s.r1[p, 0].astype(F32)).astype(BF)
            self.copies.append(send(self.ref.at[at], s.r2.at[p], s.s2, (p,), net.side(1 - p)))

    def last(self, done):
        net, s = self.net, self.s
        for p in range(2):
            await_copy(net, s.r1.at[p, 1], s.s1, (p, 1))
            await_copy(net, s.r2.at[p], s.s2, (p,))
            value = self.ref[self.at((net.y, net.x), p)].astype(F32)
            done(p, value + s.r1[p, 1].astype(F32) + s.r2[p].astype(F32))


class LineSum:
    def __init__(self, net, pieces, sems):
        self.net, self.pieces, self.sems = net, pieces, sems
        self.orders = [sum_order(net.zs, z) for z in range(net.zs)]

    def hops(self, z, i):
        zb = self.orders[z][i]
        return self.net.zs if zb == z else z if zb > z else self.net.zs - 1 - z

    def move(self, z, i, p):
        net, zs = self.net, self.net.zs
        cut, out, inn, own = self.pieces[p]
        zb = self.orders[z][i]
        value = cut(zb)
        slots = []
        if zb >= z and z > 0:
            slots.append(i)
        if zb <= z and z < zs - 1:
            slots.append(i if zb < z else zs)
        for slot in slots:
            await_copy(net, inn.at[slot], self.sems, (slot, p))
            value = value + inn[slot].astype(F32)
        if zb == z:
            own(value)
            return
        out[i] = value.astype(BF)
        nxt = z + 1 if zb > z else z - 1
        slot = self.orders[nxt].index(zb) if nxt != zb or zb > z else zs
        send(out.at[i], inn.at[slot], self.sems, (i, p), net.at_z(nxt), (slot, p))

    def run(self, chosen):
        def go(z):
            for i in range(self.net.zs):
                for p in range(len(self.pieces)):
                    if chosen(i, p, self.hops(z, i)):
                        self.move(z, i, p)
        at_each(self.net, go)

    def finish(self):
        for i in range(self.net.zs - 1):
            for p, piece in enumerate(self.pieces):
                await_copy(self.net, piece[1].at[i], self.sems, (i, p), (i, p))


def drain(copies):
    for copy in copies:
        copy.wait_send()


def by_rows(count, step, body):
    def run(i, carry):
        body(pl.ds(pl.multiple_of(i * step, step), step))
        return carry
    lax.fori_loop(0, count // step, run, 0)


def named(tree):
    return Names(**{k: named(v) if isinstance(v, dict) else v for k, v in tree.items()})


def step_body(zs, tree, inverse, *refs):
    r = Names(**jax.tree.unflatten(tree, refs[13:]))
    for key, value in vars(r).items():
        if isinstance(value, dict):
            setattr(r, key, named(value))
    (queries, keys, values, out_grad, w_gate, w_up, w_down) = refs[:7]
    (d_queries, d_keys, d_values, d_gate, d_up, d_down) = refs[7:13]
    toks, width = queries.shape
    half = width // 2
    every = 2 * toks
    rows = width // (4 * zs)
    zrows = 4 * rows
    net = Net(zs, rows, width + half)
    c = net.c
    mine, theirs = block(c, toks), block(1 - c, toks)
    gl, ul, dl = pl.ds(0, half), pl.ds(half, half), pl.ds(width, half)
    wide = pl.ds(0, width)
    hid = block(c, half)

    token_at = lambda yx, p: (block(2 * (2 * yx[0] + yx[1]) + c, toks), block(p, half))
    spot = block(2 * net.g + c, toks)
    loads = Names()
    loads.k, loads.a, loads.b, loads.c, loads.v, loads.q, loads.o = [
        pltpu.make_async_copy(src, dst, r.ld.at[i]) for i, (src, dst) in enumerate((
            (keys, r.kf), (w_gate.at[:, hid], r.wab.at[:, gl]), (w_up.at[:, hid], r.wab.at[:, ul]),
            (w_down.at[hid, :], r.wc), (values, r.vf), (queries, r.qa.at[spot, :]),
            (out_grad, r.oa.at[spot, :])))]
    for load in vars(loads).values():
        load.start()
    net.greet()
    tsem = r.tsem
    done = []

    def twin(src, dst, k):
        copy = send(src, dst, tsem, k, net.twin)
        done.append(copy)
        return copy

    xb, gu, ab, eb = r.xb, r.gu, r.ab, r.eb
    loads.k.wait()
    xb[mine, :] = r.kf[...].astype(BF)
    keys_in = twin(xb.at[mine, :], xb.at[mine, :], 0)
    qa, oa = r.qa, r.oa
    loads.q.wait()
    for p in range(2):
        plane_own(net, qa, token_at, 0, p, 0, r.qsem)
    loads.a.wait()
    loads.b.wait()
    r.abb[...] = r.wab[...].astype(BF)
    loads.c.wait()
    r.cb[...] = r.wc[...].astype(BF)
    keys_in.wait_recv()
    gu[...] = dot(xb[...], r.abb[...])

    def active_rows(at):
        g, u = gu[at, gl], gu[at, ul]
        ab[at, :] = (g * jax.nn.sigmoid(g) * u).astype(BF)
    by_rows(every, 32, active_rows)

    loads.v.wait()
    ep, er = r.ep, r.er
    ep[mine, :] = dot(ab[mine, :], r.cb[...]) - r.vf[...]
    e_out = [twin(ep.at[mine, :], er.at[mine, :], 3)]
    ep[theirs, :] = dot(ab[theirs, :], r.cb[...])
    e_out.append(twin(ep.at[theirs, :], er.at[theirs, :], 4))
    for copy, at in zip(e_out, (theirs, mine)):
        copy.wait_recv()
        eb[at, :] = (ep[at, :] + er[at, :]).astype(BF)
    da, dgu = r.da, r.dgu
    da[...] = dot_nt(eb[...], r.cb[...])

    def d_rows(at):
        g, u, d = gu[at, gl], gu[at, ul], da[at, :]
        sig = jax.nn.sigmoid(g)
        dgu[at, ul] = (d * g * sig).astype(BF)
        dgu[at, gl] = (d * u * sig * (1.0 + g * (1.0 - sig))).astype(BF)
    by_rows(every, 32, d_rows)
    r.dguT[...] = dgu[...].T
    r.eT[...] = eb[...].T

    pay = r.pay0

    def key_block(zb, i):
        at = block(zb, zrows)
        pay[at, wide] = dot(r.dguT[at, :], xb[...]).astype(BF)
        pay[at, dl] = dot(r.eT[at, :], ab[...]).astype(BF)

    def turn_weights():
        r.wabt[...] = r.wab[...].T
        r.wct[...] = r.wc[...].T

    def to_twin(ref, k):
        return [twin(ref.at[block(2 * g + c, toks), :], ref.at[block(2 * g + c, toks), :], k + g)
                for g in range(4)]

    def share_tokens():
        for p in range(2):
            plane_relay(net, qa, token_at, 0, p, r.qsem)

    def select_lanes():
        h = lax.broadcasted_iota(jnp.int32, (half, 512), 0)
        lane = lax.broadcasted_iota(jnp.int32, (half, 512), 1)
        g, l = lane // 128, lane % 128
        hit = (h == (half // 2) * (l // rows) + rows * g + l % rows) & (l < 2 * rows)
        r.sel[...] = jnp.where(hit, 1.0, 0.0).astype(BF)
        r.wgu[...] = jnp.zeros((256, width), BF)

    def turn_keys():
        r.xT[...] = xb[...].T

    grad = r.grad
    rs0 = reduce_scatter(net, pay, r.rs0, grad, key_block,
                         {0: turn_keys, 2: select_lanes, 3: turn_weights, zs + 1: share_tokens})

    own = net.chunk(net.z, (net.y, net.x))
    squares = jnp.sum(grad[:, dl] * grad[:, dl], axis=1, keepdims=True)
    r.sq[0] = jnp.broadcast_to(squares, (rows, 128))
    norm_in = twin(r.sq.at[0], r.sq.at[1], 5)
    scale_of = lambda sq: jnp.sqrt(sq / width + EPSILON)
    scale = r.scale

    gz, rz = r.gz, r.rz
    line = r.line
    gz_at = lambda zb, p: gz.at[pl.ds(rows * zb, rows), pl.ds(half * p, half)]
    rz_at = lambda zb: rz.at[pl.ds(zrows * zb, zrows), :]
    g = grad[:, wide]
    sc = scale_of(jnp.sum(g * g, axis=1, keepdims=True))
    scale[0] = jnp.broadcast_to(sc, (rows, 128))
    gz[block(net.z, rows), :] = (r.wabt[own, :] - STEP_SIZE * g / sc).astype(BF)
    at_each(net, lambda z: [pass_on(net, z, z, p, gz_at(z, p), line) for p in range(2)])
    norm_in.wait_recv()
    sc = scale_of((r.sq[0] + r.sq[1])[:, :1])
    scale[1] = jnp.broadcast_to(sc, (rows, 128))
    down = (r.wct[own, :] - STEP_SIZE * grad[:, dl] / sc).astype(BF)
    r.dsl[...] = dot(down, r.sel[...]).astype(BF)
    ssem = r.ssem
    near = [net.flip(0), net.flip(1), net.flip(0, 1)]
    near_at = [net.side(0), net.side(1), net.across()]
    lane_of = lambda yx: block(2 * yx[0] + yx[1], 128)
    rz[own, :] = r.dsl[:, lane_of((net.y, net.x))]
    slices = [send(r.dsl.at[:, lane_of(yx)], rz.at[own, :], ssem, k, peer)
              for k, (yx, peer) in enumerate(zip(near, near_at))]
    loads.o.wait()
    for ref, k, sems in ((oa, 0, r.osem), (qa, 1, r.qsem), (oa, 1, r.osem)):
        for p in range(2):
            plane_own(net, ref, token_at, 0, p, k, sems)
    xsem = r.xsem

    def direct(z):
        for other in range(zs):
            if other != z:
                send(rz_at(z), rz_at(z), xsem, (other,), net.at_z(other), (z,))
    def gather_line(first, last):
        def go(z):
            for zb in spread_order(zs, z)[first:last]:
                for p in range(2):
                    await_copy(net, gz_at(zb, p), line.z, (zb, p, 0))
                    pass_on(net, z, zb, p, gz_at(zb, p), line)
            if last == zs:
                for zb in spread_order(zs, z)[1:]:
                    await_copy(net, rz_at(zb), xsem, (zb,))
        at_each(net, go)

    gather_line(1, 2)
    for copy in slices:
        copy.wait_recv()
    at_each(net, direct)
    for p in range(2):
        plane_relay(net, oa, token_at, 0, p, r.osem)
    gather_line(2, 3)
    for p in range(2):
        plane_rest(net, qa, token_at, 0, p, r.qsem)
    q_in = to_twin(qa, 20)
    gather_line(3, zs)

    wgu, hgu, dact, hd, hact = r.wgu, r.hgu, r.dact, r.hd, r.hact
    wgu[:2 * rows, :] = gz[:2 * rows, :]
    wgu[128:128 + 2 * rows, :] = gz[2 * rows:, :]
    for copy in q_in:
        copy.wait_recv()
    for p in range(2):
        plane_rest(net, oa, token_at, 0, p, r.osem)
    o_in = to_twin(oa, 24)
    hgu[...] = dot_nt(wgu[...], qa[...])
    r.rzT[...] = rz[...].T
    for copy in o_in:
        copy.wait_recv()
    dact[...] = dot_nt(r.rzT[...], oa[...])

    def query_rows(at):
        up = pl.ds(pl.multiple_of(at.start + 128, 16), 16)
        g, u, d = hgu[at, :], hgu[up, :], dact[at, :]
        sig = jax.nn.sigmoid(g)
        hact[at, :] = (g * sig * u).astype(BF)
        hd[up, :] = (d * g * sig).astype(BF)
        hd[at, :] = (d * u * sig * (1.0 + g * (1.0 - sig))).astype(BF)
    by_rows(128, 16, query_rows)
    hsum = r.hsum
    hdn8, hgu8 = r.hdn8, r.hgu8
    hdn8[...] = dot(hact[...], oa[...])
    r.pd[...] = hdn8[...].T

    def own_down(value):
        r.dout[...] = value.astype(BF)

    def own_wide(p):
        def store(value):
            hsum[:, half * p:half * (p + 1)] = value
        return store

    def wide_cut(p):
        return lambda zb: hgu8[pl.ds(rows * zb + (128 - 2 * rows) * (zb // 2), rows),
                               half * p:half * (p + 1)]

    pieces = (
        (lambda zb: r.pd[zrows * zb:zrows * (zb + 1), :], r.ldo, r.ldi, own_down),
        (wide_cut(0), r.lgo0, r.lgi0, own_wide(0)),
        (wide_cut(1), r.lgo1, r.lgi1, own_wide(1)),
    )
    summing = LineSum(net, pieces, r.lsem)
    summing.run(lambda i, p, hops: hops == 0 and i == 0 and p == 0)
    hgu8[...] = dot(hd[...], qa[...])
    summing.run(lambda i, p, hops: hops == 0 and i + p > 0)
    r.hdT[...] = hd[...].T
    hd = r.hdT
    dqs, dqm, dqt = r.dqs, r.dqm, r.dqt
    dq_in = []
    for g in range(4):
        at = block(g, toks)
        dqs[at, :] = dot(hd[block(2 * g + 1 - c, toks), :], wgu[...]).astype(BF)
        dq_in.append(twin(dqs.at[at, :], dqt.at[at, :], 28 + g))
    for g in range(4):
        at = block(g, toks)
        mid = dot(hd[block(2 * g + c, toks), :], wgu[...])
        dq_in[g].wait_recv()
        dqm[at, :] = (mid + dqt[at, :].astype(F32)).astype(BF)
    query_sum = PlaneSum(
        net, dqm, lambda yx, p: (block(2 * yx[0] + yx[1], toks), block(p, half)), r.dqs3)
    query_sum.first()
    summing.run(lambda i, p, hops: hops == 1)
    summing.run(lambda i, p, hops: 1 < hops < zs)
    query_sum.second()
    summing.run(lambda i, p, hops: hops == zs and p == 0)
    dout, din = r.dout, r.din
    mine_at = lambda yx: block(2 * yx[0] + yx[1], rows)
    usem = r.usem
    units = [send(dout.at[mine_at(yx), :], din.at[:, lane_of((net.y, net.x))], usem, k, peer)
             for k, (yx, peer) in enumerate(zip(near, near_at))]
    din[:, lane_of((net.y, net.x))] = dout[mine_at((net.y, net.x)), :]
    summing.run(lambda i, p, hops: hops == zs and p > 0)
    for copy in units:
        copy.wait_recv()
    hsum[:, dl] = dot_nt(din[...], r.sel[...])

    product = jnp.sum(-STEP_SIZE * hsum[:, dl] * grad[:, dl], axis=1, keepdims=True)
    r.sq[2] = jnp.broadcast_to(product, (rows, 128))
    product_in = twin(r.sq.at[2], r.sq.at[3], 7)
    back = r.full1

    def turned(h, g, sc, prod):
        return (-STEP_SIZE * h / sc - g * prod / (width * sc * sc * sc)).astype(BF)

    def wide_back():
        h, g = hsum[:, wide], grad[:, wide]
        prod = jnp.sum(-STEP_SIZE * h * g, axis=1, keepdims=True)
        back[own, wide] = turned(h, g, scale[0][:, :1], prod)

    def down_back():
        product_in.wait_recv()
        prod = (r.sq[2] + r.sq[3])[:, :1]
        back[own, dl] = turned(hsum[:, dl], grad[:, dl], scale[1][:, :1], prod)

    ag1 = all_gather(net, back, r.ag1, (wide_back, down_back))

    def query_done(p, value):
        d_queries[:, p * half:(p + 1) * half] = value.astype(BF)
    query_sum.last(query_done)

    pq, tb, ec = r.pq, r.tb, r.ec
    pq[...] = dot_nt(xb[...], back[:, wide])

    def t_rows(at):
        g, u = gu[at, gl], gu[at, ul]
        p, q = pq[at, gl], pq[at, ul]
        sig = jax.nn.sigmoid(g)
        tb[at, :] = (q * g * sig + p * u * sig * (1.0 + g * (1.0 - sig))).astype(BF)
    by_rows(every, 32, t_rows)
    sp, sr, sb = r.sp, r.sr, r.sb
    second_out = []
    for k, at in enumerate((mine, theirs)):
        sp[at, :] = dot_nt(ab[at, :], back[:, dl]) + dot(tb[at, :], r.cb[...])
        second_out.append(twin(sp.at[at, :], sr.at[at, :], 8 + k))
    ec[...] = dot(eb[...], back[:, dl])
    placed, hp, hdn = r.placed, r.hp, r.hdn
    placed[...] = jnp.zeros_like(placed)
    hdn[...] = jnp.zeros_like(hdn)
    for k in range(2):
        to = pl.ds(pl.multiple_of((half // 2) * k + rows * net.g, rows), rows)
        to_up = pl.ds(pl.multiple_of(half + (half // 2) * k + rows * net.g, rows), rows)
        placed[to, :] = hgu8[k * rows:(k + 1) * rows, :]
        placed[to_up, :] = hgu8[128 + k * rows:128 + (k + 1) * rows, :]
        hdn[to, :] = hdn8[k * rows:(k + 1) * rows, :]
    hp[...] = placed[...].T
    r.taT[:, pl.ds(0, every)] = tb[...].T
    r.taT[:, pl.ds(every, every)] = ab[...].T
    for copy, at in zip(second_out, (theirs, mine)):
        copy.wait_recv()
        sb[at, :] = (sp[at, :] + sr[at, :]).astype(BF)
    prow = 2 * rows
    dsw, dloc = r.dsw, r.dloc
    dloc[...] = (r.hdn[...] + dot(r.taT[:, pl.ds(0, every)], eb[...])
                 + dot(r.taT[:, pl.ds(every, every)], sb[...])).astype(BF)
    swaps = []
    for k in range(zs // 2):
        slot = (zs // 2) * c + k
        swaps.append(twin(dloc.at[block(2 * k + 1 - c, prow), :], dsw.at[slot], 10 + k))
        dsw[slot] = dloc[block(2 * k + c, prow), :]
    d_values[...] = -(sp[mine, :] + sr[mine, :])
    ec[...] += dot_nt(sb[...], r.cb[...])
    gub = r.gub

    def pull_rows(at):
        g, u, d = gu[at, gl], gu[at, ul], da[at, :]
        p, q, back_a = pq[at, gl], pq[at, ul], ec[at, :]
        sig = jax.nn.sigmoid(g)
        sneg = 1.0 - sig
        h = g * sig
        slope = sig * (1.0 + g * sneg)
        bend = sig * sneg * (2.0 + g * (1.0 - 2.0 * sig))
        pd = p * d
        gub[at, gl] = (back_a * u * slope + pd * u * bend + q * d * slope).astype(BF)
        gub[at, ul] = (back_a * h + pd * slope).astype(BF)
    by_rows(every, 32, pull_rows)

    pay2 = r.pay2

    def last_block(zb, i):
        at = block(zb, zrows)
        pay2[at, wide] = (r.hp[at, :] + dot(r.xT[at, :], gub[...])).astype(BF)
        if i == 0:
            for copy in swaps:
                copy.wait_recv()
        for y in range(2):
            for x in range(2):
                pay2[block(4 * zb + 2 * y + x, rows), dl] = (
                    dsw[zb, y * rows:(y + 1) * rows, x * half:(x + 1) * half])

    def key_back():
        r.kp[...] = dot(dgu[...], back[:, wide])

    def key_back_second():
        r.kp[...] += dot_nt(gub[...], r.abb[...])
        r.kin = twin(r.kp.at[theirs, :], r.kr, 10 + zs // 2)

    last = r.last
    rs2 = reduce_scatter(net, pay2, r.rs2, last, last_block,
                         {0: key_back, 1: key_back_second})
    fin = r.fin
    fin[block(net.g, rows), :] = last[...].astype(BF)
    s = r.ag2
    fin_at = lambda yx, p: (block(2 * yx[0] + yx[1], rows), net.parts[p])
    for k in range(2):
        for p in range(2):
            plane_own(net, fin, fin_at, 0, p, k, s)
    for p in range(2):
        plane_relay(net, fin, fin_at, 0, p, s)
    r.kin.wait_recv()
    d_keys[...] = r.kp[mine, :] + r.kr[...]
    for p in range(2):
        plane_rest(net, fin, fin_at, 0, p, s)
    swap = twin(fin.at[block(1 - c, prow), wide], r.tw, 11 + zs // 2)
    lanes = block(c, half)
    others = block(1 - c, half)
    d_gate[:, lanes] = fin[block(c, prow), gl].astype(F32) * inverse
    d_up[:, lanes] = fin[block(c, prow), ul].astype(F32) * inverse
    for y in range(2):
        for x in range(2):
            g = 2 * y + x
            d_down[y * rows:(y + 1) * rows, x * half:(x + 1) * half] = (
                fin[g * rows:(g + 1) * rows, width:].astype(F32) * inverse)
    swap.wait_recv()
    d_gate[:, others] = r.tw[:, :half].astype(F32) * inverse
    d_up[:, others] = r.tw[:, half:].astype(F32) * inverse
    drain(done + slices + units + query_sum.copies)
    for finish in (rs0, ag1, rs2, summing.finish):
        finish()
    for p in range(2):
        plane_drain(net, qa, token_at, 0, p, r.qsem)
        plane_drain(net, oa, token_at, 0, p, r.osem)
        plane_drain(net, fin, fin_at, 0, p, s)

    def drain_line(z):
        for zb in range(zs):
            for p in range(2):
                pass_drain(net, z, zb, p, gz_at(zb, p), line)
            if zb != z:
                await_copy(net, rz_at(z), xsem, (zb,), (zb,))
    at_each(net, drain_line)


def hand_over(*refs):
    for src, dst in zip(refs[:6], refs[6:]):
        dst[...] = src[...]


def fused_step(queries, key_tokens, values, out_grad, w_gate, w_up, w_down, zs, inverse):
    toks, width = queries.shape
    half, every, rows = width // 2, 2 * toks, width // (4 * zs)
    plane = 4 * every
    total = width + half
    side, main = lane_parts(total)
    unit = side[0].size
    f32 = lambda *shape: VM(shape, F32)
    bf = lambda *shape: VM(shape, BF)
    sems = lambda *shape: (DMA(shape), DMA(shape))
    both = lambda *shape: tuple(VM(shape + (part.size,), BF) for part in main)
    summed = dict(
        r1=both(zs, 2, rows), r2=both(zs, rows), zb=both(zs - 1, rows), zr=both(zs + 1, rows),
        s1=sems(zs, 2, 2), s2=sems(zs, 2), s3=sems(zs + 1, 2), pb=bf(4 * rows, 2 * unit),
        lo=(bf(zs - 1, 4 * rows, unit),) * 2, li=(bf(zs + 1, 4 * rows, unit),) * 2,
        ls=sems(zs + 1, 2),
        ps=dict(r1=bf(2, 2, rows, unit), r2=bf(2, rows, unit), s1=sems(2, 2), s2=sems(2)))
    spread = lambda depth: dict(
        z=sems(depth, 2, 2), o=sems(depth, 2, 2), f=sems(depth, 2))
    scratch = dict(
        kf=f32(toks, width), vf=f32(toks, width), wab=f32(width, width), wc=f32(half, width),
        wabt=f32(width, width), wct=f32(width, half), gu=f32(every, width), ep=f32(every, width),
        er=f32(every, width), da=f32(every, half), grad=f32(rows, total), hsum=f32(rows, total),
        last=f32(rows, total), sq=f32(4, rows, 128), scale=f32(2, rows, 128),
        hgu=f32(256, plane), dact=f32(128, plane), hdn8=f32(128, width), hgu8=f32(256, width),
        pd=f32(width, 128), placed=f32(width, width), hp=f32(width, width), hdn=f32(half, width),
        pq=f32(every, width), ec=f32(every, half), sp=f32(every, width), sr=f32(every, width),
        kp=f32(every, width), kr=f32(toks, width),
        xb=bf(every, width), qa=bf(plane, width), oa=bf(plane, width), abb=bf(width, width),
        cb=bf(half, width), ab=bf(every, half), eb=bf(every, width), dgu=bf(every, width),
        dguT=bf(width, every), eT=bf(width, every), xT=bf(width, every), hd=bf(256, plane),
        hdT=bf(plane, 256), hact=bf(128, plane), rzT=bf(128, width), tb=bf(every, half),
        sel=bf(half, 512), wgu=bf(256, width), gz=bf(zs * rows, width), rz=bf(width, 128),
        dsl=bf(rows, 512), dout=bf(4 * rows, 128), din=bf(rows, 512), dqs=bf(4 * toks, width),
        dqm=bf(4 * toks, width), dqt=bf(4 * toks, width),
        ldo=bf(zs - 1, 4 * rows, 128), ldi=bf(zs + 1, 4 * rows, 128),
        lgo0=bf(zs - 1, rows, half), lgi0=bf(zs + 1, rows, half),
        lgo1=bf(zs - 1, rows, half), lgi1=bf(zs + 1, rows, half),
        sb=bf(every, width), taT=bf(half, 2 * every), gub=bf(every, width), dloc=bf(half, width),
        dsw=bf(zs, 2 * rows, width), pay0=bf(width, total), pay2=bf(width, total),
        full1=bf(width, total), fin=bf(4 * rows, total), tw=bf(2 * rows, width),
        rs0=summed, rs2=summed, ag1=spread(zs), ag2=spread(1), qsem=spread(1), osem=spread(1),
        line=spread(zs), lsem=sems(zs + 1, 3), xsem=sems(zs), ssem=sems(3), usem=sems(3),
        dqs3=dict(r1=bf(2, 2, toks, half), r2=bf(2, toks, half), s1=sems(2, 2), s2=sems(2)),
        tsem=sems(32), ld=DMA((7,)))
    shapes, tree = jax.tree.flatten(scratch)
    token = jax.ShapeDtypeStruct((toks, width), F32)
    weight = jax.ShapeDtypeStruct((2 * rows, width), F32)
    results = pl.pallas_call(
        functools.partial(step_body, zs, tree, inverse),
        out_shape=(jax.ShapeDtypeStruct((toks, width), BF), token, token, weight, weight, weight),
        in_specs=[pl.BlockSpec(memory_space=pltpu.HBM)] * 7,
        out_specs=[pl.BlockSpec(memory_space=VM)] * 6,
        scratch_shapes=shapes,
        compiler_params=pltpu.CompilerParams(
            collective_id=0, has_side_effects=True, vmem_limit_bytes=52 * 1024 * 1024),
    )(*(pltpu.with_memory_space_constraint(x, pltpu.HBM) for x in (
        queries, key_tokens, values, out_grad, w_gate, w_up, w_down)))
    return pl.pallas_call(
        hand_over,
        out_shape=tuple(jax.ShapeDtypeStruct(item.shape, item.dtype) for item in results),
        in_specs=[pl.BlockSpec(memory_space=VM)] * 6,
        out_specs=[pl.BlockSpec(memory_space=VM)] * 6,
        compiler_params=pltpu.CompilerParams(vmem_limit_bytes=8 * 1024 * 1024),
    )(*results)


def matmul(left, right):
    return dot(left.astype(BF), right.astype(BF))


def key_grad(w_gate, w_up, w_down, key_rows, value_rows):
    hidden_gate = matmul(key_rows, w_gate)
    hidden_up = matmul(key_rows, w_up)
    sig = jax.nn.sigmoid(hidden_gate)
    active = hidden_gate * sig * hidden_up
    error = matmul(active, w_down) - value_rows
    d_active = matmul(error, w_down.T)
    d_hup = d_active * hidden_gate * sig
    d_hgate = d_active * hidden_up * sig * (1.0 + hidden_gate * (1.0 - sig))
    return (matmul(d_hgate.T, key_rows), matmul(d_hup.T, key_rows), matmul(error.T, active))


def query_grad(fast_t, query_rows, grad_rows):
    gate_t, up_t, down_t = fast_t
    hidden_gate = dot(query_rows, gate_t.T)
    hidden_up = dot(query_rows, up_t.T)
    sig = jax.nn.sigmoid(hidden_gate)
    active = (hidden_gate * sig * hidden_up).astype(BF)
    d_active = dot(grad_rows, down_t)
    d_hup = (d_active * hidden_gate * sig).astype(BF)
    d_hgate = (d_active * hidden_up * sig * (1.0 + hidden_gate * (1.0 - sig))).astype(BF)
    d_rows = (dot(d_hgate, gate_t) + dot(d_hup, up_t)).astype(BF)
    return (d_rows, active, d_hgate, d_hup)


def general_step(queries, key_tokens, values, out_grad, w_gate, w_up, w_down, inverse):
    gs, toks = lax.axis_size("grp"), lax.axis_size("tok")
    full_width = w_gate.shape[0]
    rows = 3 * full_width // (gs * toks)
    me = lax.axis_index("tok") * gs + lax.axis_index("grp")

    def reduce_units(x):
        y = x.reshape(toks, gs * rows, full_width)
        y = lax.psum_scatter(y, "tok", scatter_dimension=0, tiled=True)[0]
        return lax.psum_scatter(y.reshape(gs, rows, full_width), "grp", scatter_dimension=0, tiled=True)[0]

    def gather_units(y):
        full = lax.all_gather(lax.all_gather(y, "grp"), "tok").reshape(3, full_width, full_width)
        return full[0], full[1], full[2]

    local_grad, pullback = jax.vjp(key_grad, w_gate, w_up, w_down, key_tokens, values)
    grad = reduce_units(jnp.stack(local_grad))
    scale = jnp.sqrt(jnp.sum(grad * grad, axis=1, keepdims=True) / full_width + EPSILON)
    weights = jnp.concatenate((w_gate, w_up, w_down), axis=1)
    mine = lax.dynamic_slice_in_dim(weights, me * rows, rows, 1).T
    fast_t = gather_units((mine - STEP_SIZE * grad / scale).astype(BF))
    d_queries, active, d_hgate, d_hup = query_grad(fast_t, queries, out_grad)
    query_part = reduce_units(
        jnp.stack((dot(d_hgate.T, queries), dot(d_hup.T, queries), dot(out_grad.T, active))))
    product = jnp.sum(-STEP_SIZE * query_part * grad, axis=1, keepdims=True)
    cot = (
        -STEP_SIZE * query_part / scale - grad * product / (full_width * scale * scale * scale)
    ).astype(BF)
    second = pullback(tuple(item.astype(F32) for item in gather_units(cot)))
    plain = (dot(queries.T, d_hgate), dot(queries.T, d_hup), dot(active.T, out_grad))
    combined = jnp.stack(tuple(left + right for left, right in zip(plain, second[:3])))
    combined = combined.reshape(3, toks, full_width // toks, full_width).transpose(1, 0, 2, 3)
    summed = lax.all_gather(reduce_units(combined).astype(BF), "grp").astype(F32) * inverse
    summed = summed.reshape(3, full_width // toks, full_width)
    return (d_queries, second[3], second[4], summed[0], summed[1], summed[2])


def on_device(*arrays):
    gs, toks = lax.axis_size("grp"), lax.axis_size("tok")
    tokens, width = arrays[0].shape
    inverse = 1.0 / (tokens * gs * toks)
    zs = toks // 2
    fits = gs == 4 and toks % 4 == 0 and zs <= 4
    if fits and width % (64 * zs) == 0 and 2 * width <= 512 * zs and width % 256 == 0 and tokens % 128 == 0:
        return fused_step(*arrays, zs, inverse)
    return general_step(*arrays, inverse)


def solution(mesh):
    token = P(("grp", "tok"), None)
    return jax.shard_map(
        on_device,
        mesh=mesh,
        in_specs=(token, token, token, token, P(), P(), P()),
        out_specs=(token, token, token, P("tok", None), P("tok", None), P("tok", None)),
        check_vma=False,
    )
```

```python
import functools
from types import SimpleNamespace as Names

import jax
import jax.numpy as jnp
from jax import lax
from jax.experimental import pallas as pl
from jax.experimental.pallas import tpu as pltpu
from jax.sharding import PartitionSpec as P

STEP_SIZE = 0.02
EPSILON = 1e-06
MESH = pl.DeviceIdType.MESH
BF = jnp.bfloat16
F32 = jnp.float32
VM = pltpu.VMEM
DMA = pltpu.SemaphoreType.DMA


def dot(left, right):
    return jnp.dot(left, right, preferred_element_type=F32)


def dot_nt(left, right):
    return lax.dot_general(left, right, (((1,), (1,)), ((), ())), preferred_element_type=F32)


def block(index, size):
    return pl.ds(pl.multiple_of(index * size, size), size)


def lane_parts(width):
    unit = 128 * max(1, width // 1152)
    cut = width - 128 * ((width // 128 - 2 * (unit // 128)) // 2)
    return ((pl.ds(0, unit), pl.ds(unit, unit)),
            (pl.ds(2 * unit, cut - 2 * unit), pl.ds(cut, width - cut)))


class Net:
    def __init__(self, zs, rows, width):
        g, t = lax.axis_index("grp"), lax.axis_index("tok")
        self.zs, self.rows = zs, rows
        self.g, self.z, self.c = g, t // 2, lax.rem(t, 2)
        self.y, self.x = g // 2, lax.rem(g, 2)
        self.t = t
        self.outer, self.lanes = lane_parts(width)
        cut = 128 * ((width // 128 + 1) // 2)
        self.parts = (pl.ds(0, cut), pl.ds(cut, width - cut))
        self.twin = (g, 2 * self.z + 1 - self.c)

    def flip(self, *directions):
        y, x = self.y, self.x
        for a in directions:
            x = x + (1 - a) * (1 - 2 * x)
            y = y + a * (1 - 2 * y)
        return y, x

    def turn(self, n):
        return lax.rem(n + self.c, 2)

    def side(self, a):
        y, x = self.flip(a)
        return (2 * y + x, self.t)

    def across(self):
        y, x = self.flip(0, 1)
        return (2 * y + x, self.t)

    def at_z(self, z):
        return (self.g, 2 * z + self.c)

    def pick(self, table):
        value = table[0]
        for z in range(1, self.zs):
            value = jnp.where(self.z == z, table[z], value)
        return value

    def chunk(self, zb, yx):
        return block(4 * zb + 2 * yx[0] + yx[1], self.rows)

    def greet(self):
        barrier = pltpu.get_barrier_semaphore()
        peers = [self.twin, self.side(0), self.side(1), self.across()]
        for d in range(1, self.zs):
            peers.append(self.at_z(lax.rem(self.z + d, self.zs)))
        for peer in peers:
            pl.semaphore_signal(barrier, inc=1, device_id=peer, device_id_type=MESH)
        pl.semaphore_wait(barrier, len(peers))


def send(src, dst, sems, at, peer, there=None):
    copy = pltpu.make_async_remote_copy(
        src_ref=src, dst_ref=dst, send_sem=sems[0].at[at],
        recv_sem=sems[1].at[at if there is None else there],
        device_id=peer, device_id_type=MESH,
    )
    copy.start()
    return copy


def await_copy(net, ref, sems, at, there=None):
    copy = pltpu.make_async_remote_copy(
        src_ref=ref, dst_ref=ref, send_sem=sems[0].at[at if there is None else there],
        recv_sem=sems[1].at[at], device_id=net.twin, device_id_type=MESH,
    )
    if there is None:
        copy.wait_recv()
    else:
        copy.wait_send()


def sum_order(zs, z):
    def key(zb):
        hops = z if zb > z else zs - 1 - z
        return (zb == z, hops, -abs(zb - z))
    return sorted(range(zs), key=key)


def spread_order(zs, z):
    return sorted(range(zs), key=lambda zb: (abs(zb - z), (zb > z) == (2 * z < zs)))


def reduce_scatter(net, pay, s, total, produce, produce_side, fillers):
    zs = net.zs
    orders = [sum_order(zs, z) for z in range(zs)]
    blocks = [net.pick([orders[z][i] for z in range(zs)]) for i in range(zs)]
    first, second = {}, {}
    unit = s.pb.shape[-1] // 2

    def line_piece(p):
        def cut(zb):
            return pay[pl.ds(4 * net.rows * zb, 4 * net.rows), net.outer[p]]

        def own(value):
            s.pb[:, unit * p:unit * (p + 1)] = value.astype(BF)
        return cut, s.lo[p], s.li[p], own

    line = LineSum(net, (line_piece(0), line_piece(1)), s.ls)
    plane = PlaneSum(net, s.pb, lambda yx, p: (
        block(2 * yx[0] + yx[1], net.rows), pl.ds(unit * p, unit)), s.ps)

    def when_inside(inside, body):
        inner = (net.z > 0) & (net.z < zs - 1)
        pl.when(inner if inside else jnp.logical_not(inner))(body)

    def start_first(i, k):
        for p in range(2):
            a = net.turn(p + i)
            yx = net.flip(a, 1 - a) if k == 0 else net.flip(a)
            first[i, p, k] = send(
                pay.at[net.chunk(blocks[i], yx), net.lanes[p]], s.r1[p].at[i, k],
                s.s1, (i, p, k), net.side(a))

    def start_second(i):
        for p in range(2):
            a = net.turn(p + i)
            first[i, p, 0].wait_recv()
            at = (net.chunk(blocks[i], net.flip(1 - a)), net.lanes[p])
            pay[at] = (pay[at].astype(F32) + s.r1[p][i, 0].astype(F32)).astype(BF)
            second[i, p] = send(pay.at[at], s.r2[p].at[i], s.s2, (i, p), net.side(1 - a))

    def along(z, i):
        zb = orders[z][i]
        for p in range(2):
            first[i, p, 1].wait_recv()
            second[i, p].wait_recv()
            at = (net.chunk(zb, (net.y, net.x)), net.lanes[p])
            value = (pay[at].astype(F32) + s.r1[p][i, 1].astype(F32)
                     + s.r2[p][i].astype(F32))
            slots = []
            if zb >= z and z > 0:
                slots.append(i)
            if zb <= z and z < zs - 1:
                slots.append(i if zb < z else zs)
            for slot in slots:
                await_copy(net, s.zr[p].at[slot], s.s3, (slot, p))
                value = value + s.zr[p][slot].astype(F32)
            if zb == z:
                total[:, net.lanes[p]] = value
            else:
                s.zb[p][i] = value.astype(BF)
                nxt = z + 1 if zb > z else z - 1
                slot = orders[nxt].index(zb) if nxt != zb or zb > z else zs
                send(s.zb[p].at[i], s.zr[p].at[slot], s.s3, (i, p), net.at_z(nxt),
                     (slot, p))

    last = 0
    steps = [{} for _ in range(zs)]
    for z in range(zs):
        for i, zb in enumerate(orders[z]):
            hops = 0 if zb == z else z if zb > z else zs - 1 - z
            when = zs + 2 if zb == z else i + 2 + min(hops, 1)
            steps[z].setdefault(when, []).append(i)
            last = max(last, when)
    for i in range(last + 1):
        if i < zs:
            produce(blocks[i], i)
            start_first(i, 0)
        if i == 0:
            produce_side()
            line.run(lambda n, p, hops: hops == 0)
        if 1 <= i <= zs:
            start_second(i - 1)
        if i < zs:
            start_first(i, 1)
        line.run(lambda n, p, hops: 0 < hops < zs and max(n + 1, 2) == i)
        for inside in (True, False):
            if i == (zs - 1 if inside else zs):
                line.run(lambda n, p, hops: hops == zs, inside)
                when_inside(inside, plane.first)
        for z in range(zs):
            if i in steps[z]:
                @pl.when(net.z == z)
                def _():
                    for k in steps[z][i]:
                        along(z, k)
        for inside in (True, False):
            if i == (zs if inside else zs + 1):
                when_inside(inside, plane.second)
        if i in fillers:
            fillers[i]()
    def plane_done(p, value):
        total[:, net.outer[p]] = value
    plane.last(plane_done)

    def finish():
        drain([*first.values(), *second.values()])
        plane.finish()
        line.finish()
        for i in range(zs - 1):
            for p in range(2):
                await_copy(net, s.zb[p].at[i], s.s3, (i, p), (i, p))
    return finish


def plane_own(net, ref, at, i, p, k, s):
    ref = ref.at[at((net.y, net.x), p)]
    return send(ref, ref, s.o, (i, p, k), net.side(net.turn(p + i + k)))


def plane_relay(net, ref, at, i, p, s):
    a = net.turn(p + i)
    ref = ref.at[at(net.flip(a), p)]
    await_copy(net, ref, s.o, (i, p, 0))
    return send(ref, ref, s.f, (i, p), net.side(1 - a))


def plane_rest(net, ref, at, i, p, s):
    a = net.turn(p + i)
    await_copy(net, ref.at[at(net.flip(1 - a), p)], s.o, (i, p, 1))
    await_copy(net, ref.at[at(net.flip(0, 1), p)], s.f, (i, p))


def plane_drain(net, ref, at, i, p, s):
    ref = ref.at[at((net.y, net.x), p)]
    for k in range(2):
        await_copy(net, ref, s.o, (i, p, k), (i, p, k))
    await_copy(net, ref, s.f, (i, p), (i, p))


def at_each(net, body):
    for z in range(net.zs):
        @pl.when(net.z == z)
        def _():
            body(z)


def onward(zs, z, zb):
    return [(k, other) for k, other in enumerate((z - 1, z + 1))
            if 0 <= other < zs and (zb == z or (zb > z) == (other < z))]


def pass_on(net, z, zb, p, ref, s):
    for k, other in onward(net.zs, z, zb):
        send(ref, ref, s.z, (zb, p, k), net.at_z(other), (zb, p, 0))


def pass_drain(net, z, zb, p, ref, s):
    for k, other in onward(net.zs, z, zb):
        await_copy(net, ref, s.z, (zb, p, 0), (zb, p, k))


def all_gather(net, full, s, parts):
    zs = net.zs
    place = lambda zb: lambda yx, p: (net.chunk(zb, yx), net.parts[p])
    mine = lambda zb, p: full.at[place(zb)((net.y, net.x), p)]

    for p in range(2):
        parts[p]()
        at_each(net, lambda z: pass_on(net, z, z, p, mine(z, p), s))
        plane_own(net, full, place(net.z), 0, p, 0, s)
    for p in range(2):
        plane_own(net, full, place(net.z), 0, p, 1, s)

    def rest(z):
        order = spread_order(zs, z)
        for i in range(1, zs):
            for p in range(2):
                await_copy(net, mine(order[i], p), s.z, (order[i], p, 0))
                pass_on(net, z, order[i], p, mine(order[i], p), s)
                plane_own(net, full, place(order[i]), i, p, 0, s)
            for p in range(2):
                plane_relay(net, full, place(order[i - 1]), i - 1, p, s)
            for p in range(2):
                plane_own(net, full, place(order[i]), i, p, 1, s)
        for p in range(2):
            plane_relay(net, full, place(order[zs - 1]), zs - 1, p, s)
        for i in range(zs):
            for p in range(2):
                plane_rest(net, full, place(order[i]), i, p, s)
    at_each(net, rest)

    def finish():
        def go(z):
            order = spread_order(zs, z)
            for i in range(zs):
                for p in range(2):
                    pass_drain(net, z, order[i], p, mine(order[i], p), s)
                    plane_drain(net, full, place(order[i]), i, p, s)
        at_each(net, go)
    return finish


class PlaneSum:
    def __init__(self, net, ref, at, s):
        self.net, self.ref, self.at, self.s = net, ref, at, s

    def first(self):
        net, s = self.net, self.s
        for k in range(2):
            for p in range(2):
                yx = net.flip(p, 1 - p) if k == 0 else net.flip(p)
                send(self.ref.at[self.at(yx, p)], s.r1.at[p, k], s.s1, (p, k), net.side(p))

    def second(self):
        net, s = self.net, self.s
        for p in range(2):
            await_copy(net, s.r1.at[p, 0], s.s1, (p, 0))
            at = self.at(net.flip(1 - p), p)
            self.ref[at] = (self.ref[at].astype(F32) + s.r1[p, 0].astype(F32)).astype(BF)
            send(self.ref.at[at], s.r2.at[p], s.s2, (p,), net.side(1 - p))

    def last(self, done):
        net, s = self.net, self.s
        for p in range(2):
            await_copy(net, s.r1.at[p, 1], s.s1, (p, 1))
            await_copy(net, s.r2.at[p], s.s2, (p,))
            value = self.ref[self.at((net.y, net.x), p)].astype(F32)
            done(p, value + s.r1[p, 1].astype(F32) + s.r2[p].astype(F32))

    def finish(self):
        net, s = self.net, self.s
        for p in range(2):
            for k in range(2):
                await_copy(net, s.r1.at[p, k], s.s1, (p, k), (p, k))
            await_copy(net, s.r2.at[p], s.s2, (p,), (p,))


class LineSum:
    def __init__(self, net, pieces, sems):
        self.net, self.pieces, self.sems = net, pieces, sems
        self.orders = [sum_order(net.zs, z) for z in range(net.zs)]

    def hops(self, z, i):
        zb = self.orders[z][i]
        return self.net.zs if zb == z else z if zb > z else self.net.zs - 1 - z

    def move(self, z, i, p):
        net, zs = self.net, self.net.zs
        cut, out, inn, own = self.pieces[p]
        zb = self.orders[z][i]
        value = cut(zb)
        slots = []
        if zb >= z and z > 0:
            slots.append(i)
        if zb <= z and z < zs - 1:
            slots.append(i if zb < z else zs)
        for slot in slots:
            await_copy(net, inn.at[slot], self.sems, (slot, p))
            value = value + inn[slot].astype(F32)
        if zb == z:
            own(value)
            return
        out[i] = value.astype(BF)
        nxt = z + 1 if zb > z else z - 1
        slot = self.orders[nxt].index(zb) if nxt != zb or zb > z else zs
        send(out.at[i], inn.at[slot], self.sems, (i, p), net.at_z(nxt), (slot, p))

    def run(self, chosen, inside=None):
        def go(z):
            if inside is not None and inside != (0 < z < self.net.zs - 1):
                return
            for i in range(self.net.zs):
                for p in range(len(self.pieces)):
                    if chosen(i, p, self.hops(z, i)):
                        self.move(z, i, p)
        at_each(self.net, go)

    def finish(self):
        for i in range(self.net.zs - 1):
            for p, piece in enumerate(self.pieces):
                await_copy(self.net, piece[1].at[i], self.sems, (i, p), (i, p))


def drain(copies):
    for copy in copies:
        copy.wait_send()


def by_rows(count, step, body):
    def run(i, carry):
        body(pl.ds(pl.multiple_of(i * step, step), step))
        return carry
    lax.fori_loop(0, count // step, run, 0)


def named(tree):
    return Names(**{k: named(v) if isinstance(v, dict) else v for k, v in tree.items()})


def step_body(zs, tree, inverse, *refs):
    r = Names(**jax.tree.unflatten(tree, refs[13:]))
    for key, value in vars(r).items():
        if isinstance(value, dict):
            setattr(r, key, named(value))
    (queries, keys, values, out_grad, w_gate, w_up, w_down) = refs[:7]
    (d_queries, d_keys, d_values, d_gate, d_up, d_down) = refs[7:13]
    toks, width = queries.shape
    half = width // 2
    every = 2 * toks
    rows = width // (4 * zs)
    zrows = 4 * rows
    net = Net(zs, rows, width + half)
    c = net.c
    mine, theirs = block(c, toks), block(1 - c, toks)
    gl, ul, dl = pl.ds(0, half), pl.ds(half, half), pl.ds(width, half)
    wide = pl.ds(0, width)
    hid = block(c, half)

    token_at = lambda yx, p: (block(2 * (2 * yx[0] + yx[1]) + c, toks), block(p, half))
    spot = block(2 * net.g + c, toks)
    loads = Names()
    loads.k, loads.a, loads.b, loads.c, loads.v, loads.q, loads.o = [
        pltpu.make_async_copy(src, dst, r.ld.at[i]) for i, (src, dst) in enumerate((
            (keys, r.kf), (w_gate.at[:, hid], r.wab.at[:, gl]), (w_up.at[:, hid], r.wab.at[:, ul]),
            (w_down.at[hid, :], r.wc), (values, r.vf), (queries, r.qa.at[spot, :]),
            (out_grad, r.oa.at[spot, :])))]
    for load in vars(loads).values():
        load.start()
    net.greet()
    tsem = r.tsem
    done = []

    def twin(src, dst, k):
        copy = send(src, dst, tsem, k, net.twin)
        done.append(copy)
        return copy

    xb, gu, ab, eb = r.xb, r.gu, r.ab, r.eb
    loads.k.wait()
    xb[mine, :] = r.kf[...].astype(BF)
    keys_in = twin(xb.at[mine, :], xb.at[mine, :], 0)
    qa, oa = r.qa, r.oa
    loads.q.wait()
    loads.o.wait()
    for ref, sems in ((qa, r.qsem), (oa, r.osem)):
        for p in range(2):
            plane_own(net, ref, token_at, 0, p, 0, sems)
    loads.a.wait()
    loads.b.wait()
    r.abb[...] = r.wab[...].astype(BF)
    loads.c.wait()
    r.cb[...] = r.wc[...].astype(BF)
    keys_in.wait_recv()
    gu[...] = dot(xb[...], r.abb[...])

    def active_rows(at):
        g, u = gu[at, gl], gu[at, ul]
        ab[at, :] = (g * jax.nn.sigmoid(g) * u).astype(BF)
    by_rows(every, 32, active_rows)

    loads.v.wait()
    ep, er = r.ep, r.er
    ep[mine, :] = dot(ab[mine, :], r.cb[...]) - r.vf[...]
    e_out = [twin(ep.at[mine, :], er.at[mine, :], 3)]
    ep[theirs, :] = dot(ab[theirs, :], r.cb[...])
    e_out.append(twin(ep.at[theirs, :], er.at[theirs, :], 4))
    for copy, at in zip(e_out, (theirs, mine)):
        copy.wait_recv()
        eb[at, :] = (ep[at, :] + er[at, :]).astype(BF)
    da, dgu = r.da, r.dgu
    da[...] = dot_nt(eb[...], r.cb[...])

    def d_rows(at):
        g, u, d = gu[at, gl], gu[at, ul], da[at, :]
        sig = jax.nn.sigmoid(g)
        dgu[at, ul] = (d * g * sig).astype(BF)
        dgu[at, gl] = (d * u * sig * (1.0 + g * (1.0 - sig))).astype(BF)
    by_rows(every, 32, d_rows)
    r.dguT[...] = dgu[...].T
    r.eT[...] = eb[...].T

    pay = r.pay0

    outer = net.lanes[0].start
    inner = pl.ds(outer, width - outer)

    def key_side():
        pay[:, :outer] = dot(r.dguT[...], xb[:, :outer]).astype(BF)

    def key_block(zb, i):
        at = block(zb, zrows)
        pay[at, inner] = dot(r.dguT[at, :], xb[:, inner]).astype(BF)
        pay[at, dl] = dot(r.eT[at, :], ab[...]).astype(BF)

    def turn_weights():
        r.wabt[...] = r.wab[...].T
        r.wct[...] = r.wc[...].T

    def to_twin(ref, k):
        return [twin(ref.at[block(2 * g + c, toks), :], ref.at[block(2 * g + c, toks), :], k + g)
                for g in range(4)]

    def select_lanes():
        h = lax.broadcasted_iota(jnp.int32, (half, 512), 0)
        lane = lax.broadcasted_iota(jnp.int32, (half, 512), 1)
        g, l = lane // 128, lane % 128
        hit = (h == (half // 2) * (l // rows) + rows * g + l % rows) & (l < 2 * rows)
        r.sel[...] = jnp.where(hit, 1.0, 0.0).astype(BF)
        r.wgu[...] = jnp.zeros((256, width), BF)

    def turn_keys():
        r.xT[...] = xb[...].T

    grad = r.grad
    rs0 = reduce_scatter(net, pay, r.rs0, grad, key_block, key_side,
                         {0: turn_keys, 2: select_lanes, 3: turn_weights})

    own = net.chunk(net.z, (net.y, net.x))
    squares = jnp.sum(grad[:, dl] * grad[:, dl], axis=1, keepdims=True)
    r.sq[0] = jnp.broadcast_to(squares, (rows, 128))
    norm_in = twin(r.sq.at[0], r.sq.at[1], 5)
    scale_of = lambda sq: jnp.sqrt(sq / width + EPSILON)
    scale = r.scale

    gz, rz = r.gz, r.rz
    line = r.line
    gz_at = lambda zb, p: gz.at[pl.ds(rows * zb, rows), pl.ds(half * p, half)]
    rz_at = lambda zb: rz.at[pl.ds(zrows * zb, zrows), :]
    g = grad[:, wide]
    sc = scale_of(jnp.sum(g * g, axis=1, keepdims=True))
    scale[0] = jnp.broadcast_to(sc, (rows, 128))
    gz[block(net.z, rows), :] = (r.wabt[own, :] - STEP_SIZE * g / sc).astype(BF)
    at_each(net, lambda z: [pass_on(net, z, z, p, gz_at(z, p), line) for p in range(2)])
    norm_in.wait_recv()
    sc = scale_of((r.sq[0] + r.sq[1])[:, :1])
    scale[1] = jnp.broadcast_to(sc, (rows, 128))
    down = (r.wct[own, :] - STEP_SIZE * grad[:, dl] / sc).astype(BF)
    r.dsl[...] = dot(down, r.sel[...]).astype(BF)
    ssem = r.ssem
    near = [net.flip(0), net.flip(1), net.flip(0, 1)]
    near_at = [net.side(0), net.side(1), net.across()]
    lane_of = lambda yx: block(2 * yx[0] + yx[1], 128)
    rz[own, :] = r.dsl[:, lane_of((net.y, net.x))]
    slices = [send(r.dsl.at[:, lane_of(yx)], rz.at[own, :], ssem, k, peer)
              for k, (yx, peer) in enumerate(zip(near, near_at))]
    for ref, sems in ((qa, r.qsem), (oa, r.osem)):
        for p in range(2):
            plane_relay(net, ref, token_at, 0, p, sems)
        for p in range(2):
            plane_own(net, ref, token_at, 0, p, 1, sems)
    xsem = r.xsem

    def direct(z):
        for other in range(zs):
            if other != z:
                send(rz_at(z), rz_at(z), xsem, (other,), net.at_z(other), (z,))
    def gather_line(first, last):
        def go(z):
            for zb in spread_order(zs, z)[first:last]:
                for p in range(2):
                    await_copy(net, gz_at(zb, p), line.z, (zb, p, 0))
                    pass_on(net, z, zb, p, gz_at(zb, p), line)
            if last == zs:
                for zb in spread_order(zs, z)[1:]:
                    await_copy(net, rz_at(zb), xsem, (zb,))
        at_each(net, go)

    gather_line(1, 2)
    for copy in slices:
        copy.wait_recv()
    at_each(net, direct)
    gather_line(2, 3)
    for p in range(2):
        plane_rest(net, qa, token_at, 0, p, r.qsem)
    q_in = to_twin(qa, 20)
    gather_line(3, zs)

    wgu, hgu, dact, hd, hact = r.wgu, r.hgu, r.dact, r.hd, r.hact
    wgu[:2 * rows, :] = gz[:2 * rows, :]
    wgu[128:128 + 2 * rows, :] = gz[2 * rows:, :]
    for copy in q_in:
        copy.wait_recv()
    for p in range(2):
        plane_rest(net, oa, token_at, 0, p, r.osem)
    o_in = to_twin(oa, 24)
    hgu[...] = dot_nt(wgu[...], qa[...])
    r.rzT[...] = rz[...].T
    for copy in o_in:
        copy.wait_recv()
    dact[...] = dot_nt(r.rzT[...], oa[...])

    def query_rows(at):
        up = pl.ds(pl.multiple_of(at.start + 128, 16), 16)
        g, u, d = hgu[at, :], hgu[up, :], dact[at, :]
        sig = jax.nn.sigmoid(g)
        hact[at, :] = (g * sig * u).astype(BF)
        hd[up, :] = (d * g * sig).astype(BF)
        hd[at, :] = (d * u * sig * (1.0 + g * (1.0 - sig))).astype(BF)
    by_rows(128, 16, query_rows)
    hsum = r.hsum
    hdn8, hgu8 = r.hdn8, r.hgu8
    hdn8[...] = dot(hact[...], oa[...])
    r.pd[...] = hdn8[...].T

    def own_down(value):
        r.dout[...] = value.astype(BF)

    def own_wide(p):
        def store(value):
            hsum[:, half * p:half * (p + 1)] = value
        return store

    def wide_cut(p):
        return lambda zb: hgu8[pl.ds(rows * zb + (128 - 2 * rows) * (zb // 2), rows),
                               half * p:half * (p + 1)]

    pieces = (
        (lambda zb: r.pd[zrows * zb:zrows * (zb + 1), :], r.ldo, r.ldi, own_down),
        (wide_cut(0), r.lgo0, r.lgi0, own_wide(0)),
        (wide_cut(1), r.lgo1, r.lgi1, own_wide(1)),
    )
    summing = LineSum(net, pieces, r.lsem)
    summing.run(lambda i, p, hops: hops == 0 and i == 0 and p == 0)
    hgu8[...] = dot(hd[...], qa[...])
    summing.run(lambda i, p, hops: hops == 0 and i + p > 0)
    r.hdT[...] = hd[...].T
    hd = r.hdT
    dqs, dqm, dqt = r.dqs, r.dqm, r.dqt
    dq_in = []
    for g in range(4):
        at = block(g, toks)
        dqs[at, :] = dot(hd[block(2 * g + 1 - c, toks), :], wgu[...]).astype(BF)
        dq_in.append(twin(dqs.at[at, :], dqt.at[at, :], 28 + g))
    for g in range(4):
        at = block(g, toks)
        mid = dot(hd[block(2 * g + c, toks), :], wgu[...])
        dq_in[g].wait_recv()
        dqm[at, :] = (mid + dqt[at, :].astype(F32)).astype(BF)
    query_sum = PlaneSum(
        net, dqm, lambda yx, p: (block(2 * yx[0] + yx[1], toks), block(p, half)), r.dqs3)
    query_sum.first()
    summing.run(lambda i, p, hops: hops == 1)
    summing.run(lambda i, p, hops: 1 < hops < zs)
    query_sum.second()
    summing.run(lambda i, p, hops: hops == zs and p == 0)
    dout, din = r.dout, r.din
    mine_at = lambda yx: block(2 * yx[0] + yx[1], rows)
    usem = r.usem
    units = [send(dout.at[mine_at(yx), :], din.at[:, lane_of((net.y, net.x))], usem, k, peer)
             for k, (yx, peer) in enumerate(zip(near, near_at))]
    din[:, lane_of((net.y, net.x))] = dout[mine_at((net.y, net.x)), :]
    summing.run(lambda i, p, hops: hops == zs and p > 0)
    back = r.full1

    def turned(h, g, sc, prod):
        return (-STEP_SIZE * h / sc - g * prod / (width * sc * sc * sc)).astype(BF)

    def wide_back():
        h, g = hsum[:, wide], grad[:, wide]
        prod = jnp.sum(-STEP_SIZE * h * g, axis=1, keepdims=True)
        back[own, wide] = turned(h, g, scale[0][:, :1], prod)

    def down_back():
        for copy in units:
            copy.wait_recv()
        hsum[:, dl] = dot_nt(din[...], r.sel[...])
        product = jnp.sum(-STEP_SIZE * hsum[:, dl] * grad[:, dl], axis=1, keepdims=True)
        r.sq[2] = jnp.broadcast_to(product, (rows, 128))
        twin(r.sq.at[2], r.sq.at[3], 7).wait_recv()
        prod = (r.sq[2] + r.sq[3])[:, :1]
        back[own, dl] = turned(hsum[:, dl], grad[:, dl], scale[1][:, :1], prod)

    ag1 = all_gather(net, back, r.ag1, (wide_back, down_back))

    def query_done(p, value):
        d_queries[:, p * half:(p + 1) * half] = value.astype(BF)
    query_sum.last(query_done)

    pq, tb, ec = r.pq, r.tb, r.ec
    pq[...] = dot_nt(xb[...], back[:, wide])

    def t_rows(at):
        g, u = gu[at, gl], gu[at, ul]
        p, q = pq[at, gl], pq[at, ul]
        sig = jax.nn.sigmoid(g)
        tb[at, :] = (q * g * sig + p * u * sig * (1.0 + g * (1.0 - sig))).astype(BF)
    by_rows(every, 32, t_rows)
    sp, sr, sb = r.sp, r.sr, r.sb
    second_out = []
    for k, at in enumerate((mine, theirs)):
        sp[at, :] = dot_nt(ab[at, :], back[:, dl]) + dot(tb[at, :], r.cb[...])
        second_out.append(twin(sp.at[at, :], sr.at[at, :], 8 + k))
    ec[...] = dot(eb[...], back[:, dl])
    placed, hp, hdn = r.placed, r.hp, r.hdn
    placed[...] = jnp.zeros_like(placed)
    hdn[...] = jnp.zeros_like(hdn)
    for k in range(2):
        to = pl.ds(pl.multiple_of((half // 2) * k + rows * net.g, rows), rows)
        to_up = pl.ds(pl.multiple_of(half + (half // 2) * k + rows * net.g, rows), rows)
        placed[to, :] = hgu8[k * rows:(k + 1) * rows, :]
        placed[to_up, :] = hgu8[128 + k * rows:128 + (k + 1) * rows, :]
        hdn[to, :] = hdn8[k * rows:(k + 1) * rows, :]
    hp[...] = placed[...].T
    r.taT[:, pl.ds(0, every)] = tb[...].T
    r.taT[:, pl.ds(every, every)] = ab[...].T
    for copy, at in zip(second_out, (theirs, mine)):
        copy.wait_recv()
        sb[at, :] = (sp[at, :] + sr[at, :]).astype(BF)
    prow = 2 * rows
    dsw, dloc = r.dsw, r.dloc
    dloc[...] = (r.hdn[...] + dot(r.taT[:, pl.ds(0, every)], eb[...])
                 + dot(r.taT[:, pl.ds(every, every)], sb[...])).astype(BF)
    swaps = []
    for k in range(zs // 2):
        slot = (zs // 2) * c + k
        swaps.append(twin(dloc.at[block(2 * k + 1 - c, prow), :], dsw.at[slot], 10 + k))
        dsw[slot] = dloc[block(2 * k + c, prow), :]
    d_values[...] = -(sp[mine, :] + sr[mine, :])
    ec[...] += dot_nt(sb[...], r.cb[...])
    gub = r.gub

    def pull_rows(at):
        g, u, d = gu[at, gl], gu[at, ul], da[at, :]
        p, q, back_a = pq[at, gl], pq[at, ul], ec[at, :]
        sig = jax.nn.sigmoid(g)
        sneg = 1.0 - sig
        h = g * sig
        slope = sig * (1.0 + g * sneg)
        bend = sig * sneg * (2.0 + g * (1.0 - 2.0 * sig))
        pd = p * d
        gub[at, gl] = (back_a * u * slope + pd * u * bend + q * d * slope).astype(BF)
        gub[at, ul] = (back_a * h + pd * slope).astype(BF)
    by_rows(every, 32, pull_rows)

    pay2 = r.pay2

    def last_side():
        pay2[:, :outer] = (r.hp[:, :outer] + dot(r.xT[...], gub[:, :outer])).astype(BF)

    def last_block(zb, i):
        at = block(zb, zrows)
        pay2[at, inner] = (r.hp[at, inner] + dot(r.xT[at, :], gub[:, inner])).astype(BF)
        if i == 0:
            for copy in swaps:
                copy.wait_recv()
        for y in range(2):
            for x in range(2):
                pay2[block(4 * zb + 2 * y + x, rows), dl] = (
                    dsw[zb, y * rows:(y + 1) * rows, x * half:(x + 1) * half])

    def key_back():
        r.kp[...] = dot(dgu[...], back[:, wide])

    def key_back_second():
        r.kp[...] += dot_nt(gub[...], r.abb[...])
        r.kin = twin(r.kp.at[theirs, :], r.kr, 10 + zs // 2)

    last = r.last
    rs2 = reduce_scatter(net, pay2, r.rs2, last, last_block, last_side,
                         {0: key_back, 1: key_back_second})
    fin = r.fin
    fin[block(net.g, rows), :] = last[...].astype(BF)
    final = [send(fin.at[block(net.g, rows), :], fin.at[block(net.g, rows), :], r.fsem, k, peer)
             for k, peer in ((2, near_at[2]), (0, near_at[0]), (1, near_at[1]))]
    r.kin.wait_recv()
    d_keys[...] = r.kp[mine, :] + r.kr[...]
    for copy in final:
        copy.wait_recv()
    swap = twin(fin.at[block(1 - c, prow), wide], r.tw, 11 + zs // 2)
    lanes = block(c, half)
    others = block(1 - c, half)
    d_gate[:, lanes] = fin[block(c, prow), gl].astype(F32) * inverse
    d_up[:, lanes] = fin[block(c, prow), ul].astype(F32) * inverse
    for y in range(2):
        for x in range(2):
            g = 2 * y + x
            d_down[y * rows:(y + 1) * rows, x * half:(x + 1) * half] = (
                fin[g * rows:(g + 1) * rows, width:].astype(F32) * inverse)
    swap.wait_recv()
    d_gate[:, others] = r.tw[:, :half].astype(F32) * inverse
    d_up[:, others] = r.tw[:, half:].astype(F32) * inverse
    drain(done + slices + units + final)
    query_sum.finish()
    for finish in (rs0, ag1, rs2, summing.finish):
        finish()
    for p in range(2):
        plane_drain(net, qa, token_at, 0, p, r.qsem)
        plane_drain(net, oa, token_at, 0, p, r.osem)

    def drain_line(z):
        for zb in range(zs):
            for p in range(2):
                pass_drain(net, z, zb, p, gz_at(zb, p), line)
            if zb != z:
                await_copy(net, rz_at(z), xsem, (zb,), (zb,))
    at_each(net, drain_line)


def hand_over(*refs):
    for src, dst in zip(refs[:6], refs[6:]):
        dst[...] = src[...]


def fused_step(queries, key_tokens, values, out_grad, w_gate, w_up, w_down, zs, inverse):
    toks, width = queries.shape
    half, every, rows = width // 2, 2 * toks, width // (4 * zs)
    plane = 4 * every
    total = width + half
    side, main = lane_parts(total)
    unit = side[0].size
    f32 = lambda *shape: VM(shape, F32)
    bf = lambda *shape: VM(shape, BF)
    sems = lambda *shape: (DMA(shape), DMA(shape))
    both = lambda *shape: tuple(VM(shape + (part.size,), BF) for part in main)
    summed = dict(
        r1=both(zs, 2, rows), r2=both(zs, rows), zb=both(zs - 1, rows), zr=both(zs + 1, rows),
        s1=sems(zs, 2, 2), s2=sems(zs, 2), s3=sems(zs + 1, 2), pb=bf(4 * rows, 2 * unit),
        lo=(bf(zs - 1, 4 * rows, unit),) * 2, li=(bf(zs + 1, 4 * rows, unit),) * 2,
        ls=sems(zs + 1, 2),
        ps=dict(r1=bf(2, 2, rows, unit), r2=bf(2, rows, unit), s1=sems(2, 2), s2=sems(2)))
    spread = lambda depth: dict(
        z=sems(depth, 2, 2), o=sems(depth, 2, 2), f=sems(depth, 2))
    scratch = dict(
        kf=f32(toks, width), vf=f32(toks, width), wab=f32(width, width), wc=f32(half, width),
        wabt=f32(width, width), wct=f32(width, half), gu=f32(every, width), ep=f32(every, width),
        er=f32(every, width), da=f32(every, half), grad=f32(rows, total), hsum=f32(rows, total),
        last=f32(rows, total), sq=f32(4, rows, 128), scale=f32(2, rows, 128),
        hgu=f32(256, plane), dact=f32(128, plane), hdn8=f32(128, width), hgu8=f32(256, width),
        pd=f32(width, 128), placed=f32(width, width), hp=f32(width, width), hdn=f32(half, width),
        pq=f32(every, width), ec=f32(every, half), sp=f32(every, width), sr=f32(every, width),
        kp=f32(every, width), kr=f32(toks, width),
        xb=bf(every, width), qa=bf(plane, width), oa=bf(plane, width), abb=bf(width, width),
        cb=bf(half, width), ab=bf(every, half), eb=bf(every, width), dgu=bf(every, width),
        dguT=bf(width, every), eT=bf(width, every), xT=bf(width, every), hd=bf(256, plane),
        hdT=bf(plane, 256), hact=bf(128, plane), rzT=bf(128, width), tb=bf(every, half),
        sel=bf(half, 512), wgu=bf(256, width), gz=bf(zs * rows, width), rz=bf(width, 128),
        dsl=bf(rows, 512), dout=bf(4 * rows, 128), din=bf(rows, 512), dqs=bf(4 * toks, width),
        dqm=bf(4 * toks, width), dqt=bf(4 * toks, width),
        ldo=bf(zs - 1, 4 * rows, 128), ldi=bf(zs + 1, 4 * rows, 128),
        lgo0=bf(zs - 1, rows, half), lgi0=bf(zs + 1, rows, half),
        lgo1=bf(zs - 1, rows, half), lgi1=bf(zs + 1, rows, half),
        sb=bf(every, width), taT=bf(half, 2 * every), gub=bf(every, width), dloc=bf(half, width),
        dsw=bf(zs, 2 * rows, width), pay0=bf(width, total), pay2=bf(width, total),
        full1=bf(width, total), fin=bf(4 * rows, total), tw=bf(2 * rows, width),
        rs0=summed, rs2=summed, ag1=spread(zs), fsem=sems(3), qsem=spread(1), osem=spread(1),
        line=spread(zs), lsem=sems(zs + 1, 3), xsem=sems(zs), ssem=sems(3), usem=sems(3),
        dqs3=dict(r1=bf(2, 2, toks, half), r2=bf(2, toks, half), s1=sems(2, 2), s2=sems(2)),
        tsem=sems(32), ld=DMA((7,)))
    shapes, tree = jax.tree.flatten(scratch)
    token = jax.ShapeDtypeStruct((toks, width), F32)
    weight = jax.ShapeDtypeStruct((2 * rows, width), F32)
    results = pl.pallas_call(
        functools.partial(step_body, zs, tree, inverse),
        out_shape=(jax.ShapeDtypeStruct((toks, width), BF), token, token, weight, weight, weight),
        in_specs=[pl.BlockSpec(memory_space=pltpu.HBM)] * 7,
        out_specs=[pl.BlockSpec(memory_space=VM)] * 6,
        scratch_shapes=shapes,
        compiler_params=pltpu.CompilerParams(
            collective_id=0, has_side_effects=True, vmem_limit_bytes=52 * 1024 * 1024),
    )(*(pltpu.with_memory_space_constraint(x, pltpu.HBM) for x in (
        queries, key_tokens, values, out_grad, w_gate, w_up, w_down)))
    return pl.pallas_call(
        hand_over,
        out_shape=tuple(jax.ShapeDtypeStruct(item.shape, item.dtype) for item in results),
        in_specs=[pl.BlockSpec(memory_space=VM)] * 6,
        out_specs=[pl.BlockSpec(memory_space=VM)] * 6,
        compiler_params=pltpu.CompilerParams(vmem_limit_bytes=8 * 1024 * 1024),
    )(*results)


def matmul(left, right):
    return dot(left.astype(BF), right.astype(BF))


def key_grad(w_gate, w_up, w_down, key_rows, value_rows):
    hidden_gate = matmul(key_rows, w_gate)
    hidden_up = matmul(key_rows, w_up)
    sig = jax.nn.sigmoid(hidden_gate)
    active = hidden_gate * sig * hidden_up
    error = matmul(active, w_down) - value_rows
    d_active = matmul(error, w_down.T)
    d_hup = d_active * hidden_gate * sig
    d_hgate = d_active * hidden_up * sig * (1.0 + hidden_gate * (1.0 - sig))
    return (matmul(d_hgate.T, key_rows), matmul(d_hup.T, key_rows), matmul(error.T, active))


def query_grad(fast_t, query_rows, grad_rows):
    gate_t, up_t, down_t = fast_t
    hidden_gate = dot(query_rows, gate_t.T)
    hidden_up = dot(query_rows, up_t.T)
    sig = jax.nn.sigmoid(hidden_gate)
    active = (hidden_gate * sig * hidden_up).astype(BF)
    d_active = dot(grad_rows, down_t)
    d_hup = (d_active * hidden_gate * sig).astype(BF)
    d_hgate = (d_active * hidden_up * sig * (1.0 + hidden_gate * (1.0 - sig))).astype(BF)
    d_rows = (dot(d_hgate, gate_t) + dot(d_hup, up_t)).astype(BF)
    return (d_rows, active, d_hgate, d_hup)


def general_step(queries, key_tokens, values, out_grad, w_gate, w_up, w_down, inverse):
    gs, toks = lax.axis_size("grp"), lax.axis_size("tok")
    full_width = w_gate.shape[0]
    rows = 3 * full_width // (gs * toks)
    me = lax.axis_index("tok") * gs + lax.axis_index("grp")

    def reduce_units(x):
        y = x.reshape(toks, gs * rows, full_width)
        y = lax.psum_scatter(y, "tok", scatter_dimension=0, tiled=True)[0]
        return lax.psum_scatter(y.reshape(gs, rows, full_width), "grp", scatter_dimension=0, tiled=True)[0]

    def gather_units(y):
        full = lax.all_gather(lax.all_gather(y, "grp"), "tok").reshape(3, full_width, full_width)
        return full[0], full[1], full[2]

    local_grad, pullback = jax.vjp(key_grad, w_gate, w_up, w_down, key_tokens, values)
    grad = reduce_units(jnp.stack(local_grad))
    scale = jnp.sqrt(jnp.sum(grad * grad, axis=1, keepdims=True) / full_width + EPSILON)
    weights = jnp.concatenate((w_gate, w_up, w_down), axis=1)
    mine = lax.dynamic_slice_in_dim(weights, me * rows, rows, 1).T
    fast_t = gather_units((mine - STEP_SIZE * grad / scale).astype(BF))
    d_queries, active, d_hgate, d_hup = query_grad(fast_t, queries, out_grad)
    query_part = reduce_units(
        jnp.stack((dot(d_hgate.T, queries), dot(d_hup.T, queries), dot(out_grad.T, active))))
    product = jnp.sum(-STEP_SIZE * query_part * grad, axis=1, keepdims=True)
    cot = (
        -STEP_SIZE * query_part / scale - grad * product / (full_width * scale * scale * scale)
    ).astype(BF)
    second = pullback(tuple(item.astype(F32) for item in gather_units(cot)))
    plain = (dot(queries.T, d_hgate), dot(queries.T, d_hup), dot(active.T, out_grad))
    combined = jnp.stack(tuple(left + right for left, right in zip(plain, second[:3])))
    combined = combined.reshape(3, toks, full_width // toks, full_width).transpose(1, 0, 2, 3)
    summed = lax.all_gather(reduce_units(combined).astype(BF), "grp").astype(F32) * inverse
    summed = summed.reshape(3, full_width // toks, full_width)
    return (d_queries, second[3], second[4], summed[0], summed[1], summed[2])


def on_device(*arrays):
    gs, toks = lax.axis_size("grp"), lax.axis_size("tok")
    tokens, width = arrays[0].shape
    inverse = 1.0 / (tokens * gs * toks)
    zs = toks // 2
    fits = gs == 4 and toks % 4 == 0 and zs <= 4
    if fits and width % (64 * zs) == 0 and 2 * width <= 512 * zs and width % 256 == 0 and tokens % 128 == 0:
        return fused_step(*arrays, zs, inverse)
    return general_step(*arrays, inverse)


def solution(mesh):
    token = P(("grp", "tok"), None)
    return jax.shard_map(
        on_device,
        mesh=mesh,
        in_specs=(token, token, token, token, P(), P(), P()),
        out_specs=(token, token, token, P("tok", None), P("tok", None), P("tok", None)),
        check_vma=False,
    )
```

```python
import functools
from types import SimpleNamespace as Names

import jax
import jax.numpy as jnp
from jax import lax
from jax.experimental import pallas as pl
from jax.experimental.pallas import tpu as pltpu
from jax.sharding import PartitionSpec as P

STEP_SIZE = 0.02
EPSILON = 1e-06
MESH = pl.DeviceIdType.MESH
BF = jnp.bfloat16
F32 = jnp.float32
VM = pltpu.VMEM
DMA = pltpu.SemaphoreType.DMA


def dot(left, right):
    return jnp.dot(left, right, preferred_element_type=F32)


def dot_nt(left, right):
    return lax.dot_general(left, right, (((1,), (1,)), ((), ())), preferred_element_type=F32)


def block(index, size):
    return pl.ds(pl.multiple_of(index * size, size), size)


def lane_parts(width):
    unit = 128 * max(1, width // 1152)
    cut = width - 128 * ((width // 128 - 2 * (unit // 128)) // 2)
    return ((pl.ds(0, unit), pl.ds(unit, unit)),
            (pl.ds(2 * unit, cut - 2 * unit), pl.ds(cut, width - cut)))


class Net:
    def __init__(self, zs, rows, width):
        g, t = lax.axis_index("grp"), lax.axis_index("tok")
        self.zs, self.rows = zs, rows
        self.g, self.z, self.c = g, t // 2, lax.rem(t, 2)
        self.y, self.x = g // 2, lax.rem(g, 2)
        self.t = t
        self.outer, self.lanes = lane_parts(width)
        cut = 128 * ((width // 128 + 1) // 2)
        self.parts = (pl.ds(0, cut), pl.ds(cut, width - cut))
        self.twin = (g, 2 * self.z + 1 - self.c)

    def flip(self, *directions):
        y, x = self.y, self.x
        for a in directions:
            x = x + (1 - a) * (1 - 2 * x)
            y = y + a * (1 - 2 * y)
        return y, x

    def turn(self, n):
        return lax.rem(n + self.c, 2)

    def side(self, a):
        y, x = self.flip(a)
        return (2 * y + x, self.t)

    def across(self):
        y, x = self.flip(0, 1)
        return (2 * y + x, self.t)

    def at_z(self, z):
        return (self.g, 2 * z + self.c)

    def pick(self, table):
        value = table[0]
        for z in range(1, self.zs):
            value = jnp.where(self.z == z, table[z], value)
        return value

    def chunk(self, zb, yx):
        return block(4 * zb + 2 * yx[0] + yx[1], self.rows)

    def greet(self):
        barrier = pltpu.get_barrier_semaphore()
        peers = [self.twin, self.side(0), self.side(1), self.across()]
        for d in range(1, self.zs):
            peers.append(self.at_z(lax.rem(self.z + d, self.zs)))
        for peer in peers:
            pl.semaphore_signal(barrier, inc=1, device_id=peer, device_id_type=MESH)
        pl.semaphore_wait(barrier, len(peers))


def send(src, dst, sems, at, peer, there=None):
    copy = pltpu.make_async_remote_copy(
        src_ref=src, dst_ref=dst, send_sem=sems[0].at[at],
        recv_sem=sems[1].at[at if there is None else there],
        device_id=peer, device_id_type=MESH,
    )
    copy.start()
    return copy


def await_copy(net, ref, sems, at, there=None):
    copy = pltpu.make_async_remote_copy(
        src_ref=ref, dst_ref=ref, send_sem=sems[0].at[at if there is None else there],
        recv_sem=sems[1].at[at], device_id=net.twin, device_id_type=MESH,
    )
    if there is None:
        copy.wait_recv()
    else:
        copy.wait_send()


def sum_order(zs, z):
    def key(zb):
        hops = z if zb > z else zs - 1 - z
        return (zb == z, hops, -abs(zb - z))
    return sorted(range(zs), key=key)


def spread_order(zs, z):
    return sorted(range(zs), key=lambda zb: (abs(zb - z), (zb > z) == (2 * z < zs)))


def reduce_scatter(net, pay, s, total, produce, produce_side, fillers, ready=None):
    zs = net.zs
    orders = [sum_order(zs, z) for z in range(zs)]
    blocks = [net.pick([orders[z][i] for z in range(zs)]) for i in range(zs)]
    first, second = {}, {}
    unit = s.pb.shape[-1] // 2

    def line_piece(p):
        def cut(zb):
            return pay[pl.ds(4 * net.rows * zb, 4 * net.rows), net.outer[p]]

        def own(value):
            s.pb[:, unit * p:unit * (p + 1)] = value.astype(BF)
        return cut, s.lo[p], s.li[p], own

    line = LineSum(net, (line_piece(0), line_piece(1)), s.ls)
    plane = PlaneSum(net, s.pb, lambda yx, p: (
        block(2 * yx[0] + yx[1], net.rows), pl.ds(unit * p, unit)), s.ps)

    def when_inside(inside, body):
        inner = (net.z > 0) & (net.z < zs - 1)
        pl.when(inner if inside else jnp.logical_not(inner))(body)

    def start_first(i, k):
        for p in (1, 0):
            a = net.turn(p + i)
            yx = net.flip(a, 1 - a) if k == 0 else net.flip(a)
            first[i, p, k] = send(
                pay.at[net.chunk(blocks[i], yx), net.lanes[p]], s.r1[p].at[i, k],
                s.s1, (i, p, k), net.side(a))

    def start_second(i):
        for p in (1, 0):
            a = net.turn(p + i)
            first[i, p, 0].wait_recv()
            at = (net.chunk(blocks[i], net.flip(1 - a)), net.lanes[p])
            pay[at] = (pay[at].astype(F32) + s.r1[p][i, 0].astype(F32)).astype(BF)
            second[i, p] = send(pay.at[at], s.r2[p].at[i], s.s2, (i, p), net.side(1 - a))

    def along(z, i):
        zb = orders[z][i]
        for p in (1, 0):
            first[i, p, 1].wait_recv()
            second[i, p].wait_recv()
            at = (net.chunk(zb, (net.y, net.x)), net.lanes[p])
            value = (pay[at].astype(F32) + s.r1[p][i, 1].astype(F32)
                     + s.r2[p][i].astype(F32))
            slots = []
            if zb >= z and z > 0:
                slots.append(i)
            if zb <= z and z < zs - 1:
                slots.append(i if zb < z else zs)
            for slot in slots:
                await_copy(net, s.zr[p].at[slot], s.s3, (slot, p))
                value = value + s.zr[p][slot].astype(F32)
            if zb == z:
                total[:, net.lanes[p]] = value
                if p == 1 and ready is not None:
                    ready()
            else:
                s.zb[p][i] = value.astype(BF)
                nxt = z + 1 if zb > z else z - 1
                slot = orders[nxt].index(zb) if nxt != zb or zb > z else zs
                send(s.zb[p].at[i], s.zr[p].at[slot], s.s3, (i, p), net.at_z(nxt),
                     (slot, p))

    last = 0
    steps = [{} for _ in range(zs)]
    for z in range(zs):
        for i, zb in enumerate(orders[z]):
            hops = 0 if zb == z else z if zb > z else zs - 1 - z
            when = zs + 2 if zb == z else i + 2 + min(hops, 1)
            steps[z].setdefault(when, []).append(i)
            last = max(last, when)
    for i in range(last + 1):
        if i < zs:
            produce(blocks[i], i)
            start_first(i, 0)
        if i == 0:
            produce_side()
            line.run(lambda n, p, hops: hops == 0)
        if 1 <= i <= zs:
            start_second(i - 1)
        if i < zs:
            start_first(i, 1)
        line.run(lambda n, p, hops: 0 < hops < zs and max(n + 1, 2) == i)
        for inside in (True, False):
            if i == (zs - 1 if inside else zs):
                line.run(lambda n, p, hops: hops == zs, inside)
                when_inside(inside, plane.first)
        for z in range(zs):
            if i in steps[z]:
                @pl.when(net.z == z)
                def _():
                    for k in steps[z][i]:
                        along(z, k)
        for inside in (True, False):
            if i == (zs if inside else zs + 1):
                when_inside(inside, plane.second)
        if i in fillers:
            fillers[i]()
    def plane_done(p, value):
        total[:, net.outer[p]] = value
    plane.last(plane_done)

    def finish():
        drain([*first.values(), *second.values()])
        plane.finish()
        line.finish()
        for i in range(zs - 1):
            for p in range(2):
                await_copy(net, s.zb[p].at[i], s.s3, (i, p), (i, p))
    return finish


def plane_own(net, ref, at, i, p, k, s):
    ref = ref.at[at((net.y, net.x), p)]
    return send(ref, ref, s.o, (i, p, k), net.side(net.turn(p + i + k)))


def plane_relay(net, ref, at, i, p, s):
    a = net.turn(p + i)
    ref = ref.at[at(net.flip(a), p)]
    await_copy(net, ref, s.o, (i, p, 0))
    return send(ref, ref, s.f, (i, p), net.side(1 - a))


def plane_rest(net, ref, at, i, p, s):
    a = net.turn(p + i)
    await_copy(net, ref.at[at(net.flip(1 - a), p)], s.o, (i, p, 1))
    await_copy(net, ref.at[at(net.flip(0, 1), p)], s.f, (i, p))


def plane_drain(net, ref, at, i, p, s):
    ref = ref.at[at((net.y, net.x), p)]
    for k in range(2):
        await_copy(net, ref, s.o, (i, p, k), (i, p, k))
    await_copy(net, ref, s.f, (i, p), (i, p))


def at_each(net, body):
    for z in range(net.zs):
        @pl.when(net.z == z)
        def _():
            body(z)


def onward(zs, z, zb):
    return [(k, other) for k, other in enumerate((z - 1, z + 1))
            if 0 <= other < zs and (zb == z or (zb > z) == (other < z))]


def pass_on(net, z, zb, p, ref, s):
    for k, other in onward(net.zs, z, zb):
        send(ref, ref, s.z, (zb, p, k), net.at_z(other), (zb, p, 0))


def pass_drain(net, z, zb, p, ref, s):
    for k, other in onward(net.zs, z, zb):
        await_copy(net, ref, s.z, (zb, p, 0), (zb, p, k))


def all_gather(net, full, s, parts, idle):
    zs = net.zs
    place = lambda zb: lambda yx, p: (net.chunk(zb, yx), net.parts[p])
    mine = lambda zb, p: full.at[place(zb)((net.y, net.x), p)]

    for p in range(2):
        parts[p]()
        at_each(net, lambda z: pass_on(net, z, z, p, mine(z, p), s))
        plane_own(net, full, place(net.z), 0, p, 0, s)
    for p in range(2):
        plane_own(net, full, place(net.z), 0, p, 1, s)

    def rest(z):
        order = spread_order(zs, z)
        for i in range(1, zs):
            for p in range(2):
                await_copy(net, mine(order[i], p), s.z, (order[i], p, 0))
                pass_on(net, z, order[i], p, mine(order[i], p), s)
                plane_own(net, full, place(order[i]), i, p, 0, s)
            for p in range(2):
                plane_relay(net, full, place(order[i - 1]), i - 1, p, s)
            for p in range(2):
                plane_own(net, full, place(order[i]), i, p, 1, s)
        for p in range(2):
            plane_relay(net, full, place(order[zs - 1]), zs - 1, p, s)

    def arrive(z):
        for i, zb in enumerate(spread_order(zs, z)):
            for p in range(2):
                plane_rest(net, full, place(zb), i, p, s)
    at_each(net, rest)
    idle()
    at_each(net, arrive)

    def finish():
        def go(z):
            order = spread_order(zs, z)
            for i in range(zs):
                for p in range(2):
                    pass_drain(net, z, order[i], p, mine(order[i], p), s)
                    plane_drain(net, full, place(order[i]), i, p, s)
        at_each(net, go)
    return finish


class PlaneSum:
    def __init__(self, net, ref, at, s):
        self.net, self.ref, self.at, self.s = net, ref, at, s

    def first(self):
        net, s = self.net, self.s
        for k in range(2):
            for p in range(2):
                yx = net.flip(p, 1 - p) if k == 0 else net.flip(p)
                send(self.ref.at[self.at(yx, p)], s.r1.at[p, k], s.s1, (p, k), net.side(p))

    def second(self):
        net, s = self.net, self.s
        for p in range(2):
            await_copy(net, s.r1.at[p, 0], s.s1, (p, 0))
            at = self.at(net.flip(1 - p), p)
            self.ref[at] = (self.ref[at].astype(F32) + s.r1[p, 0].astype(F32)).astype(BF)
            send(self.ref.at[at], s.r2.at[p], s.s2, (p,), net.side(1 - p))

    def last(self, done):
        net, s = self.net, self.s
        for p in range(2):
            await_copy(net, s.r1.at[p, 1], s.s1, (p, 1))
            await_copy(net, s.r2.at[p], s.s2, (p,))
            value = self.ref[self.at((net.y, net.x), p)].astype(F32)
            done(p, value + s.r1[p, 1].astype(F32) + s.r2[p].astype(F32))

    def finish(self):
        net, s = self.net, self.s
        for p in range(2):
            for k in range(2):
                await_copy(net, s.r1.at[p, k], s.s1, (p, k), (p, k))
            await_copy(net, s.r2.at[p], s.s2, (p,), (p,))


class LineSum:
    def __init__(self, net, pieces, sems):
        self.net, self.pieces, self.sems = net, pieces, sems
        self.orders = [sum_order(net.zs, z) for z in range(net.zs)]

    def hops(self, z, i):
        zb = self.orders[z][i]
        return self.net.zs if zb == z else z if zb > z else self.net.zs - 1 - z

    def move(self, z, i, p):
        net, zs = self.net, self.net.zs
        cut, out, inn, own = self.pieces[p]
        zb = self.orders[z][i]
        value = cut(zb)
        slots = []
        if zb >= z and z > 0:
            slots.append(i)
        if zb <= z and z < zs - 1:
            slots.append(i if zb < z else zs)
        for slot in slots:
            await_copy(net, inn.at[slot], self.sems, (slot, p))
            value = value + inn[slot].astype(F32)
        if zb == z:
            own(value)
            return
        out[i] = value.astype(BF)
        nxt = z + 1 if zb > z else z - 1
        slot = self.orders[nxt].index(zb) if nxt != zb or zb > z else zs
        send(out.at[i], inn.at[slot], self.sems, (i, p), net.at_z(nxt), (slot, p))

    def run(self, chosen, inside=None):
        def go(z):
            if inside is not None and inside != (0 < z < self.net.zs - 1):
                return
            for i in range(self.net.zs):
                for p in range(len(self.pieces)):
                    if chosen(i, p, self.hops(z, i)):
                        self.move(z, i, p)
        at_each(self.net, go)

    def finish(self):
        for i in range(self.net.zs - 1):
            for p, piece in enumerate(self.pieces):
                await_copy(self.net, piece[1].at[i], self.sems, (i, p), (i, p))


def drain(copies):
    for copy in copies:
        copy.wait_send()


def by_rows(count, step, body):
    def run(i, carry):
        body(pl.ds(pl.multiple_of(i * step, step), step))
        return carry
    lax.fori_loop(0, count // step, run, 0)


def named(tree):
    return Names(**{k: named(v) if isinstance(v, dict) else v for k, v in tree.items()})


def step_body(zs, tree, inverse, *refs):
    r = Names(**jax.tree.unflatten(tree, refs[13:]))
    for key, value in vars(r).items():
        if isinstance(value, dict):
            setattr(r, key, named(value))
    (queries, keys, values, out_grad, w_gate, w_up, w_down) = refs[:7]
    (d_queries, d_keys, d_values, d_gate, d_up, d_down) = refs[7:13]
    toks, width = queries.shape
    half = width // 2
    every = 2 * toks
    rows = width // (4 * zs)
    zrows = 4 * rows
    net = Net(zs, rows, width + half)
    c = net.c
    mine, theirs = block(c, toks), block(1 - c, toks)
    gl, ul, dl = pl.ds(0, half), pl.ds(half, half), pl.ds(width, half)
    wide = pl.ds(0, width)
    hid = block(c, half)

    token_at = lambda yx, p: (block(2 * (2 * yx[0] + yx[1]) + c, toks), block(p, half))
    spot = block(2 * net.g + c, toks)
    loads = Names()
    loads.k, loads.a, loads.b, loads.c, loads.v, loads.q, loads.o = [
        pltpu.make_async_copy(src, dst, r.ld.at[i]) for i, (src, dst) in enumerate((
            (keys, r.kf), (w_gate.at[:, hid], r.wab.at[:, gl]), (w_up.at[:, hid], r.wab.at[:, ul]),
            (w_down.at[hid, :], r.wc), (values, r.vf), (queries, r.qa.at[spot, :]),
            (out_grad, r.oa.at[spot, :])))]
    for load in vars(loads).values():
        load.start()
    net.greet()
    tsem = r.tsem
    done = []

    def twin(src, dst, k):
        copy = send(src, dst, tsem, k, net.twin)
        done.append(copy)
        return copy

    xb, gu, ab, eb = r.xb, r.gu, r.ab, r.eb
    loads.k.wait()
    xb[mine, :] = r.kf[...].astype(BF)
    keys_in = twin(xb.at[mine, :], xb.at[mine, :], 0)
    qa, oa = r.qa, r.oa
    loads.q.wait()
    loads.o.wait()
    for ref, sems in ((qa, r.qsem), (oa, r.osem)):
        for p in range(2):
            plane_own(net, ref, token_at, 0, p, 0, sems)
    loads.a.wait()
    loads.b.wait()
    r.abb[...] = r.wab[...].astype(BF)
    loads.c.wait()
    r.cb[...] = r.wc[...].astype(BF)
    keys_in.wait_recv()
    gu[...] = dot(xb[...], r.abb[...])

    def active_rows(at):
        g, u = gu[at, gl], gu[at, ul]
        ab[at, :] = (g * jax.nn.sigmoid(g) * u).astype(BF)
    by_rows(every, 32, active_rows)

    loads.v.wait()
    ep, er = r.ep, r.er
    ep[mine, :] = dot(ab[mine, :], r.cb[...]) - r.vf[...]
    e_out = [twin(ep.at[mine, :], er.at[mine, :], 3)]
    ep[theirs, :] = dot(ab[theirs, :], r.cb[...])
    e_out.append(twin(ep.at[theirs, :], er.at[theirs, :], 4))
    for copy, at in zip(e_out, (theirs, mine)):
        copy.wait_recv()
        eb[at, :] = (ep[at, :] + er[at, :]).astype(BF)
    da, dgu = r.da, r.dgu
    da[...] = dot_nt(eb[...], r.cb[...])

    def d_rows(at):
        g, u, d = gu[at, gl], gu[at, ul], da[at, :]
        sig = jax.nn.sigmoid(g)
        dgu[at, ul] = (d * g * sig).astype(BF)
        dgu[at, gl] = (d * u * sig * (1.0 + g * (1.0 - sig))).astype(BF)
    by_rows(every, 32, d_rows)
    r.dguT[...] = dgu[...].T
    r.eT[...] = eb[...].T

    pay = r.pay0

    outer = net.lanes[0].start
    inner = pl.ds(outer, width - outer)

    def key_side():
        pay[:, :outer] = dot(r.dguT[...], xb[:, :outer]).astype(BF)

    def key_block(zb, i):
        at = block(zb, zrows)
        pay[at, inner] = dot(r.dguT[at, :], xb[:, inner]).astype(BF)
        pay[at, dl] = dot(r.eT[at, :], ab[...]).astype(BF)

    def turn_weights():
        r.wabt[...] = r.wab[...].T
        r.wct[...] = r.wc[...].T

    def to_twin(ref, k):
        return [twin(ref.at[block(2 * g + c, toks), :], ref.at[block(2 * g + c, toks), :], k + g)
                for g in range(4)]

    def select_lanes():
        h = lax.broadcasted_iota(jnp.int32, (half, 512), 0)
        lane = lax.broadcasted_iota(jnp.int32, (half, 512), 1)
        g, l = lane // 128, lane % 128
        hit = (h == (half // 2) * (l // rows) + rows * g + l % rows) & (l < 2 * rows)
        r.sel[...] = jnp.where(hit, 1.0, 0.0).astype(BF)
        r.wgu[...] = jnp.zeros((256, width), BF)

    def turn_keys():
        r.xT[...] = xb[...].T

    def turn_arrays():
        turn_weights()
        select_lanes()
        turn_keys()

    grad = r.grad

    def down_norm():
        squares = jnp.sum(grad[:, dl] * grad[:, dl], axis=1, keepdims=True)
        r.sq[0] = jnp.broadcast_to(squares, (rows, 128))
        send(r.sq.at[0], r.sq.at[1], tsem, 5, net.twin)

    rs0 = reduce_scatter(net, pay, r.rs0, grad, key_block, key_side,
                         {0: turn_arrays},
                         down_norm)

    own = net.chunk(net.z, (net.y, net.x))
    scale_of = lambda sq: jnp.sqrt(sq / width + EPSILON)
    scale = r.scale

    gz, rz = r.gz, r.rz
    line = r.line
    gz_at = lambda zb, p: gz.at[pl.ds(rows * zb, rows), pl.ds(half * p, half)]
    rz_at = lambda zb: rz.at[pl.ds(zrows * zb, zrows), :]
    g = grad[:, wide]
    sc = scale_of(jnp.sum(g * g, axis=1, keepdims=True))
    scale[0] = jnp.broadcast_to(sc, (rows, 128))
    gz[block(net.z, rows), :] = (r.wabt[own, :] - STEP_SIZE * g / sc).astype(BF)
    at_each(net, lambda z: [pass_on(net, z, z, p, gz_at(z, p), line) for p in range(2)])
    await_copy(net, r.sq.at[1], tsem, 5)
    sc = scale_of((r.sq[0] + r.sq[1])[:, :1])
    scale[1] = jnp.broadcast_to(sc, (rows, 128))
    down = (r.wct[own, :] - STEP_SIZE * grad[:, dl] / sc).astype(BF)
    r.dsl[...] = dot(down, r.sel[...]).astype(BF)
    ssem = r.ssem
    near = [net.flip(0), net.flip(1), net.flip(0, 1)]
    near_at = [net.side(0), net.side(1), net.across()]
    lane_of = lambda yx: block(2 * yx[0] + yx[1], 128)
    rz[own, :] = r.dsl[:, lane_of((net.y, net.x))]
    slices = [send(r.dsl.at[:, lane_of(yx)], rz.at[own, :], ssem, k, peer)
              for k, (yx, peer) in enumerate(zip(near, near_at))]
    for ref, sems in ((qa, r.qsem), (oa, r.osem)):
        for p in range(2):
            plane_relay(net, ref, token_at, 0, p, sems)
        for p in range(2):
            plane_own(net, ref, token_at, 0, p, 1, sems)
    xsem = r.xsem

    def direct(z):
        for other in range(zs):
            if other != z:
                send(rz_at(z), rz_at(z), xsem, (other,), net.at_z(other), (z,))
    def gather_line(first, last):
        def go(z):
            for zb in spread_order(zs, z)[first:last]:
                for p in range(2):
                    await_copy(net, gz_at(zb, p), line.z, (zb, p, 0))
                    pass_on(net, z, zb, p, gz_at(zb, p), line)
            if last == zs:
                for zb in spread_order(zs, z)[1:]:
                    await_copy(net, rz_at(zb), xsem, (zb,))
        at_each(net, go)

    gather_line(1, 2)
    for copy in slices:
        copy.wait_recv()
    at_each(net, direct)
    gather_line(2, 3)
    for p in range(2):
        plane_rest(net, qa, token_at, 0, p, r.qsem)
    q_in = to_twin(qa, 20)
    gather_line(3, zs)

    wgu, hgu, dact, hd, hact = r.wgu, r.hgu, r.dact, r.hd, r.hact
    wgu[:2 * rows, :] = gz[:2 * rows, :]
    wgu[128:128 + 2 * rows, :] = gz[2 * rows:, :]
    for copy in q_in:
        copy.wait_recv()
    for p in range(2):
        plane_rest(net, oa, token_at, 0, p, r.osem)
    o_in = to_twin(oa, 24)
    hgu[...] = dot_nt(wgu[...], qa[...])
    r.rzT[...] = rz[...].T
    for copy in o_in:
        copy.wait_recv()
    dact[...] = dot_nt(r.rzT[...], oa[...])

    def query_rows(at):
        up = pl.ds(pl.multiple_of(at.start + 128, 16), 16)
        g, u, d = hgu[at, :], hgu[up, :], dact[at, :]
        sig = jax.nn.sigmoid(g)
        hact[at, :] = (g * sig * u).astype(BF)
        hd[up, :] = (d * g * sig).astype(BF)
        hd[at, :] = (d * u * sig * (1.0 + g * (1.0 - sig))).astype(BF)
    by_rows(128, 16, query_rows)
    hsum = r.hsum
    hdn8, hgu8 = r.hdn8, r.hgu8
    hdn8[...] = dot(hact[...], oa[...])
    r.pd[...] = hdn8[...].T

    def own_down(value):
        r.dout[...] = value.astype(BF)

    def own_wide(p):
        def store(value):
            hsum[:, half * p:half * (p + 1)] = value
        return store

    def wide_cut(p):
        return lambda zb: hgu8[pl.ds(rows * zb + (128 - 2 * rows) * (zb // 2), rows),
                               half * p:half * (p + 1)]

    pieces = (
        (lambda zb: r.pd[zrows * zb:zrows * (zb + 1), :], r.ldo, r.ldi, own_down),
        (wide_cut(0), r.lgo0, r.lgi0, own_wide(0)),
        (wide_cut(1), r.lgo1, r.lgi1, own_wide(1)),
    )
    summing = LineSum(net, pieces, r.lsem)
    summing.run(lambda i, p, hops: hops == 0 and i == 0 and p == 0)
    hgu8[...] = dot(hd[...], qa[...])
    summing.run(lambda i, p, hops: hops == 0 and i + p > 0)
    r.hdT[...] = hd[...].T
    hd = r.hdT
    dqs, dqm, dqt = r.dqs, r.dqm, r.dqt
    dq_in = []
    for g in range(4):
        at = block(g, toks)
        dqs[at, :] = dot(hd[block(2 * g + 1 - c, toks), :], wgu[...]).astype(BF)
        dq_in.append(twin(dqs.at[at, :], dqt.at[at, :], 28 + g))
    for g in range(4):
        at = block(g, toks)
        mid = dot(hd[block(2 * g + c, toks), :], wgu[...])
        dq_in[g].wait_recv()
        dqm[at, :] = (mid + dqt[at, :].astype(F32)).astype(BF)
    query_sum = PlaneSum(
        net, dqm, lambda yx, p: (block(2 * yx[0] + yx[1], toks), block(p, half)), r.dqs3)
    query_sum.first()
    summing.run(lambda i, p, hops: hops == 1)
    summing.run(lambda i, p, hops: 1 < hops < zs)
    query_sum.second()
    summing.run(lambda i, p, hops: hops == zs and p == 0)
    dout, din = r.dout, r.din
    mine_at = lambda yx: block(2 * yx[0] + yx[1], rows)
    usem = r.usem
    units = [send(dout.at[mine_at(yx), :], din.at[:, lane_of((net.y, net.x))], usem, k, peer)
             for k, (yx, peer) in enumerate(zip(near, near_at))]
    din[:, lane_of((net.y, net.x))] = dout[mine_at((net.y, net.x)), :]
    summing.run(lambda i, p, hops: hops == zs and p > 0)
    back = r.full1

    def turned(h, g, sc, prod):
        return (-STEP_SIZE * h / sc - g * prod / (width * sc * sc * sc)).astype(BF)

    def wide_back():
        h, g = hsum[:, wide], grad[:, wide]
        prod = jnp.sum(-STEP_SIZE * h * g, axis=1, keepdims=True)
        back[own, wide] = turned(h, g, scale[0][:, :1], prod)

    def down_back():
        for copy in units:
            copy.wait_recv()
        hsum[:, dl] = dot_nt(din[...], r.sel[...])
        product = jnp.sum(-STEP_SIZE * hsum[:, dl] * grad[:, dl], axis=1, keepdims=True)
        r.sq[2] = jnp.broadcast_to(product, (rows, 128))
        twin(r.sq.at[2], r.sq.at[3], 7).wait_recv()
        prod = (r.sq[2] + r.sq[3])[:, :1]
        back[own, dl] = turned(hsum[:, dl], grad[:, dl], scale[1][:, :1], prod)

    placed, hp, hdn = r.placed, r.hp, r.hdn

    def place_sums():
        placed[...] = jnp.zeros_like(placed)
        hdn[...] = jnp.zeros_like(hdn)
        for k in range(2):
            to = pl.ds(pl.multiple_of((half // 2) * k + rows * net.g, rows), rows)
            to_up = pl.ds(pl.multiple_of(half + (half // 2) * k + rows * net.g, rows), rows)
            placed[to, :] = hgu8[k * rows:(k + 1) * rows, :]
            placed[to_up, :] = hgu8[128 + k * rows:128 + (k + 1) * rows, :]
            hdn[to, :] = hdn8[k * rows:(k + 1) * rows, :]
        hp[...] = placed[...].T
        r.taT[:, pl.ds(every, every)] = ab[...].T

    ag1 = all_gather(net, back, r.ag1, (wide_back, down_back), place_sums)

    def query_done(p, value):
        d_queries[:, p * half:(p + 1) * half] = value.astype(BF)
    query_sum.last(query_done)

    pq, tb, ec = r.pq, r.tb, r.ec
    pq[...] = dot_nt(xb[...], back[:, wide])

    def t_rows(at):
        g, u = gu[at, gl], gu[at, ul]
        p, q = pq[at, gl], pq[at, ul]
        sig = jax.nn.sigmoid(g)
        tb[at, :] = (q * g * sig + p * u * sig * (1.0 + g * (1.0 - sig))).astype(BF)
    by_rows(every, 32, t_rows)
    sp, sr, sb = r.sp, r.sr, r.sb
    second_out = []
    for k, at in enumerate((mine, theirs)):
        sp[at, :] = dot_nt(ab[at, :], back[:, dl]) + dot(tb[at, :], r.cb[...])
        second_out.append(twin(sp.at[at, :], sr.at[at, :], 8 + k))
    ec[...] = dot(eb[...], back[:, dl])
    r.taT[:, pl.ds(0, every)] = tb[...].T
    for copy, at in zip(second_out, (theirs, mine)):
        copy.wait_recv()
        sb[at, :] = (sp[at, :] + sr[at, :]).astype(BF)
    prow = 2 * rows
    dsw, dloc = r.dsw, r.dloc
    dloc[...] = (r.hdn[...] + dot(r.taT[:, pl.ds(0, every)], eb[...])
                 + dot(r.taT[:, pl.ds(every, every)], sb[...])).astype(BF)
    swaps = []
    for k in range(zs // 2):
        slot = (zs // 2) * c + k
        swaps.append(twin(dloc.at[block(2 * k + 1 - c, prow), :], dsw.at[slot], 10 + k))
        dsw[slot] = dloc[block(2 * k + c, prow), :]
    d_values[...] = -(sp[mine, :] + sr[mine, :])
    ec[...] += dot_nt(sb[...], r.cb[...])
    gub = r.gub

    def pull_rows(at):
        g, u, d = gu[at, gl], gu[at, ul], da[at, :]
        p, q, back_a = pq[at, gl], pq[at, ul], ec[at, :]
        sig = jax.nn.sigmoid(g)
        sneg = 1.0 - sig
        h = g * sig
        slope = sig * (1.0 + g * sneg)
        bend = sig * sneg * (2.0 + g * (1.0 - 2.0 * sig))
        pd = p * d
        gub[at, gl] = (back_a * u * slope + pd * u * bend + q * d * slope).astype(BF)
        gub[at, ul] = (back_a * h + pd * slope).astype(BF)
    by_rows(every, 32, pull_rows)

    pay2 = r.pay2

    def last_side():
        pay2[:, :outer] = (r.hp[:, :outer] + dot(r.xT[...], gub[:, :outer])).astype(BF)

    def last_block(zb, i):
        at = block(zb, zrows)
        pay2[at, inner] = (r.hp[at, inner] + dot(r.xT[at, :], gub[:, inner])).astype(BF)
        if i == 0:
            for copy in swaps:
                copy.wait_recv()
        for y in range(2):
            for x in range(2):
                pay2[block(4 * zb + 2 * y + x, rows), dl] = (
                    dsw[zb, y * rows:(y + 1) * rows, x * half:(x + 1) * half])

    def key_back():
        r.kp[...] = dot(dgu[...], back[:, wide])

    def key_back_second():
        r.kp[...] += dot_nt(gub[...], r.abb[...])
        r.kin = twin(r.kp.at[theirs, :], r.kr, 10 + zs // 2)

    last = r.last
    rs2 = reduce_scatter(net, pay2, r.rs2, last, last_block, last_side,
                         {0: key_back, 1: key_back_second})
    fin = r.fin
    fin[block(net.g, rows), :] = last[...].astype(BF)
    final = [send(fin.at[block(net.g, rows), :], fin.at[block(net.g, rows), :], r.fsem, k, peer)
             for k, peer in ((2, near_at[2]), (0, near_at[0]), (1, near_at[1]))]
    r.kin.wait_recv()
    d_keys[...] = r.kp[mine, :] + r.kr[...]
    for copy in final:
        copy.wait_recv()
    swap = twin(fin.at[block(1 - c, prow), wide], r.tw, 11 + zs // 2)
    lanes = block(c, half)
    others = block(1 - c, half)
    d_gate[:, lanes] = fin[block(c, prow), gl].astype(F32) * inverse
    d_up[:, lanes] = fin[block(c, prow), ul].astype(F32) * inverse
    for y in range(2):
        for x in range(2):
            g = 2 * y + x
            d_down[y * rows:(y + 1) * rows, x * half:(x + 1) * half] = (
                fin[g * rows:(g + 1) * rows, width:].astype(F32) * inverse)
    swap.wait_recv()
    d_gate[:, others] = r.tw[:, :half].astype(F32) * inverse
    d_up[:, others] = r.tw[:, half:].astype(F32) * inverse
    await_copy(net, r.sq.at[0], tsem, 5, 5)
    drain(done + slices + units + final)
    query_sum.finish()
    for finish in (rs0, ag1, rs2, summing.finish):
        finish()
    for p in range(2):
        plane_drain(net, qa, token_at, 0, p, r.qsem)
        plane_drain(net, oa, token_at, 0, p, r.osem)

    def drain_line(z):
        for zb in range(zs):
            for p in range(2):
                pass_drain(net, z, zb, p, gz_at(zb, p), line)
            if zb != z:
                await_copy(net, rz_at(z), xsem, (zb,), (zb,))
    at_each(net, drain_line)


def hand_over(*refs):
    for src, dst in zip(refs[:6], refs[6:]):
        dst[...] = src[...]


def fused_step(queries, key_tokens, values, out_grad, w_gate, w_up, w_down, zs, inverse):
    toks, width = queries.shape
    half, every, rows = width // 2, 2 * toks, width // (4 * zs)
    plane = 4 * every
    total = width + half
    side, main = lane_parts(total)
    unit = side[0].size
    f32 = lambda *shape: VM(shape, F32)
    bf = lambda *shape: VM(shape, BF)
    sems = lambda *shape: (DMA(shape), DMA(shape))
    both = lambda *shape: tuple(VM(shape + (part.size,), BF) for part in main)
    summed = dict(
        r1=both(zs, 2, rows), r2=both(zs, rows), zb=both(zs - 1, rows), zr=both(zs + 1, rows),
        s1=sems(zs, 2, 2), s2=sems(zs, 2), s3=sems(zs + 1, 2), pb=bf(4 * rows, 2 * unit),
        lo=(bf(zs - 1, 4 * rows, unit),) * 2, li=(bf(zs + 1, 4 * rows, unit),) * 2,
        ls=sems(zs + 1, 2),
        ps=dict(r1=bf(2, 2, rows, unit), r2=bf(2, rows, unit), s1=sems(2, 2), s2=sems(2)))
    spread = lambda depth: dict(
        z=sems(depth, 2, 2), o=sems(depth, 2, 2), f=sems(depth, 2))
    scratch = dict(
        kf=f32(toks, width), vf=f32(toks, width), wab=f32(width, width), wc=f32(half, width),
        wabt=f32(width, width), wct=f32(width, half), gu=f32(every, width), ep=f32(every, width),
        er=f32(every, width), da=f32(every, half), grad=f32(rows, total), hsum=f32(rows, total),
        last=f32(rows, total), sq=f32(4, rows, 128), scale=f32(2, rows, 128),
        hgu=f32(256, plane), dact=f32(128, plane), hdn8=f32(128, width), hgu8=f32(256, width),
        pd=f32(width, 128), placed=f32(width, width), hp=f32(width, width), hdn=f32(half, width),
        pq=f32(every, width), ec=f32(every, half), sp=f32(every, width), sr=f32(every, width),
        kp=f32(every, width), kr=f32(toks, width),
        xb=bf(every, width), qa=bf(plane, width), oa=bf(plane, width), abb=bf(width, width),
        cb=bf(half, width), ab=bf(every, half), eb=bf(every, width), dgu=bf(every, width),
        dguT=bf(width, every), eT=bf(width, every), xT=bf(width, every), hd=bf(256, plane),
        hdT=bf(plane, 256), hact=bf(128, plane), rzT=bf(128, width), tb=bf(every, half),
        sel=bf(half, 512), wgu=bf(256, width), gz=bf(zs * rows, width), rz=bf(width, 128),
        dsl=bf(rows, 512), dout=bf(4 * rows, 128), din=bf(rows, 512), dqs=bf(4 * toks, width),
        dqm=bf(4 * toks, width), dqt=bf(4 * toks, width),
        ldo=bf(zs - 1, 4 * rows, 128), ldi=bf(zs + 1, 4 * rows, 128),
        lgo0=bf(zs - 1, rows, half), lgi0=bf(zs + 1, rows, half),
        lgo1=bf(zs - 1, rows, half), lgi1=bf(zs + 1, rows, half),
        sb=bf(every, width), taT=bf(half, 2 * every), gub=bf(every, width), dloc=bf(half, width),
        dsw=bf(zs, 2 * rows, width), pay0=bf(width, total), pay2=bf(width, total),
        full1=bf(width, total), fin=bf(4 * rows, total), tw=bf(2 * rows, width),
        rs0=summed, rs2=summed, ag1=spread(zs), fsem=sems(3), qsem=spread(1), osem=spread(1),
        line=spread(zs), lsem=sems(zs + 1, 3), xsem=sems(zs), ssem=sems(3), usem=sems(3),
        dqs3=dict(r1=bf(2, 2, toks, half), r2=bf(2, toks, half), s1=sems(2, 2), s2=sems(2)),
        tsem=sems(32), ld=DMA((7,)))
    shapes, tree = jax.tree.flatten(scratch)
    token = jax.ShapeDtypeStruct((toks, width), F32)
    weight = jax.ShapeDtypeStruct((2 * rows, width), F32)
    results = pl.pallas_call(
        functools.partial(step_body, zs, tree, inverse),
        out_shape=(jax.ShapeDtypeStruct((toks, width), BF), token, token, weight, weight, weight),
        in_specs=[pl.BlockSpec(memory_space=pltpu.HBM)] * 7,
        out_specs=[pl.BlockSpec(memory_space=VM)] * 6,
        scratch_shapes=shapes,
        compiler_params=pltpu.CompilerParams(
            collective_id=0, has_side_effects=True, vmem_limit_bytes=52 * 1024 * 1024),
    )(*(pltpu.with_memory_space_constraint(x, pltpu.HBM) for x in (
        queries, key_tokens, values, out_grad, w_gate, w_up, w_down)))
    return pl.pallas_call(
        hand_over,
        out_shape=tuple(jax.ShapeDtypeStruct(item.shape, item.dtype) for item in results),
        in_specs=[pl.BlockSpec(memory_space=VM)] * 6,
        out_specs=[pl.BlockSpec(memory_space=VM)] * 6,
        compiler_params=pltpu.CompilerParams(vmem_limit_bytes=8 * 1024 * 1024),
    )(*results)


def matmul(left, right):
    return dot(left.astype(BF), right.astype(BF))


def key_grad(w_gate, w_up, w_down, key_rows, value_rows):
    hidden_gate = matmul(key_rows, w_gate)
    hidden_up = matmul(key_rows, w_up)
    sig = jax.nn.sigmoid(hidden_gate)
    active = hidden_gate * sig * hidden_up
    error = matmul(active, w_down) - value_rows
    d_active = matmul(error, w_down.T)
    d_hup = d_active * hidden_gate * sig
    d_hgate = d_active * hidden_up * sig * (1.0 + hidden_gate * (1.0 - sig))
    return (matmul(d_hgate.T, key_rows), matmul(d_hup.T, key_rows), matmul(error.T, active))


def query_grad(fast_t, query_rows, grad_rows):
    gate_t, up_t, down_t = fast_t
    hidden_gate = dot(query_rows, gate_t.T)
    hidden_up = dot(query_rows, up_t.T)
    sig = jax.nn.sigmoid(hidden_gate)
    active = (hidden_gate * sig * hidden_up).astype(BF)
    d_active = dot(grad_rows, down_t)
    d_hup = (d_active * hidden_gate * sig).astype(BF)
    d_hgate = (d_active * hidden_up * sig * (1.0 + hidden_gate * (1.0 - sig))).astype(BF)
    d_rows = (dot(d_hgate, gate_t) + dot(d_hup, up_t)).astype(BF)
    return (d_rows, active, d_hgate, d_hup)


def general_step(queries, key_tokens, values, out_grad, w_gate, w_up, w_down, inverse):
    gs, toks = lax.axis_size("grp"), lax.axis_size("tok")
    full_width = w_gate.shape[0]
    rows = 3 * full_width // (gs * toks)
    me = lax.axis_index("tok") * gs + lax.axis_index("grp")

    def reduce_units(x):
        y = x.reshape(toks, gs * rows, full_width)
        y = lax.psum_scatter(y, "tok", scatter_dimension=0, tiled=True)[0]
        return lax.psum_scatter(y.reshape(gs, rows, full_width), "grp", scatter_dimension=0, tiled=True)[0]

    def gather_units(y):
        full = lax.all_gather(lax.all_gather(y, "grp"), "tok").reshape(3, full_width, full_width)
        return full[0], full[1], full[2]

    local_grad, pullback = jax.vjp(key_grad, w_gate, w_up, w_down, key_tokens, values)
    grad = reduce_units(jnp.stack(local_grad))
    scale = jnp.sqrt(jnp.sum(grad * grad, axis=1, keepdims=True) / full_width + EPSILON)
    weights = jnp.concatenate((w_gate, w_up, w_down), axis=1)
    mine = lax.dynamic_slice_in_dim(weights, me * rows, rows, 1).T
    fast_t = gather_units((mine - STEP_SIZE * grad / scale).astype(BF))
    d_queries, active, d_hgate, d_hup = query_grad(fast_t, queries, out_grad)
    query_part = reduce_units(
        jnp.stack((dot(d_hgate.T, queries), dot(d_hup.T, queries), dot(out_grad.T, active))))
    product = jnp.sum(-STEP_SIZE * query_part * grad, axis=1, keepdims=True)
    cot = (
        -STEP_SIZE * query_part / scale - grad * product / (full_width * scale * scale * scale)
    ).astype(BF)
    second = pullback(tuple(item.astype(F32) for item in gather_units(cot)))
    plain = (dot(queries.T, d_hgate), dot(queries.T, d_hup), dot(active.T, out_grad))
    combined = jnp.stack(tuple(left + right for left, right in zip(plain, second[:3])))
    combined = combined.reshape(3, toks, full_width // toks, full_width).transpose(1, 0, 2, 3)
    summed = lax.all_gather(reduce_units(combined).astype(BF), "grp").astype(F32) * inverse
    summed = summed.reshape(3, full_width // toks, full_width)
    return (d_queries, second[3], second[4], summed[0], summed[1], summed[2])


def on_device(*arrays):
    gs, toks = lax.axis_size("grp"), lax.axis_size("tok")
    tokens, width = arrays[0].shape
    inverse = 1.0 / (tokens * gs * toks)
    zs = toks // 2
    fits = gs == 4 and toks % 4 == 0 and zs <= 4
    if fits and width % (64 * zs) == 0 and 2 * width <= 512 * zs and width % 256 == 0 and tokens % 128 == 0:
        return fused_step(*arrays, zs, inverse)
    return general_step(*arrays, inverse)


def solution(mesh):
    token = P(("grp", "tok"), None)
    return jax.shard_map(
        on_device,
        mesh=mesh,
        in_specs=(token, token, token, token, P(), P(), P()),
        out_specs=(token, token, token, P("tok", None), P("tok", None), P("tok", None)),
        check_vma=False,
    )
```

```python
import functools
from types import SimpleNamespace as Names

import jax
import jax.numpy as jnp
from jax import lax
from jax.experimental import pallas as pl
from jax.experimental.pallas import tpu as pltpu
from jax.sharding import PartitionSpec as P

STEP_SIZE = 0.02
EPSILON = 1e-06
MESH = pl.DeviceIdType.MESH
BF = jnp.bfloat16
F32 = jnp.float32
VM = pltpu.VMEM
DMA = pltpu.SemaphoreType.DMA


def dot(left, right):
    return jnp.dot(left, right, preferred_element_type=F32)


def dot_nt(left, right):
    return lax.dot_general(left, right, (((1,), (1,)), ((), ())), preferred_element_type=F32)


def block(index, size):
    return pl.ds(pl.multiple_of(index * size, size), size)


def lane_parts(width):
    unit = 128 * max(1, width // 1152)
    cut = width - 128 * ((width // 128 - 2 * (unit // 128)) // 2)
    return ((pl.ds(0, unit), pl.ds(unit, unit)),
            (pl.ds(2 * unit, cut - 2 * unit), pl.ds(cut, width - cut)))


class Net:
    def __init__(self, zs, rows, width):
        g, t = lax.axis_index("grp"), lax.axis_index("tok")
        self.zs, self.rows = zs, rows
        self.g, self.z, self.c = g, t // 2, lax.rem(t, 2)
        self.y, self.x = g // 2, lax.rem(g, 2)
        self.t = t
        self.outer, self.lanes = lane_parts(width)
        cut = 128 * ((width // 128 + 1) // 2)
        self.parts = (pl.ds(0, cut), pl.ds(cut, width - cut))
        self.twin = (g, 2 * self.z + 1 - self.c)

    def flip(self, *directions):
        y, x = self.y, self.x
        for a in directions:
            x = x + (1 - a) * (1 - 2 * x)
            y = y + a * (1 - 2 * y)
        return y, x

    def turn(self, n):
        return lax.rem(n + self.c, 2)

    def side(self, a):
        y, x = self.flip(a)
        return (2 * y + x, self.t)

    def across(self):
        y, x = self.flip(0, 1)
        return (2 * y + x, self.t)

    def at_z(self, z):
        return (self.g, 2 * z + self.c)

    def pick(self, table):
        value = table[0]
        for z in range(1, self.zs):
            value = jnp.where(self.z == z, table[z], value)
        return value

    def chunk(self, zb, yx):
        return block(4 * zb + 2 * yx[0] + yx[1], self.rows)

    def greet(self):
        barrier = pltpu.get_barrier_semaphore()
        peers = [self.twin, self.side(0), self.side(1), self.across()]
        for d in range(1, self.zs):
            peers.append(self.at_z(lax.rem(self.z + d, self.zs)))
        for peer in peers:
            pl.semaphore_signal(barrier, inc=1, device_id=peer, device_id_type=MESH)
        pl.semaphore_wait(barrier, len(peers))


def send(src, dst, sems, at, peer, there=None):
    copy = pltpu.make_async_remote_copy(
        src_ref=src, dst_ref=dst, send_sem=sems[0].at[at],
        recv_sem=sems[1].at[at if there is None else there],
        device_id=peer, device_id_type=MESH,
    )
    copy.start()
    return copy


def await_copy(net, ref, sems, at, there=None):
    copy = pltpu.make_async_remote_copy(
        src_ref=ref, dst_ref=ref, send_sem=sems[0].at[at if there is None else there],
        recv_sem=sems[1].at[at], device_id=net.twin, device_id_type=MESH,
    )
    if there is None:
        copy.wait_recv()
    else:
        copy.wait_send()


def sum_order(zs, z):
    def key(zb):
        hops = z if zb > z else zs - 1 - z
        return (zb == z, hops, -abs(zb - z))
    return sorted(range(zs), key=key)


def spread_order(zs, z):
    return sorted(range(zs), key=lambda zb: (abs(zb - z), (zb > z) == (2 * z < zs)))


def reduce_scatter(net, pay, s, total, produce, produce_side, fillers, ready=None):
    zs = net.zs
    orders = [sum_order(zs, z) for z in range(zs)]
    blocks = [net.pick([orders[z][i] for z in range(zs)]) for i in range(zs)]
    first, second = {}, {}
    unit = s.pb.shape[-1] // 2

    def line_piece(p):
        def cut(zb):
            return pay[pl.ds(4 * net.rows * zb, 4 * net.rows), net.outer[p]]

        def own(value):
            s.pb[:, unit * p:unit * (p + 1)] = value.astype(BF)
        return cut, s.lo[p], s.li[p], own

    line = LineSum(net, (line_piece(0), line_piece(1)), s.ls)
    plane = PlaneSum(net, s.pb, lambda yx, p: (
        block(2 * yx[0] + yx[1], net.rows), pl.ds(unit * p, unit)), s.ps)

    def when_inside(inside, body):
        inner = (net.z > 0) & (net.z < zs - 1)
        pl.when(inner if inside else jnp.logical_not(inner))(body)

    def start_first(i, k):
        for p in (1, 0):
            a = net.turn(p + i)
            yx = net.flip(a, 1 - a) if k == 0 else net.flip(a)
            first[i, p, k] = send(
                pay.at[net.chunk(blocks[i], yx), net.lanes[p]], s.r1[p].at[i, k],
                s.s1, (i, p, k), net.side(a))

    def start_second(i):
        for p in (1, 0):
            a = net.turn(p + i)
            first[i, p, 0].wait_recv()
            at = (net.chunk(blocks[i], net.flip(1 - a)), net.lanes[p])
            pay[at] = (pay[at].astype(F32) + s.r1[p][i, 0].astype(F32)).astype(BF)
            second[i, p] = send(pay.at[at], s.r2[p].at[i], s.s2, (i, p), net.side(1 - a))

    def along(z, i):
        zb = orders[z][i]
        for p in (1, 0):
            first[i, p, 1].wait_recv()
            second[i, p].wait_recv()
            at = (net.chunk(zb, (net.y, net.x)), net.lanes[p])
            value = (pay[at].astype(F32) + s.r1[p][i, 1].astype(F32)
                     + s.r2[p][i].astype(F32))
            slots = []
            if zb >= z and z > 0:
                slots.append(i)
            if zb <= z and z < zs - 1:
                slots.append(i if zb < z else zs)
            for slot in slots:
                await_copy(net, s.zr[p].at[slot], s.s3, (slot, p))
                value = value + s.zr[p][slot].astype(F32)
            if zb == z:
                total[:, net.lanes[p]] = value
                if p == 1 and ready is not None:
                    ready()
            else:
                s.zb[p][i] = value.astype(BF)
                nxt = z + 1 if zb > z else z - 1
                slot = orders[nxt].index(zb) if nxt != zb or zb > z else zs
                send(s.zb[p].at[i], s.zr[p].at[slot], s.s3, (i, p), net.at_z(nxt),
                     (slot, p))

    last = 0
    steps = [{} for _ in range(zs)]
    for z in range(zs):
        for i, zb in enumerate(orders[z]):
            hops = 0 if zb == z else z if zb > z else zs - 1 - z
            when = zs + 2 if zb == z else i + 2 + min(hops, 1)
            steps[z].setdefault(when, []).append(i)
            last = max(last, when)
    for i in range(last + 1):
        if i < zs:
            produce(blocks[i], i)
            start_first(i, 0)
        if i == 0:
            produce_side()
            line.run(lambda n, p, hops: hops == 0)
        if 1 <= i <= zs:
            start_second(i - 1)
        if i < zs:
            start_first(i, 1)
        line.run(lambda n, p, hops: 0 < hops < zs and max(n + 1, 2) == i)
        for inside in (True, False):
            if i == (zs - 1 if inside else zs):
                line.run(lambda n, p, hops: hops == zs, inside)
                when_inside(inside, plane.first)
        for z in range(zs):
            if i in steps[z]:
                @pl.when(net.z == z)
                def _():
                    for k in steps[z][i]:
                        along(z, k)
        for inside in (True, False):
            if i == (zs if inside else zs + 1):
                when_inside(inside, plane.second)
        if i in fillers:
            fillers[i]()
    def plane_done(p, value):
        total[:, net.outer[p]] = value
    plane.last(plane_done)

    def finish():
        drain([*first.values(), *second.values()])
        plane.finish()
        line.finish()
        for i in range(zs - 1):
            for p in range(2):
                await_copy(net, s.zb[p].at[i], s.s3, (i, p), (i, p))
    return finish


def plane_own(net, ref, at, i, p, k, s):
    ref = ref.at[at((net.y, net.x), p)]
    return send(ref, ref, s.o, (i, p, k), net.side(net.turn(p + i + k)))


def plane_relay(net, ref, at, i, p, s):
    a = net.turn(p + i)
    ref = ref.at[at(net.flip(a), p)]
    await_copy(net, ref, s.o, (i, p, 0))
    return send(ref, ref, s.f, (i, p), net.side(1 - a))


def plane_rest(net, ref, at, i, p, s):
    a = net.turn(p + i)
    await_copy(net, ref.at[at(net.flip(1 - a), p)], s.o, (i, p, 1))
    await_copy(net, ref.at[at(net.flip(0, 1), p)], s.f, (i, p))


def plane_drain(net, ref, at, i, p, s):
    ref = ref.at[at((net.y, net.x), p)]
    for k in range(2):
        await_copy(net, ref, s.o, (i, p, k), (i, p, k))
    await_copy(net, ref, s.f, (i, p), (i, p))


def at_each(net, body):
    for z in range(net.zs):
        @pl.when(net.z == z)
        def _():
            body(z)


def onward(zs, z, zb):
    return [(k, other) for k, other in enumerate((z - 1, z + 1))
            if 0 <= other < zs and (zb == z or (zb > z) == (other < z))]


def pass_on(net, z, zb, p, ref, s):
    for k, other in onward(net.zs, z, zb):
        send(ref, ref, s.z, (zb, p, k), net.at_z(other), (zb, p, 0))


def pass_drain(net, z, zb, p, ref, s):
    for k, other in onward(net.zs, z, zb):
        await_copy(net, ref, s.z, (zb, p, 0), (zb, p, k))


def all_gather(net, full, s, parts, idle):
    zs = net.zs
    place = lambda zb: lambda yx, p: (net.chunk(zb, yx), net.parts[p])
    mine = lambda zb, p: full.at[place(zb)((net.y, net.x), p)]

    for p in range(2):
        parts[p]()
        at_each(net, lambda z: pass_on(net, z, z, p, mine(z, p), s))
        plane_own(net, full, place(net.z), 0, p, 0, s)
    for p in range(2):
        plane_own(net, full, place(net.z), 0, p, 1, s)

    def rest(z):
        order = spread_order(zs, z)
        for i in range(1, zs):
            for p in range(2):
                await_copy(net, mine(order[i], p), s.z, (order[i], p, 0))
                pass_on(net, z, order[i], p, mine(order[i], p), s)
                plane_own(net, full, place(order[i]), i, p, 0, s)
            for p in range(2):
                plane_own(net, full, place(order[i]), i, p, 1, s)
            for p in range(2):
                plane_relay(net, full, place(order[i - 1]), i - 1, p, s)
        for p in range(2):
            plane_relay(net, full, place(order[zs - 1]), zs - 1, p, s)

    def arrive(z):
        for i, zb in enumerate(spread_order(zs, z)):
            for p in range(2):
                plane_rest(net, full, place(zb), i, p, s)
    at_each(net, rest)
    idle()
    at_each(net, arrive)

    def finish():
        def go(z):
            order = spread_order(zs, z)
            for i in range(zs):
                for p in range(2):
                    pass_drain(net, z, order[i], p, mine(order[i], p), s)
                    plane_drain(net, full, place(order[i]), i, p, s)
        at_each(net, go)
    return finish


class PlaneSum:
    def __init__(self, net, ref, at, s):
        self.net, self.ref, self.at, self.s = net, ref, at, s

    def first(self):
        net, s = self.net, self.s
        for k in range(2):
            for p in range(2):
                yx = net.flip(p, 1 - p) if k == 0 else net.flip(p)
                send(self.ref.at[self.at(yx, p)], s.r1.at[p, k], s.s1, (p, k), net.side(p))

    def second(self):
        net, s = self.net, self.s
        for p in range(2):
            await_copy(net, s.r1.at[p, 0], s.s1, (p, 0))
            at = self.at(net.flip(1 - p), p)
            self.ref[at] = (self.ref[at].astype(F32) + s.r1[p, 0].astype(F32)).astype(BF)
            send(self.ref.at[at], s.r2.at[p], s.s2, (p,), net.side(1 - p))

    def last(self, done):
        net, s = self.net, self.s
        for p in range(2):
            await_copy(net, s.r1.at[p, 1], s.s1, (p, 1))
            await_copy(net, s.r2.at[p], s.s2, (p,))
            value = self.ref[self.at((net.y, net.x), p)].astype(F32)
            done(p, value + s.r1[p, 1].astype(F32) + s.r2[p].astype(F32))

    def finish(self):
        net, s = self.net, self.s
        for p in range(2):
            for k in range(2):
                await_copy(net, s.r1.at[p, k], s.s1, (p, k), (p, k))
            await_copy(net, s.r2.at[p], s.s2, (p,), (p,))


class LineSum:
    def __init__(self, net, pieces, sems):
        self.net, self.pieces, self.sems = net, pieces, sems
        self.orders = [sum_order(net.zs, z) for z in range(net.zs)]

    def hops(self, z, i):
        zb = self.orders[z][i]
        return self.net.zs if zb == z else z if zb > z else self.net.zs - 1 - z

    def move(self, z, i, p):
        net, zs = self.net, self.net.zs
        cut, out, inn, own = self.pieces[p]
        zb = self.orders[z][i]
        value = cut(zb)
        slots = []
        if zb >= z and z > 0:
            slots.append(i)
        if zb <= z and z < zs - 1:
            slots.append(i if zb < z else zs)
        for slot in slots:
            await_copy(net, inn.at[slot], self.sems, (slot, p))
            value = value + inn[slot].astype(F32)
        if zb == z:
            own(value)
            return
        out[i] = value.astype(BF)
        nxt = z + 1 if zb > z else z - 1
        slot = self.orders[nxt].index(zb) if nxt != zb or zb > z else zs
        send(out.at[i], inn.at[slot], self.sems, (i, p), net.at_z(nxt), (slot, p))

    def run(self, chosen, inside=None):
        def go(z):
            if inside is not None and inside != (0 < z < self.net.zs - 1):
                return
            for i in range(self.net.zs):
                for p in range(len(self.pieces)):
                    if chosen(i, p, self.hops(z, i)):
                        self.move(z, i, p)
        at_each(self.net, go)

    def finish(self):
        for i in range(self.net.zs - 1):
            for p, piece in enumerate(self.pieces):
                await_copy(self.net, piece[1].at[i], self.sems, (i, p), (i, p))


def drain(copies):
    for copy in copies:
        copy.wait_send()


def by_rows(count, step, body):
    def run(i, carry):
        body(pl.ds(pl.multiple_of(i * step, step), step))
        return carry
    lax.fori_loop(0, count // step, run, 0)


def named(tree):
    return Names(**{k: named(v) if isinstance(v, dict) else v for k, v in tree.items()})


def step_body(zs, tree, inverse, *refs):
    r = Names(**jax.tree.unflatten(tree, refs[13:]))
    for key, value in vars(r).items():
        if isinstance(value, dict):
            setattr(r, key, named(value))
    (queries, keys, values, out_grad, w_gate, w_up, w_down) = refs[:7]
    (d_queries, d_keys, d_values, d_gate, d_up, d_down) = refs[7:13]
    toks, width = queries.shape
    half = width // 2
    every = 2 * toks
    rows = width // (4 * zs)
    zrows = 4 * rows
    net = Net(zs, rows, width + half)
    c = net.c
    mine, theirs = block(c, toks), block(1 - c, toks)
    gl, ul, dl = pl.ds(0, half), pl.ds(half, half), pl.ds(width, half)
    wide = pl.ds(0, width)
    hid = block(c, half)

    token_at = lambda yx, p: (block(2 * (2 * yx[0] + yx[1]) + c, toks), block(p, half))
    spot = block(2 * net.g + c, toks)
    loads = Names()
    loads.k, loads.a, loads.b, loads.c, loads.v, loads.q, loads.o = [
        pltpu.make_async_copy(src, dst, r.ld.at[i]) for i, (src, dst) in enumerate((
            (keys, r.kf), (w_gate.at[:, hid], r.wab.at[:, gl]), (w_up.at[:, hid], r.wab.at[:, ul]),
            (w_down.at[hid, :], r.wc), (values, r.vf), (queries, r.qa.at[spot, :]),
            (out_grad, r.oa.at[spot, :])))]
    for load in vars(loads).values():
        load.start()
    net.greet()
    tsem = r.tsem
    done = []

    def twin(src, dst, k):
        copy = send(src, dst, tsem, k, net.twin)
        done.append(copy)
        return copy

    xb, gu, ab, eb = r.xb, r.gu, r.ab, r.eb
    loads.k.wait()
    xb[mine, :] = r.kf[...].astype(BF)
    keys_in = twin(xb.at[mine, :], xb.at[mine, :], 0)
    qa, oa = r.qa, r.oa
    loads.q.wait()
    loads.o.wait()
    for ref, sems in ((qa, r.qsem), (oa, r.osem)):
        for p in range(2):
            plane_own(net, ref, token_at, 0, p, 0, sems)
    loads.a.wait()
    loads.b.wait()
    r.abb[...] = r.wab[...].astype(BF)
    loads.c.wait()
    r.cb[...] = r.wc[...].astype(BF)
    keys_in.wait_recv()
    gu[...] = dot(xb[...], r.abb[...])

    def active_rows(at):
        g, u = gu[at, gl], gu[at, ul]
        ab[at, :] = (g * jax.nn.sigmoid(g) * u).astype(BF)
    by_rows(every, 32, active_rows)

    loads.v.wait()
    ep, er = r.ep, r.er
    ep[mine, :] = dot(ab[mine, :], r.cb[...]) - r.vf[...]
    e_out = [twin(ep.at[mine, :], er.at[mine, :], 3)]
    ep[theirs, :] = dot(ab[theirs, :], r.cb[...])
    e_out.append(twin(ep.at[theirs, :], er.at[theirs, :], 4))
    for copy, at in zip(e_out, (theirs, mine)):
        copy.wait_recv()
        eb[at, :] = (ep[at, :] + er[at, :]).astype(BF)
    da, dgu = r.da, r.dgu
    da[...] = dot_nt(eb[...], r.cb[...])

    def d_rows(at):
        g, u, d = gu[at, gl], gu[at, ul], da[at, :]
        sig = jax.nn.sigmoid(g)
        dgu[at, ul] = (d * g * sig).astype(BF)
        dgu[at, gl] = (d * u * sig * (1.0 + g * (1.0 - sig))).astype(BF)
    by_rows(every, 32, d_rows)
    r.dguT[...] = dgu[...].T
    r.eT[...] = eb[...].T

    pay = r.pay0

    outer = net.lanes[0].start
    inner = pl.ds(outer, width - outer)

    def key_side():
        pay[:, :outer] = dot(r.dguT[...], xb[:, :outer]).astype(BF)

    def key_block(zb, i):
        at = block(zb, zrows)
        pay[at, inner] = dot(r.dguT[at, :], xb[:, inner]).astype(BF)
        pay[at, dl] = dot(r.eT[at, :], ab[...]).astype(BF)

    def turn_weights():
        r.wabt[...] = r.wab[...].T
        r.wct[...] = r.wc[...].T

    def to_twin(ref, k):
        return [twin(ref.at[block(2 * g + c, toks), :], ref.at[block(2 * g + c, toks), :], k + g)
                for g in range(4)]

    def select_lanes():
        h = lax.broadcasted_iota(jnp.int32, (half, 512), 0)
        lane = lax.broadcasted_iota(jnp.int32, (half, 512), 1)
        g, l = lane // 128, lane % 128
        hit = (h == (half // 2) * (l // rows) + rows * g + l % rows) & (l < 2 * rows)
        r.sel[...] = jnp.where(hit, 1.0, 0.0).astype(BF)
        r.wgu[...] = jnp.zeros((256, width), BF)

    def turn_keys():
        r.xT[...] = xb[...].T

    def turn_arrays():
        turn_weights()
        select_lanes()
        turn_keys()

    grad = r.grad

    def down_norm():
        squares = jnp.sum(grad[:, dl] * grad[:, dl], axis=1, keepdims=True)
        r.sq[0] = jnp.broadcast_to(squares, (rows, 128))
        send(r.sq.at[0], r.sq.at[1], tsem, 5, net.twin)

    rs0 = reduce_scatter(net, pay, r.rs0, grad, key_block, key_side,
                         {0: turn_arrays},
                         down_norm)

    own = net.chunk(net.z, (net.y, net.x))
    scale_of = lambda sq: jnp.sqrt(sq / width + EPSILON)
    scale = r.scale

    gz, rz = r.gz, r.rz
    line = r.line
    gz_at = lambda zb, p: gz.at[pl.ds(rows * zb, rows), pl.ds(half * p, half)]
    rz_at = lambda zb: rz.at[pl.ds(zrows * zb, zrows), :]
    g = grad[:, wide]
    sc = scale_of(jnp.sum(g * g, axis=1, keepdims=True))
    scale[0] = jnp.broadcast_to(sc, (rows, 128))
    gz[block(net.z, rows), :] = (r.wabt[own, :] - STEP_SIZE * g / sc).astype(BF)
    at_each(net, lambda z: [pass_on(net, z, z, p, gz_at(z, p), line) for p in range(2)])
    await_copy(net, r.sq.at[1], tsem, 5)
    sc = scale_of((r.sq[0] + r.sq[1])[:, :1])
    scale[1] = jnp.broadcast_to(sc, (rows, 128))
    down = (r.wct[own, :] - STEP_SIZE * grad[:, dl] / sc).astype(BF)
    r.dsl[...] = dot(down, r.sel[...]).astype(BF)
    ssem = r.ssem
    near = [net.flip(0), net.flip(1), net.flip(0, 1)]
    near_at = [net.side(0), net.side(1), net.across()]
    lane_of = lambda yx: block(2 * yx[0] + yx[1], 128)
    rz[own, :] = r.dsl[:, lane_of((net.y, net.x))]
    slices = [send(r.dsl.at[:, lane_of(yx)], rz.at[own, :], ssem, k, peer)
              for k, (yx, peer) in enumerate(zip(near, near_at))]
    for ref, sems in ((qa, r.qsem), (oa, r.osem)):
        for p in range(2):
            plane_relay(net, ref, token_at, 0, p, sems)
        for p in range(2):
            plane_own(net, ref, token_at, 0, p, 1, sems)
    xsem = r.xsem

    def direct(z):
        for other in range(zs):
            if other != z:
                send(rz_at(z), rz_at(z), xsem, (other,), net.at_z(other), (z,))
    def gather_line(first, last):
        def go(z):
            for zb in spread_order(zs, z)[first:last]:
                for p in range(2):
                    await_copy(net, gz_at(zb, p), line.z, (zb, p, 0))
                    pass_on(net, z, zb, p, gz_at(zb, p), line)
            if last == zs:
                for zb in spread_order(zs, z)[1:]:
                    await_copy(net, rz_at(zb), xsem, (zb,))
        at_each(net, go)

    gather_line(1, 2)
    for copy in slices:
        copy.wait_recv()
    at_each(net, direct)
    gather_line(2, 3)
    for p in range(2):
        plane_rest(net, qa, token_at, 0, p, r.qsem)
    q_in = to_twin(qa, 20)
    gather_line(3, zs)

    wgu, hgu, dact, hd, hact = r.wgu, r.hgu, r.dact, r.hd, r.hact
    wgu[:2 * rows, :] = gz[:2 * rows, :]
    wgu[128:128 + 2 * rows, :] = gz[2 * rows:, :]
    for copy in q_in:
        copy.wait_recv()
    for p in range(2):
        plane_rest(net, oa, token_at, 0, p, r.osem)
    o_in = to_twin(oa, 24)
    hgu[...] = dot_nt(wgu[...], qa[...])
    r.rzT[...] = rz[...].T
    for copy in o_in:
        copy.wait_recv()
    dact[...] = dot_nt(r.rzT[...], oa[...])

    def query_rows(at):
        up = pl.ds(pl.multiple_of(at.start + 128, 16), 16)
        g, u, d = hgu[at, :], hgu[up, :], dact[at, :]
        sig = jax.nn.sigmoid(g)
        hact[at, :] = (g * sig * u).astype(BF)
        hd[up, :] = (d * g * sig).astype(BF)
        hd[at, :] = (d * u * sig * (1.0 + g * (1.0 - sig))).astype(BF)
    by_rows(128, 16, query_rows)
    hsum = r.hsum
    hdn8, hgu8 = r.hdn8, r.hgu8
    hdn8[...] = dot(hact[...], oa[...])
    r.pd[...] = hdn8[...].T

    def own_down(value):
        r.dout[...] = value.astype(BF)

    def own_wide(p):
        def store(value):
            hsum[:, half * p:half * (p + 1)] = value
        return store

    def wide_cut(p):
        return lambda zb: hgu8[pl.ds(rows * zb + (128 - 2 * rows) * (zb // 2), rows),
                               half * p:half * (p + 1)]

    pieces = (
        (lambda zb: r.pd[zrows * zb:zrows * (zb + 1), :], r.ldo, r.ldi, own_down),
        (wide_cut(0), r.lgo0, r.lgi0, own_wide(0)),
        (wide_cut(1), r.lgo1, r.lgi1, own_wide(1)),
    )
    summing = LineSum(net, pieces, r.lsem)
    summing.run(lambda i, p, hops: hops == 0 and i == 0 and p == 0)
    hgu8[...] = dot(hd[...], qa[...])
    summing.run(lambda i, p, hops: hops == 0 and i + p > 0)
    r.hdT[...] = hd[...].T
    hd = r.hdT
    dqs, dqm, dqt = r.dqs, r.dqm, r.dqt
    dq_in = []
    for g in range(4):
        at = block(g, toks)
        dqs[at, :] = dot(hd[block(2 * g + 1 - c, toks), :], wgu[...]).astype(BF)
        dq_in.append(twin(dqs.at[at, :], dqt.at[at, :], 28 + g))
    for g in range(4):
        at = block(g, toks)
        mid = dot(hd[block(2 * g + c, toks), :], wgu[...])
        dq_in[g].wait_recv()
        dqm[at, :] = (mid + dqt[at, :].astype(F32)).astype(BF)
    query_sum = PlaneSum(
        net, dqm, lambda yx, p: (block(2 * yx[0] + yx[1], toks), block(p, half)), r.dqs3)
    query_sum.first()
    summing.run(lambda i, p, hops: hops == 1)
    summing.run(lambda i, p, hops: 1 < hops < zs)
    query_sum.second()
    summing.run(lambda i, p, hops: hops == zs and p == 0)
    dout, din = r.dout, r.din
    mine_at = lambda yx: block(2 * yx[0] + yx[1], rows)
    usem = r.usem
    units = [send(dout.at[mine_at(yx), :], din.at[:, lane_of((net.y, net.x))], usem, k, peer)
             for k, (yx, peer) in enumerate(zip(near, near_at))]
    din[:, lane_of((net.y, net.x))] = dout[mine_at((net.y, net.x)), :]
    summing.run(lambda i, p, hops: hops == zs and p > 0)
    back = r.full1

    def turned(h, g, sc, prod):
        return (-STEP_SIZE * h / sc - g * prod / (width * sc * sc * sc)).astype(BF)

    def wide_back():
        h, g = hsum[:, wide], grad[:, wide]
        prod = jnp.sum(-STEP_SIZE * h * g, axis=1, keepdims=True)
        back[own, wide] = turned(h, g, scale[0][:, :1], prod)

    def down_back():
        for copy in units:
            copy.wait_recv()
        hsum[:, dl] = dot_nt(din[...], r.sel[...])
        product = jnp.sum(-STEP_SIZE * hsum[:, dl] * grad[:, dl], axis=1, keepdims=True)
        r.sq[2] = jnp.broadcast_to(product, (rows, 128))
        twin(r.sq.at[2], r.sq.at[3], 7).wait_recv()
        prod = (r.sq[2] + r.sq[3])[:, :1]
        back[own, dl] = turned(hsum[:, dl], grad[:, dl], scale[1][:, :1], prod)

    placed, hp, hdn = r.placed, r.hp, r.hdn

    def place_sums():
        placed[...] = jnp.zeros_like(placed)
        hdn[...] = jnp.zeros_like(hdn)
        for k in range(2):
            to = pl.ds(pl.multiple_of((half // 2) * k + rows * net.g, rows), rows)
            to_up = pl.ds(pl.multiple_of(half + (half // 2) * k + rows * net.g, rows), rows)
            placed[to, :] = hgu8[k * rows:(k + 1) * rows, :]
            placed[to_up, :] = hgu8[128 + k * rows:128 + (k + 1) * rows, :]
            hdn[to, :] = hdn8[k * rows:(k + 1) * rows, :]
        hp[...] = placed[...].T
        r.taT[:, pl.ds(every, every)] = ab[...].T

    ag1 = all_gather(net, back, r.ag1, (wide_back, down_back), place_sums)

    def query_done(p, value):
        d_queries[:, p * half:(p + 1) * half] = value.astype(BF)
    query_sum.last(query_done)

    pq, tb, ec = r.pq, r.tb, r.ec
    pq[...] = dot_nt(xb[...], back[:, wide])

    def t_rows(at):
        g, u = gu[at, gl], gu[at, ul]
        p, q = pq[at, gl], pq[at, ul]
        sig = jax.nn.sigmoid(g)
        tb[at, :] = (q * g * sig + p * u * sig * (1.0 + g * (1.0 - sig))).astype(BF)
    by_rows(every, 32, t_rows)
    sp, sr, sb = r.sp, r.sr, r.sb
    second_out = []
    for k, at in enumerate((mine, theirs)):
        sp[at, :] = dot_nt(ab[at, :], back[:, dl]) + dot(tb[at, :], r.cb[...])
        second_out.append(twin(sp.at[at, :], sr.at[at, :], 8 + k))
    ec[...] = dot(eb[...], back[:, dl])
    r.taT[:, pl.ds(0, every)] = tb[...].T
    for copy, at in zip(second_out, (theirs, mine)):
        copy.wait_recv()
        sb[at, :] = (sp[at, :] + sr[at, :]).astype(BF)
    prow = 2 * rows
    dsw, dloc = r.dsw, r.dloc
    dloc[...] = (r.hdn[...] + dot(r.taT[:, pl.ds(0, every)], eb[...])
                 + dot(r.taT[:, pl.ds(every, every)], sb[...])).astype(BF)
    swaps = []
    for k in range(zs // 2):
        slot = (zs // 2) * c + k
        swaps.append(twin(dloc.at[block(2 * k + 1 - c, prow), :], dsw.at[slot], 10 + k))
        dsw[slot] = dloc[block(2 * k + c, prow), :]
    d_values[...] = -(sp[mine, :] + sr[mine, :])
    ec[...] += dot_nt(sb[...], r.cb[...])
    gub = r.gub

    def pull_rows(at):
        g, u, d = gu[at, gl], gu[at, ul], da[at, :]
        p, q, back_a = pq[at, gl], pq[at, ul], ec[at, :]
        sig = jax.nn.sigmoid(g)
        sneg = 1.0 - sig
        h = g * sig
        slope = sig * (1.0 + g * sneg)
        bend = sig * sneg * (2.0 + g * (1.0 - 2.0 * sig))
        pd = p * d
        gub[at, gl] = (back_a * u * slope + pd * u * bend + q * d * slope).astype(BF)
        gub[at, ul] = (back_a * h + pd * slope).astype(BF)
    by_rows(every, 32, pull_rows)

    pay2 = r.pay2

    def last_side():
        pay2[:, :outer] = (r.hp[:, :outer] + dot(r.xT[...], gub[:, :outer])).astype(BF)

    def last_block(zb, i):
        at = block(zb, zrows)
        pay2[at, inner] = (r.hp[at, inner] + dot(r.xT[at, :], gub[:, inner])).astype(BF)
        if i == 0:
            for copy in swaps:
                copy.wait_recv()
        for y in range(2):
            for x in range(2):
                pay2[block(4 * zb + 2 * y + x, rows), dl] = (
                    dsw[zb, y * rows:(y + 1) * rows, x * half:(x + 1) * half])

    def key_back():
        r.kp[...] = dot(dgu[...], back[:, wide])

    def key_back_second():
        r.kp[...] += dot_nt(gub[...], r.abb[...])
        r.kin = twin(r.kp.at[theirs, :], r.kr, 10 + zs // 2)

    last = r.last
    rs2 = reduce_scatter(net, pay2, r.rs2, last, last_block, last_side,
                         {0: key_back, 1: key_back_second})
    fin = r.fin
    fin[block(net.g, rows), :] = last[...].astype(BF)
    final = [send(fin.at[block(net.g, rows), :], fin.at[block(net.g, rows), :], r.fsem, k, peer)
             for k, peer in ((2, near_at[2]), (0, near_at[0]), (1, near_at[1]))]
    r.kin.wait_recv()
    d_keys[...] = r.kp[mine, :] + r.kr[...]
    for copy in final:
        copy.wait_recv()
    swap = twin(fin.at[block(1 - c, prow), wide], r.tw, 11 + zs // 2)
    lanes = block(c, half)
    others = block(1 - c, half)
    d_gate[:, lanes] = fin[block(c, prow), gl].astype(F32) * inverse
    d_up[:, lanes] = fin[block(c, prow), ul].astype(F32) * inverse
    for y in range(2):
        for x in range(2):
            g = 2 * y + x
            d_down[y * rows:(y + 1) * rows, x * half:(x + 1) * half] = (
                fin[g * rows:(g + 1) * rows, width:].astype(F32) * inverse)
    swap.wait_recv()
    d_gate[:, others] = r.tw[:, :half].astype(F32) * inverse
    d_up[:, others] = r.tw[:, half:].astype(F32) * inverse
    await_copy(net, r.sq.at[0], tsem, 5, 5)
    drain(done + slices + units + final)
    query_sum.finish()
    for finish in (rs0, ag1, rs2, summing.finish):
        finish()
    for p in range(2):
        plane_drain(net, qa, token_at, 0, p, r.qsem)
        plane_drain(net, oa, token_at, 0, p, r.osem)

    def drain_line(z):
        for zb in range(zs):
            for p in range(2):
                pass_drain(net, z, zb, p, gz_at(zb, p), line)
            if zb != z:
                await_copy(net, rz_at(z), xsem, (zb,), (zb,))
    at_each(net, drain_line)


def hand_over(*refs):
    for src, dst in zip(refs[:6], refs[6:]):
        dst[...] = src[...]


def fused_step(queries, key_tokens, values, out_grad, w_gate, w_up, w_down, zs, inverse):
    toks, width = queries.shape
    half, every, rows = width // 2, 2 * toks, width // (4 * zs)
    plane = 4 * every
    total = width + half
    side, main = lane_parts(total)
    unit = side[0].size
    f32 = lambda *shape: VM(shape, F32)
    bf = lambda *shape: VM(shape, BF)
    sems = lambda *shape: (DMA(shape), DMA(shape))
    both = lambda *shape: tuple(VM(shape + (part.size,), BF) for part in main)
    summed = dict(
        r1=both(zs, 2, rows), r2=both(zs, rows), zb=both(zs - 1, rows), zr=both(zs + 1, rows),
        s1=sems(zs, 2, 2), s2=sems(zs, 2), s3=sems(zs + 1, 2), pb=bf(4 * rows, 2 * unit),
        lo=(bf(zs - 1, 4 * rows, unit),) * 2, li=(bf(zs + 1, 4 * rows, unit),) * 2,
        ls=sems(zs + 1, 2),
        ps=dict(r1=bf(2, 2, rows, unit), r2=bf(2, rows, unit), s1=sems(2, 2), s2=sems(2)))
    spread = lambda depth: dict(
        z=sems(depth, 2, 2), o=sems(depth, 2, 2), f=sems(depth, 2))
    scratch = dict(
        kf=f32(toks, width), vf=f32(toks, width), wab=f32(width, width), wc=f32(half, width),
        wabt=f32(width, width), wct=f32(width, half), gu=f32(every, width), ep=f32(every, width),
        er=f32(every, width), da=f32(every, half), grad=f32(rows, total), hsum=f32(rows, total),
        last=f32(rows, total), sq=f32(4, rows, 128), scale=f32(2, rows, 128),
        hgu=f32(256, plane), dact=f32(128, plane), hdn8=f32(128, width), hgu8=f32(256, width),
        pd=f32(width, 128), placed=f32(width, width), hp=f32(width, width), hdn=f32(half, width),
        pq=f32(every, width), ec=f32(every, half), sp=f32(every, width), sr=f32(every, width),
        kp=f32(every, width), kr=f32(toks, width),
        xb=bf(every, width), qa=bf(plane, width), oa=bf(plane, width), abb=bf(width, width),
        cb=bf(half, width), ab=bf(every, half), eb=bf(every, width), dgu=bf(every, width),
        dguT=bf(width, every), eT=bf(width, every), xT=bf(width, every), hd=bf(256, plane),
        hdT=bf(plane, 256), hact=bf(128, plane), rzT=bf(128, width), tb=bf(every, half),
        sel=bf(half, 512), wgu=bf(256, width), gz=bf(zs * rows, width), rz=bf(width, 128),
        dsl=bf(rows, 512), dout=bf(4 * rows, 128), din=bf(rows, 512), dqs=bf(4 * toks, width),
        dqm=bf(4 * toks, width), dqt=bf(4 * toks, width),
        ldo=bf(zs - 1, 4 * rows, 128), ldi=bf(zs + 1, 4 * rows, 128),
        lgo0=bf(zs - 1, rows, half), lgi0=bf(zs + 1, rows, half),
        lgo1=bf(zs - 1, rows, half), lgi1=bf(zs + 1, rows, half),
        sb=bf(every, width), taT=bf(half, 2 * every), gub=bf(every, width), dloc=bf(half, width),
        dsw=bf(zs, 2 * rows, width), pay0=bf(width, total), pay2=bf(width, total),
        full1=bf(width, total), fin=bf(4 * rows, total), tw=bf(2 * rows, width),
        rs0=summed, rs2=summed, ag1=spread(zs), fsem=sems(3), qsem=spread(1), osem=spread(1),
        line=spread(zs), lsem=sems(zs + 1, 3), xsem=sems(zs), ssem=sems(3), usem=sems(3),
        dqs3=dict(r1=bf(2, 2, toks, half), r2=bf(2, toks, half), s1=sems(2, 2), s2=sems(2)),
        tsem=sems(32), ld=DMA((7,)))
    shapes, tree = jax.tree.flatten(scratch)
    token = jax.ShapeDtypeStruct((toks, width), F32)
    weight = jax.ShapeDtypeStruct((2 * rows, width), F32)
    results = pl.pallas_call(
        functools.partial(step_body, zs, tree, inverse),
        out_shape=(jax.ShapeDtypeStruct((toks, width), BF), token, token, weight, weight, weight),
        in_specs=[pl.BlockSpec(memory_space=pltpu.HBM)] * 7,
        out_specs=[pl.BlockSpec(memory_space=VM)] * 6,
        scratch_shapes=shapes,
        compiler_params=pltpu.CompilerParams(
            collective_id=0, has_side_effects=True, vmem_limit_bytes=52 * 1024 * 1024),
    )(*(pltpu.with_memory_space_constraint(x, pltpu.HBM) for x in (
        queries, key_tokens, values, out_grad, w_gate, w_up, w_down)))
    return pl.pallas_call(
        hand_over,
        out_shape=tuple(jax.ShapeDtypeStruct(item.shape, item.dtype) for item in results),
        in_specs=[pl.BlockSpec(memory_space=VM)] * 6,
        out_specs=[pl.BlockSpec(memory_space=VM)] * 6,
        compiler_params=pltpu.CompilerParams(vmem_limit_bytes=8 * 1024 * 1024),
    )(*results)


def matmul(left, right):
    return dot(left.astype(BF), right.astype(BF))


def key_grad(w_gate, w_up, w_down, key_rows, value_rows):
    hidden_gate = matmul(key_rows, w_gate)
    hidden_up = matmul(key_rows, w_up)
    sig = jax.nn.sigmoid(hidden_gate)
    active = hidden_gate * sig * hidden_up
    error = matmul(active, w_down) - value_rows
    d_active = matmul(error, w_down.T)
    d_hup = d_active * hidden_gate * sig
    d_hgate = d_active * hidden_up * sig * (1.0 + hidden_gate * (1.0 - sig))
    return (matmul(d_hgate.T, key_rows), matmul(d_hup.T, key_rows), matmul(error.T, active))


def query_grad(fast_t, query_rows, grad_rows):
    gate_t, up_t, down_t = fast_t
    hidden_gate = dot(query_rows, gate_t.T)
    hidden_up = dot(query_rows, up_t.T)
    sig = jax.nn.sigmoid(hidden_gate)
    active = (hidden_gate * sig * hidden_up).astype(BF)
    d_active = dot(grad_rows, down_t)
    d_hup = (d_active * hidden_gate * sig).astype(BF)
    d_hgate = (d_active * hidden_up * sig * (1.0 + hidden_gate * (1.0 - sig))).astype(BF)
    d_rows = (dot(d_hgate, gate_t) + dot(d_hup, up_t)).astype(BF)
    return (d_rows, active, d_hgate, d_hup)


def general_step(queries, key_tokens, values, out_grad, w_gate, w_up, w_down, inverse):
    gs, toks = lax.axis_size("grp"), lax.axis_size("tok")
    full_width = w_gate.shape[0]
    rows = 3 * full_width // (gs * toks)
    me = lax.axis_index("tok") * gs + lax.axis_index("grp")

    def reduce_units(x):
        y = x.reshape(toks, gs * rows, full_width)
        y = lax.psum_scatter(y, "tok", scatter_dimension=0, tiled=True)[0]
        return lax.psum_scatter(y.reshape(gs, rows, full_width), "grp", scatter_dimension=0, tiled=True)[0]

    def gather_units(y):
        full = lax.all_gather(lax.all_gather(y, "grp"), "tok").reshape(3, full_width, full_width)
        return full[0], full[1], full[2]

    local_grad, pullback = jax.vjp(key_grad, w_gate, w_up, w_down, key_tokens, values)
    grad = reduce_units(jnp.stack(local_grad))
    scale = jnp.sqrt(jnp.sum(grad * grad, axis=1, keepdims=True) / full_width + EPSILON)
    weights = jnp.concatenate((w_gate, w_up, w_down), axis=1)
    mine = lax.dynamic_slice_in_dim(weights, me * rows, rows, 1).T
    fast_t = gather_units((mine - STEP_SIZE * grad / scale).astype(BF))
    d_queries, active, d_hgate, d_hup = query_grad(fast_t, queries, out_grad)
    query_part = reduce_units(
        jnp.stack((dot(d_hgate.T, queries), dot(d_hup.T, queries), dot(out_grad.T, active))))
    product = jnp.sum(-STEP_SIZE * query_part * grad, axis=1, keepdims=True)
    cot = (
        -STEP_SIZE * query_part / scale - grad * product / (full_width * scale * scale * scale)
    ).astype(BF)
    second = pullback(tuple(item.astype(F32) for item in gather_units(cot)))
    plain = (dot(queries.T, d_hgate), dot(queries.T, d_hup), dot(active.T, out_grad))
    combined = jnp.stack(tuple(left + right for left, right in zip(plain, second[:3])))
    combined = combined.reshape(3, toks, full_width // toks, full_width).transpose(1, 0, 2, 3)
    summed = lax.all_gather(reduce_units(combined).astype(BF), "grp").astype(F32) * inverse
    summed = summed.reshape(3, full_width // toks, full_width)
    return (d_queries, second[3], second[4], summed[0], summed[1], summed[2])


def on_device(*arrays):
    gs, toks = lax.axis_size("grp"), lax.axis_size("tok")
    tokens, width = arrays[0].shape
    inverse = 1.0 / (tokens * gs * toks)
    zs = toks // 2
    fits = gs == 4 and toks % 4 == 0 and zs <= 4
    if fits and width % (64 * zs) == 0 and 2 * width <= 512 * zs and width % 256 == 0 and tokens % 128 == 0:
        return fused_step(*arrays, zs, inverse)
    return general_step(*arrays, inverse)


def solution(mesh):
    token = P(("grp", "tok"), None)
    return jax.shard_map(
        on_device,
        mesh=mesh,
        in_specs=(token, token, token, token, P(), P(), P()),
        out_specs=(token, token, token, P("tok", None), P("tok", None), P("tok", None)),
        check_vma=False,
    )
```

```python
import functools
from types import SimpleNamespace as Names

import jax
import jax.numpy as jnp
from jax import lax
from jax.experimental import pallas as pl
from jax.experimental.pallas import tpu as pltpu
from jax.sharding import PartitionSpec as P

STEP_SIZE = 0.02
EPSILON = 1e-06
MESH = pl.DeviceIdType.MESH
BF = jnp.bfloat16
F32 = jnp.float32
VM = pltpu.VMEM
DMA = pltpu.SemaphoreType.DMA


def dot(left, right):
    return jnp.dot(left, right, preferred_element_type=F32)


def dot_nt(left, right):
    return lax.dot_general(left, right, (((1,), (1,)), ((), ())), preferred_element_type=F32)


def block(index, size):
    return pl.ds(pl.multiple_of(index * size, size), size)


def lane_parts(width):
    unit = 128 * max(1, width // 1152)
    cut = width - 128 * ((width // 128 - 2 * (unit // 128)) // 2)
    return ((pl.ds(0, unit), pl.ds(unit, unit)),
            (pl.ds(2 * unit, cut - 2 * unit), pl.ds(cut, width - cut)))


class Net:
    def __init__(self, zs, rows, width):
        g, t = lax.axis_index("grp"), lax.axis_index("tok")
        self.zs, self.rows = zs, rows
        self.g, self.z, self.c = g, t // 2, lax.rem(t, 2)
        self.y, self.x = g // 2, lax.rem(g, 2)
        self.t = t
        self.outer, self.lanes = lane_parts(width)
        cut = 128 * ((width // 128 + 1) // 2)
        self.parts = (pl.ds(0, cut), pl.ds(cut, width - cut))
        self.twin = (g, 2 * self.z + 1 - self.c)

    def flip(self, *directions):
        y, x = self.y, self.x
        for a in directions:
            x = x + (1 - a) * (1 - 2 * x)
            y = y + a * (1 - 2 * y)
        return y, x

    def turn(self, n):
        return lax.rem(n + self.c, 2)

    def side(self, a):
        y, x = self.flip(a)
        return (2 * y + x, self.t)

    def across(self):
        y, x = self.flip(0, 1)
        return (2 * y + x, self.t)

    def at_z(self, z):
        return (self.g, 2 * z + self.c)

    def pick(self, table):
        value = table[0]
        for z in range(1, self.zs):
            value = jnp.where(self.z == z, table[z], value)
        return value

    def chunk(self, zb, yx):
        return block(4 * zb + 2 * yx[0] + yx[1], self.rows)

    def greet(self, work):
        barrier = pltpu.get_barrier_semaphore()
        peers = [self.twin, self.side(0), self.side(1), self.across()]
        for d in range(1, self.zs):
            peers.append(self.at_z(lax.rem(self.z + d, self.zs)))
        for peer in peers:
            pl.semaphore_signal(barrier, inc=1, device_id=peer, device_id_type=MESH)
        work()
        pl.semaphore_wait(barrier, len(peers))


def send(src, dst, sems, at, peer, there=None):
    copy = pltpu.make_async_remote_copy(
        src_ref=src, dst_ref=dst, send_sem=sems[0].at[at],
        recv_sem=sems[1].at[at if there is None else there],
        device_id=peer, device_id_type=MESH,
    )
    copy.start()
    return copy


def await_copy(net, ref, sems, at, there=None):
    copy = pltpu.make_async_remote_copy(
        src_ref=ref, dst_ref=ref, send_sem=sems[0].at[at if there is None else there],
        recv_sem=sems[1].at[at], device_id=net.twin, device_id_type=MESH,
    )
    if there is None:
        copy.wait_recv()
    else:
        copy.wait_send()


def sum_order(zs, z):
    def key(zb):
        hops = z if zb > z else zs - 1 - z
        return (zb == z, hops, -abs(zb - z))
    return sorted(range(zs), key=key)


def spread_order(zs, z):
    return sorted(range(zs), key=lambda zb: (abs(zb - z), (zb > z) == (2 * z < zs)))


def reduce_scatter(net, pay, s, total, produce, produce_side, fillers, ready=None):
    zs = net.zs
    orders = [sum_order(zs, z) for z in range(zs)]
    blocks = [net.pick([orders[z][i] for z in range(zs)]) for i in range(zs)]
    first, second = {}, {}
    unit = s.pb.shape[-1] // 2

    def line_piece(p):
        def cut(zb):
            return pay[pl.ds(4 * net.rows * zb, 4 * net.rows), net.outer[p]]

        def own(value):
            s.pb[:, unit * p:unit * (p + 1)] = value.astype(BF)
        return cut, s.lo[p], s.li[p], own

    line = LineSum(net, (line_piece(0), line_piece(1)), s.ls)
    plane = PlaneSum(net, s.pb, lambda yx, p: (
        block(2 * yx[0] + yx[1], net.rows), pl.ds(unit * p, unit)), s.ps)

    def when_inside(inside, body):
        inner = (net.z > 0) & (net.z < zs - 1)
        pl.when(inner if inside else jnp.logical_not(inner))(body)

    def start_first(i, k):
        for p in (1, 0):
            a = net.turn(p + i)
            yx = net.flip(a, 1 - a) if k == 0 else net.flip(a)
            first[i, p, k] = send(
                pay.at[net.chunk(blocks[i], yx), net.lanes[p]], s.r1[p].at[i, k],
                s.s1, (i, p, k), net.side(a))

    def start_second(i):
        for p in (1, 0):
            a = net.turn(p + i)
            first[i, p, 0].wait_recv()
            at = (net.chunk(blocks[i], net.flip(1 - a)), net.lanes[p])
            pay[at] = (pay[at].astype(F32) + s.r1[p][i, 0].astype(F32)).astype(BF)
            second[i, p] = send(pay.at[at], s.r2[p].at[i], s.s2, (i, p), net.side(1 - a))

    def along(z, i):
        zb = orders[z][i]
        for p in (1, 0):
            first[i, p, 1].wait_recv()
            second[i, p].wait_recv()
            at = (net.chunk(zb, (net.y, net.x)), net.lanes[p])
            value = (pay[at].astype(F32) + s.r1[p][i, 1].astype(F32)
                     + s.r2[p][i].astype(F32))
            slots = []
            if zb >= z and z > 0:
                slots.append(i)
            if zb <= z and z < zs - 1:
                slots.append(i if zb < z else zs)
            for slot in slots:
                await_copy(net, s.zr[p].at[slot], s.s3, (slot, p))
                value = value + s.zr[p][slot].astype(F32)
            if zb == z:
                total[:, net.lanes[p]] = value
                if p == 1 and ready is not None:
                    ready()
            else:
                s.zb[p][i] = value.astype(BF)
                nxt = z + 1 if zb > z else z - 1
                slot = orders[nxt].index(zb) if nxt != zb or zb > z else zs
                send(s.zb[p].at[i], s.zr[p].at[slot], s.s3, (i, p), net.at_z(nxt),
                     (slot, p))

    last = 0
    steps = [{} for _ in range(zs)]
    for z in range(zs):
        for i, zb in enumerate(orders[z]):
            hops = 0 if zb == z else z if zb > z else zs - 1 - z
            when = zs + 2 if zb == z else i + 2 + min(hops, 1)
            steps[z].setdefault(when, []).append(i)
            last = max(last, when)
    for i in range(last + 1):
        if i < zs:
            produce(blocks[i], i)
            start_first(i, 0)
        if i == 0:
            produce_side()
            line.run(lambda n, p, hops: hops == 0)
        if 1 <= i <= zs:
            start_second(i - 1)
        if i < zs:
            start_first(i, 1)
        line.run(lambda n, p, hops: 0 < hops < zs and max(n + 1, 2) == i)
        for inside in (True, False):
            if i == (zs - 1 if inside else zs):
                line.run(lambda n, p, hops: hops == zs, inside)
                when_inside(inside, plane.first)
        for z in range(zs):
            if i in steps[z]:
                @pl.when(net.z == z)
                def _():
                    for k in steps[z][i]:
                        along(z, k)
        for inside in (True, False):
            if i == (zs if inside else zs + 1):
                when_inside(inside, plane.second)
        if i in fillers:
            fillers[i]()
    def plane_done(p, value):
        total[:, net.outer[p]] = value
    plane.last(plane_done)

    def finish():
        drain([*first.values(), *second.values()])
        plane.finish()
        line.finish()
        for i in range(zs - 1):
            for p in range(2):
                await_copy(net, s.zb[p].at[i], s.s3, (i, p), (i, p))
    return finish


def plane_own(net, ref, at, i, p, k, s):
    ref = ref.at[at((net.y, net.x), p)]
    return send(ref, ref, s.o, (i, p, k), net.side(net.turn(p + i + k)))


def plane_relay(net, ref, at, i, p, s):
    a = net.turn(p + i)
    ref = ref.at[at(net.flip(a), p)]
    await_copy(net, ref, s.o, (i, p, 0))
    return send(ref, ref, s.f, (i, p), net.side(1 - a))


def plane_rest(net, ref, at, i, p, s):
    a = net.turn(p + i)
    await_copy(net, ref.at[at(net.flip(1 - a), p)], s.o, (i, p, 1))
    await_copy(net, ref.at[at(net.flip(0, 1), p)], s.f, (i, p))


def plane_drain(net, ref, at, i, p, s):
    ref = ref.at[at((net.y, net.x), p)]
    for k in range(2):
        await_copy(net, ref, s.o, (i, p, k), (i, p, k))
    await_copy(net, ref, s.f, (i, p), (i, p))


def at_each(net, body):
    for z in range(net.zs):
        @pl.when(net.z == z)
        def _():
            body(z)


def onward(zs, z, zb):
    return [(k, other) for k, other in enumerate((z - 1, z + 1))
            if 0 <= other < zs and (zb == z or (zb > z) == (other < z))]


def pass_on(net, z, zb, p, ref, s):
    for k, other in onward(net.zs, z, zb):
        send(ref, ref, s.z, (zb, p, k), net.at_z(other), (zb, p, 0))


def pass_drain(net, z, zb, p, ref, s):
    for k, other in onward(net.zs, z, zb):
        await_copy(net, ref, s.z, (zb, p, 0), (zb, p, k))


def all_gather(net, full, s, parts, idle):
    zs = net.zs
    place = lambda zb: lambda yx, p: (net.chunk(zb, yx), net.parts[p])
    mine = lambda zb, p: full.at[place(zb)((net.y, net.x), p)]

    for p in range(2):
        parts[p]()
        at_each(net, lambda z: pass_on(net, z, z, p, mine(z, p), s))
        plane_own(net, full, place(net.z), 0, p, 0, s)
    for p in range(2):
        plane_own(net, full, place(net.z), 0, p, 1, s)

    def rest(z):
        order = spread_order(zs, z)
        for i in range(1, zs):
            for p in range(2):
                await_copy(net, mine(order[i], p), s.z, (order[i], p, 0))
                pass_on(net, z, order[i], p, mine(order[i], p), s)
                plane_own(net, full, place(order[i]), i, p, 0, s)
            for p in range(2):
                plane_own(net, full, place(order[i]), i, p, 1, s)
            for p in range(2):
                plane_relay(net, full, place(order[i - 1]), i - 1, p, s)
        for p in range(2):
            plane_relay(net, full, place(order[zs - 1]), zs - 1, p, s)

    def arrive(z):
        for i, zb in enumerate(spread_order(zs, z)):
            for p in range(2):
                plane_rest(net, full, place(zb), i, p, s)
    at_each(net, rest)
    idle()
    at_each(net, arrive)

    def finish():
        def go(z):
            order = spread_order(zs, z)
            for i in range(zs):
                for p in range(2):
                    pass_drain(net, z, order[i], p, mine(order[i], p), s)
                    plane_drain(net, full, place(order[i]), i, p, s)
        at_each(net, go)
    return finish


class PlaneSum:
    def __init__(self, net, ref, at, s):
        self.net, self.ref, self.at, self.s = net, ref, at, s

    def first(self):
        net, s = self.net, self.s
        for k in range(2):
            for p in range(2):
                yx = net.flip(p, 1 - p) if k == 0 else net.flip(p)
                send(self.ref.at[self.at(yx, p)], s.r1.at[p, k], s.s1, (p, k), net.side(p))

    def second(self):
        net, s = self.net, self.s
        for p in range(2):
            await_copy(net, s.r1.at[p, 0], s.s1, (p, 0))
            at = self.at(net.flip(1 - p), p)
            self.ref[at] = (self.ref[at].astype(F32) + s.r1[p, 0].astype(F32)).astype(BF)
            send(self.ref.at[at], s.r2.at[p], s.s2, (p,), net.side(1 - p))

    def last(self, done):
        net, s = self.net, self.s
        for p in range(2):
            await_copy(net, s.r1.at[p, 1], s.s1, (p, 1))
            await_copy(net, s.r2.at[p], s.s2, (p,))
            value = self.ref[self.at((net.y, net.x), p)].astype(F32)
            done(p, value + s.r1[p, 1].astype(F32) + s.r2[p].astype(F32))

    def finish(self):
        net, s = self.net, self.s
        for p in range(2):
            for k in range(2):
                await_copy(net, s.r1.at[p, k], s.s1, (p, k), (p, k))
            await_copy(net, s.r2.at[p], s.s2, (p,), (p,))


class LineSum:
    def __init__(self, net, pieces, sems):
        self.net, self.pieces, self.sems = net, pieces, sems
        self.orders = [sum_order(net.zs, z) for z in range(net.zs)]

    def hops(self, z, i):
        zb = self.orders[z][i]
        return self.net.zs if zb == z else z if zb > z else self.net.zs - 1 - z

    def move(self, z, i, p):
        net, zs = self.net, self.net.zs
        cut, out, inn, own = self.pieces[p]
        zb = self.orders[z][i]
        value = cut(zb)
        slots = []
        if zb >= z and z > 0:
            slots.append(i)
        if zb <= z and z < zs - 1:
            slots.append(i if zb < z else zs)
        for slot in slots:
            await_copy(net, inn.at[slot], self.sems, (slot, p))
            value = value + inn[slot].astype(F32)
        if zb == z:
            own(value)
            return
        out[i] = value.astype(BF)
        nxt = z + 1 if zb > z else z - 1
        slot = self.orders[nxt].index(zb) if nxt != zb or zb > z else zs
        send(out.at[i], inn.at[slot], self.sems, (i, p), net.at_z(nxt), (slot, p))

    def run(self, chosen, inside=None):
        def go(z):
            if inside is not None and inside != (0 < z < self.net.zs - 1):
                return
            for i in range(self.net.zs):
                for p in range(len(self.pieces)):
                    if chosen(i, p, self.hops(z, i)):
                        self.move(z, i, p)
        at_each(self.net, go)

    def finish(self):
        for i in range(self.net.zs - 1):
            for p, piece in enumerate(self.pieces):
                await_copy(self.net, piece[1].at[i], self.sems, (i, p), (i, p))


def drain(copies):
    for copy in copies:
        copy.wait_send()


def by_rows(count, step, body):
    def run(i, carry):
        body(pl.ds(pl.multiple_of(i * step, step), step))
        return carry
    lax.fori_loop(0, count // step, run, 0)


def named(tree):
    return Names(**{k: named(v) if isinstance(v, dict) else v for k, v in tree.items()})


def step_body(zs, tree, inverse, *refs):
    r = Names(**jax.tree.unflatten(tree, refs[13:]))
    for key, value in vars(r).items():
        if isinstance(value, dict):
            setattr(r, key, named(value))
    (queries, keys, values, out_grad, w_gate, w_up, w_down) = refs[:7]
    (d_queries, d_keys, d_values, d_gate, d_up, d_down) = refs[7:13]
    toks, width = queries.shape
    half = width // 2
    every = 2 * toks
    rows = width // (4 * zs)
    zrows = 4 * rows
    net = Net(zs, rows, width + half)
    c = net.c
    mine, theirs = block(c, toks), block(1 - c, toks)
    gl, ul, dl = pl.ds(0, half), pl.ds(half, half), pl.ds(width, half)
    wide = pl.ds(0, width)
    hid = block(c, half)

    token_at = lambda yx, p: (block(2 * (2 * yx[0] + yx[1]) + c, toks), block(p, half))
    spot = block(2 * net.g + c, toks)
    loads = Names()
    loads.k, loads.a, loads.b, loads.c, loads.v, loads.q, loads.o = [
        pltpu.make_async_copy(src, dst, r.ld.at[i]) for i, (src, dst) in enumerate((
            (keys, r.kf), (w_gate.at[:, hid], r.wab.at[:, gl]), (w_up.at[:, hid], r.wab.at[:, ul]),
            (w_down.at[hid, :], r.wc), (values, r.vf), (queries, r.qa.at[spot, :]),
            (out_grad, r.oa.at[spot, :])))]
    for load in vars(loads).values():
        load.start()
    xb, gu, ab, eb = r.xb, r.gu, r.ab, r.eb

    def own_hidden():
        loads.k.wait()
        xb[mine, :] = r.kf[...].astype(BF)
        loads.a.wait()
        loads.b.wait()
        r.abb[...] = r.wab[...].astype(BF)
        gu[mine, :] = dot(xb[mine, :], r.abb[...])
        loads.c.wait()
        r.cb[...] = r.wc[...].astype(BF)
        loads.q.wait()
        loads.o.wait()
        loads.v.wait()
    net.greet(own_hidden)
    tsem = r.tsem
    done = []

    def twin(src, dst, k):
        copy = send(src, dst, tsem, k, net.twin)
        done.append(copy)
        return copy

    keys_in = twin(xb.at[mine, :], xb.at[mine, :], 0)
    qa, oa = r.qa, r.oa
    for ref, sems in ((qa, r.qsem), (oa, r.osem)):
        for p in range(2):
            plane_own(net, ref, token_at, 0, p, 0, sems)
    keys_in.wait_recv()
    gu[theirs, :] = dot(xb[theirs, :], r.abb[...])

    def active_rows(at):
        g, u = gu[at, gl], gu[at, ul]
        ab[at, :] = (g * jax.nn.sigmoid(g) * u).astype(BF)
    by_rows(every, 32, active_rows)

    ep, er = r.ep, r.er
    ep[mine, :] = dot(ab[mine, :], r.cb[...]) - r.vf[...]
    e_out = [twin(ep.at[mine, :], er.at[mine, :], 3)]
    ep[theirs, :] = dot(ab[theirs, :], r.cb[...])
    e_out.append(twin(ep.at[theirs, :], er.at[theirs, :], 4))
    for copy, at in zip(e_out, (theirs, mine)):
        copy.wait_recv()
        eb[at, :] = (ep[at, :] + er[at, :]).astype(BF)
    da, dgu = r.da, r.dgu
    da[...] = dot_nt(eb[...], r.cb[...])

    def d_rows(at):
        g, u, d = gu[at, gl], gu[at, ul], da[at, :]
        sig = jax.nn.sigmoid(g)
        dgu[at, ul] = (d * g * sig).astype(BF)
        dgu[at, gl] = (d * u * sig * (1.0 + g * (1.0 - sig))).astype(BF)
    by_rows(every, 32, d_rows)
    r.dguT[...] = dgu[...].T
    r.eT[...] = eb[...].T

    pay = r.pay0

    outer = net.lanes[0].start
    inner = pl.ds(outer, width - outer)

    def key_side():
        pay[:, :outer] = dot(r.dguT[...], xb[:, :outer]).astype(BF)

    def key_block(zb, i):
        at = block(zb, zrows)
        pay[at, inner] = dot(r.dguT[at, :], xb[:, inner]).astype(BF)
        pay[at, dl] = dot(r.eT[at, :], ab[...]).astype(BF)

    def turn_weights():
        r.wabt[...] = r.wab[...].T
        r.wct[...] = r.wc[...].T

    def to_twin(ref, k):
        return [twin(ref.at[block(2 * g + c, toks), :], ref.at[block(2 * g + c, toks), :], k + g)
                for g in range(4)]

    def select_lanes():
        h = lax.broadcasted_iota(jnp.int32, (half, 512), 0)
        lane = lax.broadcasted_iota(jnp.int32, (half, 512), 1)
        g, l = lane // 128, lane % 128
        hit = (h == (half // 2) * (l // rows) + rows * g + l % rows) & (l < 2 * rows)
        r.sel[...] = jnp.where(hit, 1.0, 0.0).astype(BF)
        r.wgu[...] = jnp.zeros((256, width), BF)

    def turn_keys():
        r.xT[...] = xb[...].T

    def turn_arrays():
        turn_weights()
        select_lanes()
        turn_keys()

    grad = r.grad

    def down_norm():
        squares = jnp.sum(grad[:, dl] * grad[:, dl], axis=1, keepdims=True)
        r.sq[0] = jnp.broadcast_to(squares, (rows, 128))
        send(r.sq.at[0], r.sq.at[1], tsem, 5, net.twin)

    rs0 = reduce_scatter(net, pay, r.rs0, grad, key_block, key_side,
                         {0: turn_arrays},
                         down_norm)

    own = net.chunk(net.z, (net.y, net.x))
    scale_of = lambda sq: jnp.sqrt(sq / width + EPSILON)
    scale = r.scale

    gz, rz = r.gz, r.rz
    line = r.line
    gz_at = lambda zb, p: gz.at[pl.ds(rows * zb, rows), pl.ds(half * p, half)]
    rz_at = lambda zb: rz.at[pl.ds(zrows * zb, zrows), :]
    g = grad[:, wide]
    sc = scale_of(jnp.sum(g * g, axis=1, keepdims=True))
    scale[0] = jnp.broadcast_to(sc, (rows, 128))
    gz[block(net.z, rows), :] = (r.wabt[own, :] - STEP_SIZE * g / sc).astype(BF)
    at_each(net, lambda z: [pass_on(net, z, z, p, gz_at(z, p), line) for p in range(2)])
    await_copy(net, r.sq.at[1], tsem, 5)
    sc = scale_of((r.sq[0] + r.sq[1])[:, :1])
    scale[1] = jnp.broadcast_to(sc, (rows, 128))
    down = (r.wct[own, :] - STEP_SIZE * grad[:, dl] / sc).astype(BF)
    r.dsl[...] = dot(down, r.sel[...]).astype(BF)
    ssem = r.ssem
    near = [net.flip(0), net.flip(1), net.flip(0, 1)]
    near_at = [net.side(0), net.side(1), net.across()]
    lane_of = lambda yx: block(2 * yx[0] + yx[1], 128)
    rz[own, :] = r.dsl[:, lane_of((net.y, net.x))]
    slices = [send(r.dsl.at[:, lane_of(yx)], rz.at[own, :], ssem, k, peer)
              for k, (yx, peer) in enumerate(zip(near, near_at))]
    for ref, sems in ((qa, r.qsem), (oa, r.osem)):
        for p in range(2):
            plane_relay(net, ref, token_at, 0, p, sems)
        for p in range(2):
            plane_own(net, ref, token_at, 0, p, 1, sems)
    xsem = r.xsem

    def direct(z):
        for other in range(zs):
            if other != z:
                send(rz_at(z), rz_at(z), xsem, (other,), net.at_z(other), (z,))
    def gather_line(first, last):
        def go(z):
            for zb in spread_order(zs, z)[first:last]:
                for p in range(2):
                    await_copy(net, gz_at(zb, p), line.z, (zb, p, 0))
                    pass_on(net, z, zb, p, gz_at(zb, p), line)
            if last == zs:
                for zb in spread_order(zs, z)[1:]:
                    await_copy(net, rz_at(zb), xsem, (zb,))
        at_each(net, go)

    gather_line(1, 2)
    for copy in slices:
        copy.wait_recv()
    at_each(net, direct)
    gather_line(2, 3)
    for p in range(2):
        plane_rest(net, qa, token_at, 0, p, r.qsem)
    q_in = to_twin(qa, 20)
    gather_line(3, zs)

    wgu, hgu, dact, hd, hact = r.wgu, r.hgu, r.dact, r.hd, r.hact
    wgu[:2 * rows, :] = gz[:2 * rows, :]
    wgu[128:128 + 2 * rows, :] = gz[2 * rows:, :]
    for copy in q_in:
        copy.wait_recv()
    for p in range(2):
        plane_rest(net, oa, token_at, 0, p, r.osem)
    o_in = to_twin(oa, 24)
    hgu[...] = dot_nt(wgu[...], qa[...])
    r.rzT[...] = rz[...].T
    for copy in o_in:
        copy.wait_recv()
    dact[...] = dot_nt(r.rzT[...], oa[...])

    def query_rows(at):
        up = pl.ds(pl.multiple_of(at.start + 128, 16), 16)
        g, u, d = hgu[at, :], hgu[up, :], dact[at, :]
        sig = jax.nn.sigmoid(g)
        hact[at, :] = (g * sig * u).astype(BF)
        hd[up, :] = (d * g * sig).astype(BF)
        hd[at, :] = (d * u * sig * (1.0 + g * (1.0 - sig))).astype(BF)
    by_rows(128, 16, query_rows)
    hsum = r.hsum
    hdn8, hgu8 = r.hdn8, r.hgu8
    hdn8[...] = dot(hact[...], oa[...])
    r.pd[...] = hdn8[...].T

    def own_down(value):
        r.dout[...] = value.astype(BF)

    def own_wide(p):
        def store(value):
            hsum[:, half * p:half * (p + 1)] = value
        return store

    def wide_cut(p):
        return lambda zb: hgu8[pl.ds(rows * zb + (128 - 2 * rows) * (zb // 2), rows),
                               half * p:half * (p + 1)]

    pieces = (
        (lambda zb: r.pd[zrows * zb:zrows * (zb + 1), :], r.ldo, r.ldi, own_down),
        (wide_cut(0), r.lgo0, r.lgi0, own_wide(0)),
        (wide_cut(1), r.lgo1, r.lgi1, own_wide(1)),
    )
    summing = LineSum(net, pieces, r.lsem)
    summing.run(lambda i, p, hops: hops == 0 and i == 0 and p == 0)
    hgu8[...] = dot(hd[...], qa[...])
    summing.run(lambda i, p, hops: hops == 0 and i + p > 0)
    r.hdT[...] = hd[...].T
    hd = r.hdT
    dqs, dqm, dqt = r.dqs, r.dqm, r.dqt
    dq_in = []
    for g in range(4):
        at = block(g, toks)
        dqs[at, :] = dot(hd[block(2 * g + 1 - c, toks), :], wgu[...]).astype(BF)
        dq_in.append(twin(dqs.at[at, :], dqt.at[at, :], 28 + g))
    for g in range(4):
        at = block(g, toks)
        mid = dot(hd[block(2 * g + c, toks), :], wgu[...])
        dq_in[g].wait_recv()
        dqm[at, :] = (mid + dqt[at, :].astype(F32)).astype(BF)
    query_sum = PlaneSum(
        net, dqm, lambda yx, p: (block(2 * yx[0] + yx[1], toks), block(p, half)), r.dqs3)
    query_sum.first()
    summing.run(lambda i, p, hops: hops == 1)
    summing.run(lambda i, p, hops: 1 < hops < zs)
    query_sum.second()
    summing.run(lambda i, p, hops: hops == zs and p == 0)
    dout, din = r.dout, r.din
    mine_at = lambda yx: block(2 * yx[0] + yx[1], rows)
    usem = r.usem
    units = [send(dout.at[mine_at(yx), :], din.at[:, lane_of((net.y, net.x))], usem, k, peer)
             for k, (yx, peer) in enumerate(zip(near, near_at))]
    din[:, lane_of((net.y, net.x))] = dout[mine_at((net.y, net.x)), :]
    summing.run(lambda i, p, hops: hops == zs and p > 0)
    back = r.full1

    def turned(h, g, sc, prod):
        return (-STEP_SIZE * h / sc - g * prod / (width * sc * sc * sc)).astype(BF)

    def wide_back():
        h, g = hsum[:, wide], grad[:, wide]
        prod = jnp.sum(-STEP_SIZE * h * g, axis=1, keepdims=True)
        back[own, wide] = turned(h, g, scale[0][:, :1], prod)

    def down_back():
        for copy in units:
            copy.wait_recv()
        hsum[:, dl] = dot_nt(din[...], r.sel[...])
        product = jnp.sum(-STEP_SIZE * hsum[:, dl] * grad[:, dl], axis=1, keepdims=True)
        r.sq[2] = jnp.broadcast_to(product, (rows, 128))
        twin(r.sq.at[2], r.sq.at[3], 7).wait_recv()
        prod = (r.sq[2] + r.sq[3])[:, :1]
        back[own, dl] = turned(hsum[:, dl], grad[:, dl], scale[1][:, :1], prod)

    placed, hp, hdn = r.placed, r.hp, r.hdn

    def place_sums():
        placed[...] = jnp.zeros_like(placed)
        hdn[...] = jnp.zeros_like(hdn)
        for k in range(2):
            to = pl.ds(pl.multiple_of((half // 2) * k + rows * net.g, rows), rows)
            to_up = pl.ds(pl.multiple_of(half + (half // 2) * k + rows * net.g, rows), rows)
            placed[to, :] = hgu8[k * rows:(k + 1) * rows, :]
            placed[to_up, :] = hgu8[128 + k * rows:128 + (k + 1) * rows, :]
            hdn[to, :] = hdn8[k * rows:(k + 1) * rows, :]
        hp[...] = placed[...].T
        r.taT[:, pl.ds(every, every)] = ab[...].T

    ag1 = all_gather(net, back, r.ag1, (wide_back, down_back), place_sums)

    def query_done(p, value):
        d_queries[:, p * half:(p + 1) * half] = value.astype(BF)
    query_sum.last(query_done)

    pq, tb, ec = r.pq, r.tb, r.ec
    pq[...] = dot_nt(xb[...], back[:, wide])

    def t_rows(at):
        g, u = gu[at, gl], gu[at, ul]
        p, q = pq[at, gl], pq[at, ul]
        sig = jax.nn.sigmoid(g)
        tb[at, :] = (q * g * sig + p * u * sig * (1.0 + g * (1.0 - sig))).astype(BF)
    by_rows(every, 32, t_rows)
    sp, sr, sb = r.sp, r.sr, r.sb
    second_out = []
    for k, at in enumerate((mine, theirs)):
        sp[at, :] = dot_nt(ab[at, :], back[:, dl]) + dot(tb[at, :], r.cb[...])
        second_out.append(twin(sp.at[at, :], sr.at[at, :], 8 + k))
    ec[...] = dot(eb[...], back[:, dl])
    r.taT[:, pl.ds(0, every)] = tb[...].T
    for copy, at in zip(second_out, (theirs, mine)):
        copy.wait_recv()
        sb[at, :] = (sp[at, :] + sr[at, :]).astype(BF)
    prow = 2 * rows
    dsw, dloc = r.dsw, r.dloc
    dloc[...] = (r.hdn[...] + dot(r.taT[:, pl.ds(0, every)], eb[...])
                 + dot(r.taT[:, pl.ds(every, every)], sb[...])).astype(BF)
    swaps = []
    for k in range(zs // 2):
        slot = (zs // 2) * c + k
        swaps.append(twin(dloc.at[block(2 * k + 1 - c, prow), :], dsw.at[slot], 10 + k))
        dsw[slot] = dloc[block(2 * k + c, prow), :]
    d_values[...] = -(sp[mine, :] + sr[mine, :])
    ec[...] += dot_nt(sb[...], r.cb[...])
    gub = r.gub

    def pull_rows(at):
        g, u, d = gu[at, gl], gu[at, ul], da[at, :]
        p, q, back_a = pq[at, gl], pq[at, ul], ec[at, :]
        sig = jax.nn.sigmoid(g)
        sneg = 1.0 - sig
        h = g * sig
        slope = sig * (1.0 + g * sneg)
        bend = sig * sneg * (2.0 + g * (1.0 - 2.0 * sig))
        pd = p * d
        gub[at, gl] = (back_a * u * slope + pd * u * bend + q * d * slope).astype(BF)
        gub[at, ul] = (back_a * h + pd * slope).astype(BF)
    by_rows(every, 32, pull_rows)

    pay2 = r.pay2

    def last_side():
        pay2[:, :outer] = (r.hp[:, :outer] + dot(r.xT[...], gub[:, :outer])).astype(BF)

    def last_block(zb, i):
        at = block(zb, zrows)
        pay2[at, inner] = (r.hp[at, inner] + dot(r.xT[at, :], gub[:, inner])).astype(BF)
        if i == 0:
            for copy in swaps:
                copy.wait_recv()
        for y in range(2):
            for x in range(2):
                pay2[block(4 * zb + 2 * y + x, rows), dl] = (
                    dsw[zb, y * rows:(y + 1) * rows, x * half:(x + 1) * half])

    def key_back():
        r.kp[...] = dot(dgu[...], back[:, wide])

    def key_back_second():
        r.kp[...] += dot_nt(gub[...], r.abb[...])
        r.kin = twin(r.kp.at[theirs, :], r.kr, 10 + zs // 2)

    last = r.last
    rs2 = reduce_scatter(net, pay2, r.rs2, last, last_block, last_side,
                         {0: key_back, 1: key_back_second})
    fin = r.fin
    fin[block(net.g, rows), :] = last[...].astype(BF)
    final = [send(fin.at[block(net.g, rows), :], fin.at[block(net.g, rows), :], r.fsem, k, peer)
             for k, peer in ((2, near_at[2]), (0, near_at[0]), (1, near_at[1]))]
    r.kin.wait_recv()
    d_keys[...] = r.kp[mine, :] + r.kr[...]
    for copy in final:
        copy.wait_recv()
    swap = twin(fin.at[block(1 - c, prow), wide], r.tw, 11 + zs // 2)
    lanes = block(c, half)
    others = block(1 - c, half)
    d_gate[:, lanes] = fin[block(c, prow), gl].astype(F32) * inverse
    d_up[:, lanes] = fin[block(c, prow), ul].astype(F32) * inverse
    for y in range(2):
        for x in range(2):
            g = 2 * y + x
            d_down[y * rows:(y + 1) * rows, x * half:(x + 1) * half] = (
                fin[g * rows:(g + 1) * rows, width:].astype(F32) * inverse)
    swap.wait_recv()
    d_gate[:, others] = r.tw[:, :half].astype(F32) * inverse
    d_up[:, others] = r.tw[:, half:].astype(F32) * inverse
    await_copy(net, r.sq.at[0], tsem, 5, 5)
    drain(done + slices + units + final)
    query_sum.finish()
    for finish in (rs0, ag1, rs2, summing.finish):
        finish()
    for p in range(2):
        plane_drain(net, qa, token_at, 0, p, r.qsem)
        plane_drain(net, oa, token_at, 0, p, r.osem)

    def drain_line(z):
        for zb in range(zs):
            for p in range(2):
                pass_drain(net, z, zb, p, gz_at(zb, p), line)
            if zb != z:
                await_copy(net, rz_at(z), xsem, (zb,), (zb,))
    at_each(net, drain_line)


def hand_over(*refs):
    copies = [pltpu.make_async_copy(src, dst, refs[12].at[i])
              for i, (src, dst) in enumerate(zip(refs[:6], refs[6:12]))]
    for copy in copies:
        copy.start()
    for copy in copies:
        copy.wait()


def fused_step(queries, key_tokens, values, out_grad, w_gate, w_up, w_down, zs, inverse):
    toks, width = queries.shape
    half, every, rows = width // 2, 2 * toks, width // (4 * zs)
    plane = 4 * every
    total = width + half
    side, main = lane_parts(total)
    unit = side[0].size
    f32 = lambda *shape: VM(shape, F32)
    bf = lambda *shape: VM(shape, BF)
    sems = lambda *shape: (DMA(shape), DMA(shape))
    both = lambda *shape: tuple(VM(shape + (part.size,), BF) for part in main)
    summed = dict(
        r1=both(zs, 2, rows), r2=both(zs, rows), zb=both(zs - 1, rows), zr=both(zs + 1, rows),
        s1=sems(zs, 2, 2), s2=sems(zs, 2), s3=sems(zs + 1, 2), pb=bf(4 * rows, 2 * unit),
        lo=(bf(zs - 1, 4 * rows, unit),) * 2, li=(bf(zs + 1, 4 * rows, unit),) * 2,
        ls=sems(zs + 1, 2),
        ps=dict(r1=bf(2, 2, rows, unit), r2=bf(2, rows, unit), s1=sems(2, 2), s2=sems(2)))
    spread = lambda depth: dict(
        z=sems(depth, 2, 2), o=sems(depth, 2, 2), f=sems(depth, 2))
    scratch = dict(
        kf=f32(toks, width), vf=f32(toks, width), wab=f32(width, width), wc=f32(half, width),
        wabt=f32(width, width), wct=f32(width, half), gu=f32(every, width), ep=f32(every, width),
        er=f32(every, width), da=f32(every, half), grad=f32(rows, total), hsum=f32(rows, total),
        last=f32(rows, total), sq=f32(4, rows, 128), scale=f32(2, rows, 128),
        hgu=f32(256, plane), dact=f32(128, plane), hdn8=f32(128, width), hgu8=f32(256, width),
        pd=f32(width, 128), placed=f32(width, width), hp=f32(width, width), hdn=f32(half, width),
        pq=f32(every, width), ec=f32(every, half), sp=f32(every, width), sr=f32(every, width),
        kp=f32(every, width), kr=f32(toks, width),
        xb=bf(every, width), qa=bf(plane, width), oa=bf(plane, width), abb=bf(width, width),
        cb=bf(half, width), ab=bf(every, half), eb=bf(every, width), dgu=bf(every, width),
        dguT=bf(width, every), eT=bf(width, every), xT=bf(width, every), hd=bf(256, plane),
        hdT=bf(plane, 256), hact=bf(128, plane), rzT=bf(128, width), tb=bf(every, half),
        sel=bf(half, 512), wgu=bf(256, width), gz=bf(zs * rows, width), rz=bf(width, 128),
        dsl=bf(rows, 512), dout=bf(4 * rows, 128), din=bf(rows, 512), dqs=bf(4 * toks, width),
        dqm=bf(4 * toks, width), dqt=bf(4 * toks, width),
        ldo=bf(zs - 1, 4 * rows, 128), ldi=bf(zs + 1, 4 * rows, 128),
        lgo0=bf(zs - 1, rows, half), lgi0=bf(zs + 1, rows, half),
        lgo1=bf(zs - 1, rows, half), lgi1=bf(zs + 1, rows, half),
        sb=bf(every, width), taT=bf(half, 2 * every), gub=bf(every, width), dloc=bf(half, width),
        dsw=bf(zs, 2 * rows, width), pay0=bf(width, total), pay2=bf(width, total),
        full1=bf(width, total), fin=bf(4 * rows, total), tw=bf(2 * rows, width),
        rs0=summed, rs2=summed, ag1=spread(zs), fsem=sems(3), qsem=spread(1), osem=spread(1),
        line=spread(zs), lsem=sems(zs + 1, 3), xsem=sems(zs), ssem=sems(3), usem=sems(3),
        dqs3=dict(r1=bf(2, 2, toks, half), r2=bf(2, toks, half), s1=sems(2, 2), s2=sems(2)),
        tsem=sems(32), ld=DMA((7,)))
    shapes, tree = jax.tree.flatten(scratch)
    token = jax.ShapeDtypeStruct((toks, width), F32)
    weight = jax.ShapeDtypeStruct((2 * rows, width), F32)
    results = pl.pallas_call(
        functools.partial(step_body, zs, tree, inverse),
        out_shape=(jax.ShapeDtypeStruct((toks, width), BF), token, token, weight, weight, weight),
        in_specs=[pl.BlockSpec(memory_space=pltpu.HBM)] * 7,
        out_specs=[pl.BlockSpec(memory_space=VM)] * 6,
        scratch_shapes=shapes,
        compiler_params=pltpu.CompilerParams(
            collective_id=0, has_side_effects=True, vmem_limit_bytes=52 * 1024 * 1024),
    )(*(pltpu.with_memory_space_constraint(x, pltpu.HBM) for x in (
        queries, key_tokens, values, out_grad, w_gate, w_up, w_down)))
    return pl.pallas_call(
        hand_over,
        out_shape=tuple(jax.ShapeDtypeStruct(item.shape, item.dtype) for item in results),
        in_specs=[pl.BlockSpec(memory_space=VM)] * 6,
        out_specs=[pl.BlockSpec(memory_space=pltpu.HBM)] * 6,
        scratch_shapes=[DMA((6,))],
        compiler_params=pltpu.CompilerParams(vmem_limit_bytes=8 * 1024 * 1024),
    )(*results)


def matmul(left, right):
    return dot(left.astype(BF), right.astype(BF))


def key_grad(w_gate, w_up, w_down, key_rows, value_rows):
    hidden_gate = matmul(key_rows, w_gate)
    hidden_up = matmul(key_rows, w_up)
    sig = jax.nn.sigmoid(hidden_gate)
    active = hidden_gate * sig * hidden_up
    error = matmul(active, w_down) - value_rows
    d_active = matmul(error, w_down.T)
    d_hup = d_active * hidden_gate * sig
    d_hgate = d_active * hidden_up * sig * (1.0 + hidden_gate * (1.0 - sig))
    return (matmul(d_hgate.T, key_rows), matmul(d_hup.T, key_rows), matmul(error.T, active))


def query_grad(fast_t, query_rows, grad_rows):
    gate_t, up_t, down_t = fast_t
    hidden_gate = dot(query_rows, gate_t.T)
    hidden_up = dot(query_rows, up_t.T)
    sig = jax.nn.sigmoid(hidden_gate)
    active = (hidden_gate * sig * hidden_up).astype(BF)
    d_active = dot(grad_rows, down_t)
    d_hup = (d_active * hidden_gate * sig).astype(BF)
    d_hgate = (d_active * hidden_up * sig * (1.0 + hidden_gate * (1.0 - sig))).astype(BF)
    d_rows = (dot(d_hgate, gate_t) + dot(d_hup, up_t)).astype(BF)
    return (d_rows, active, d_hgate, d_hup)


def general_step(queries, key_tokens, values, out_grad, w_gate, w_up, w_down, inverse):
    gs, toks = lax.axis_size("grp"), lax.axis_size("tok")
    full_width = w_gate.shape[0]
    rows = 3 * full_width // (gs * toks)
    me = lax.axis_index("tok") * gs + lax.axis_index("grp")

    def reduce_units(x):
        y = x.reshape(toks, gs * rows, full_width)
        y = lax.psum_scatter(y, "tok", scatter_dimension=0, tiled=True)[0]
        return lax.psum_scatter(y.reshape(gs, rows, full_width), "grp", scatter_dimension=0, tiled=True)[0]

    def gather_units(y):
        full = lax.all_gather(lax.all_gather(y, "grp"), "tok").reshape(3, full_width, full_width)
        return full[0], full[1], full[2]

    local_grad, pullback = jax.vjp(key_grad, w_gate, w_up, w_down, key_tokens, values)
    grad = reduce_units(jnp.stack(local_grad))
    scale = jnp.sqrt(jnp.sum(grad * grad, axis=1, keepdims=True) / full_width + EPSILON)
    weights = jnp.concatenate((w_gate, w_up, w_down), axis=1)
    mine = lax.dynamic_slice_in_dim(weights, me * rows, rows, 1).T
    fast_t = gather_units((mine - STEP_SIZE * grad / scale).astype(BF))
    d_queries, active, d_hgate, d_hup = query_grad(fast_t, queries, out_grad)
    query_part = reduce_units(
        jnp.stack((dot(d_hgate.T, queries), dot(d_hup.T, queries), dot(out_grad.T, active))))
    product = jnp.sum(-STEP_SIZE * query_part * grad, axis=1, keepdims=True)
    cot = (
        -STEP_SIZE * query_part / scale - grad * product / (full_width * scale * scale * scale)
    ).astype(BF)
    second = pullback(tuple(item.astype(F32) for item in gather_units(cot)))
    plain = (dot(queries.T, d_hgate), dot(queries.T, d_hup), dot(active.T, out_grad))
    combined = jnp.stack(tuple(left + right for left, right in zip(plain, second[:3])))
    combined = combined.reshape(3, toks, full_width // toks, full_width).transpose(1, 0, 2, 3)
    summed = lax.all_gather(reduce_units(combined).astype(BF), "grp").astype(F32) * inverse
    summed = summed.reshape(3, full_width // toks, full_width)
    return (d_queries, second[3], second[4], summed[0], summed[1], summed[2])


def on_device(*arrays):
    gs, toks = lax.axis_size("grp"), lax.axis_size("tok")
    tokens, width = arrays[0].shape
    inverse = 1.0 / (tokens * gs * toks)
    zs = toks // 2
    fits = gs == 4 and toks % 4 == 0 and zs <= 4
    if fits and width % (64 * zs) == 0 and 2 * width <= 512 * zs and width % 256 == 0 and tokens % 128 == 0:
        return fused_step(*arrays, zs, inverse)
    return general_step(*arrays, inverse)


def solution(mesh):
    token = P(("grp", "tok"), None)
    return jax.shard_map(
        on_device,
        mesh=mesh,
        in_specs=(token, token, token, token, P(), P(), P()),
        out_specs=(token, token, token, P("tok", None), P("tok", None), P("tok", None)),
        check_vma=False,
    )
```
